256 devices in a mesh: pb: 16 (over x, y_lo, core), ha: 16 (over y_hi, z).
Axes of the slice: x: 4, y: 4 (y_hi: 2, y_lo: 2; y = y_hi * 2 + y_lo), z: 8, core: 2. Of those that a mesh axis runs over, the one named last changes fastest.
Arguments:
- main_query: bfloat16 [2048, 128, 576], P('pb', 'ha'), may hold values from -1.8 to 1.8
- latent: bfloat16 [2048, 576], P('pb'), may hold values from -6 to 6
- log_sums: float32 [2048, 128], P('pb', 'ha'), may hold values from 0 to 4
- window_start: int32 [2048], P('pb'), may hold values from 0 to 2046, as said below
- index_query: bfloat16 [2048, 64, 128], P('pb', 'ha'), may hold values from -0.6 to 0.6
- index_key: bfloat16 [2048, 128], P('pb'), may hold values from -4 to 4
- index_weight: float32 [2048, 64], P('pb', 'ha'), may hold values from -4 to 4
Outputs:
- index_query_grad: bfloat16 [2048, 64, 128], P('pb', 'ha')
- index_key_grad: bfloat16 [2048, 128], P('pb')
- index_weight_grad: float32 [2048, 64], P('pb', 'ha')
The draws below stay inside these ranges and needn't reach their ends.
Inputs may be any that keep to these rules, and one draw needn't show every extreme that they name: window_start[0] is 0, window_start[t] is at most t - 1 for t >= 1, and window_start[2047] is 2046, so every query sees itself and, past the first, at least one earlier key.
All inputs are finite; a program needn't handle non-finite values.
Results may differ from the reference program's by a relative error of at most 0.0049.
Values may be sent and summed in bfloat16 or wider, within the bound.
A program may use at most 64 MiB of HBM per device.

```python
import jax
import jax.numpy as jnp
from jax import lax

HEADS = 128
LAT = 576
IHEADS = 64
IDIM = 128
TOK_DEV = 128
TOKENS = 2048


def draw_window_start(key, part):
    positions = jnp.arange(TOKENS, dtype=jnp.int32)
    upper = jnp.maximum(positions, 1)
    starts = jax.random.randint(jax.random.fold_in(key, 7), (TOKENS,), 0, upper, dtype=jnp.int32)
    return jnp.where(positions == TOKENS - 1, jnp.int32(TOKENS - 2), starts).astype(jnp.int32)


def draw_main_query(key, part):
    base_key = jax.random.fold_in(key, 31)
    values = jnp.clip(0.3 * jax.random.normal(base_key, (TOKENS, HEADS, LAT), jnp.float32), -1.8, 1.8)
    return values.astype(jnp.bfloat16)


def draw_latent(key, part):
    base_key = jax.random.fold_in(key, 41)
    values = jnp.clip(jax.random.normal(base_key, (TOKENS, LAT), jnp.float32), -6.0, 6.0)
    return values.astype(jnp.bfloat16)


def index_tables(key):
    weight_key = jax.random.fold_in(key, 21)
    keys_key = jax.random.fold_in(key, 22)
    query_key = jax.random.fold_in(key, 23)
    scale_key = jax.random.fold_in(key, 24)
    weights = jnp.clip(jax.random.normal(weight_key, (TOKENS, IHEADS), jnp.float32), -4.0, 4.0)
    keys = jnp.clip(jax.random.normal(keys_key, (TOKENS, IDIM), jnp.float32), -4.0, 4.0)
    queries = 0.044 * jnp.clip(jax.random.normal(query_key, (TOKENS, IHEADS, IDIM), jnp.float32), -4.0, 4.0)
    scales = jnp.exp(jax.random.uniform(scale_key, (TOKENS, 1, 1), jnp.float32, jnp.log(0.5), jnp.log(2.0)))
    queries = queries * scales
    return (weights, keys, queries)


def draw_index_query(key, part):
    return index_tables(key)[2].astype(jnp.bfloat16)


def draw_index_key(key, part):
    return index_tables(key)[1].astype(jnp.bfloat16)


def draw_index_weight(key, part):
    return index_tables(key)[0]


def steps_of(rng, dims, shards, smallest, largest):
    def one(dim, blocks):
        steps = jax.random.uniform(jax.random.fold_in(jax.random.fold_in(rng, 6), dim), (blocks,), jnp.float32, smallest / len(shards), largest / len(shards))
        return jnp.repeat(jnp.exp(steps), dims[dim] // blocks).reshape((-1,) + (1,) * (len(dims) - dim - 1))

    gain = one(*shards[0])
    for cut in shards[1:]:
        gain = gain * one(*cut)
    return gain


def setup_inputs(seed: int = 0) -> dict:
    key_of = jax.random.split(jax.random.key(seed), 8)
    return {
        "main_query": draw_main_query(jax.random.fold_in(key_of[7], 71), 0),
        "latent": draw_latent(jax.random.fold_in(key_of[7], 71), 0),
        "log_sums": jnp.clip(4.0 * jax.random.uniform(key_of[2], (TOKENS, HEADS), jnp.float32) ** steps_of(key_of[2], (TOKENS, HEADS), ((0, 16), (1, 16)), -0.2, 0.2), 0.0, 4.0),
        "window_start": draw_window_start(jax.random.fold_in(key_of[7], 71), 0),
        "index_query": draw_index_query(jax.random.fold_in(key_of[7], 71), 0),
        "index_key": draw_index_key(jax.random.fold_in(key_of[7], 71), 0),
        "index_weight": draw_index_weight(jax.random.fold_in(key_of[7], 71), 0),
    }


main_scale = 192.0 ** -0.5
very_low = -1e30


def reference(main_query, latent, log_sums, window_start, index_query, index_key, index_weight):
    tokens = latent.shape[0]
    blocks = tokens // TOK_DEV
    columns = jnp.arange(tokens, dtype=jnp.int32)
    latent_wide = latent.astype(jnp.float32)
    keys_wide = index_key.astype(jnp.float32)
    first_rows = jnp.arange(blocks, dtype=jnp.int32) * TOK_DEV

    def one_block(key_grad, inputs):
        query_block, sums_block, start_block, index_block, weight_block, first_row = inputs
        positions = first_row + jnp.arange(TOK_DEV, dtype=jnp.int32)
        visible_mask = (columns[None, :] >= start_block[:, None]) & (columns[None, :] <= positions[:, None])
        scores = jnp.dot(query_block.reshape(TOK_DEV * HEADS, LAT).astype(jnp.float32), latent_wide.T, preferred_element_type=jnp.float32)
        scores = scores.reshape(TOK_DEV, HEADS, tokens) * main_scale
        head_probs = jnp.where(visible_mask, jnp.sum(jnp.exp(scores - sums_block[:, :, None]), axis=1), 0.0)
        target = head_probs / jnp.sum(head_probs, axis=1, keepdims=True)
        flat_index = index_block.reshape(TOK_DEV * IHEADS, IDIM)
        act = jnp.dot(flat_index.astype(jnp.float32), keys_wide.T, preferred_element_type=jnp.float32)
        act = act.reshape(TOK_DEV, IHEADS, tokens)
        relu_act = jnp.maximum(act, 0.0)
        logits = jnp.sum(weight_block[:, :, None] * relu_act, axis=1)
        masked = jnp.where(visible_mask, logits, very_low)
        row_top = jnp.max(masked, axis=1, keepdims=True)
        expo = jnp.where(visible_mask, jnp.exp(masked - row_top), 0.0)
        logit_grad = jnp.where(visible_mask, expo / jnp.sum(expo, axis=1, keepdims=True) - target, 0.0)
        weight_grad = jnp.sum(logit_grad[:, None, :] * relu_act, axis=2)
        coeffs = jnp.where(act > 0.0, logit_grad[:, None, :] * weight_block[:, :, None], 0.0).astype(jnp.bfloat16)
        coeffs = coeffs.reshape(TOK_DEV * IHEADS, tokens).astype(jnp.float32)
        query_grad = jnp.dot(coeffs, keys_wide, preferred_element_type=jnp.float32).astype(jnp.bfloat16)
        key_grad = key_grad + jnp.dot(coeffs.T, flat_index.astype(jnp.float32), preferred_element_type=jnp.float32)
        return key_grad, (query_grad.reshape(TOK_DEV, IHEADS, IDIM), weight_grad)

    inputs = (main_query.reshape(blocks, TOK_DEV, HEADS, LAT), log_sums.reshape(blocks, TOK_DEV, HEADS),
              window_start.reshape(blocks, TOK_DEV), index_query.reshape(blocks, TOK_DEV, IHEADS, IDIM),
              index_weight.reshape(blocks, TOK_DEV, IHEADS), first_rows)
    key_grad, outputs = lax.scan(one_block, jnp.zeros((tokens, IDIM), jnp.float32), inputs)
    query_grads, weight_grads = outputs
    return (query_grads.reshape(tokens, IHEADS, IDIM), key_grad.astype(jnp.bfloat16), weight_grads.reshape(tokens, IHEADS))
```

```python
import math

import jax
import jax.numpy as jnp
from jax import lax
from jax.sharding import PartitionSpec as P

main_scale = 192.0 ** (-0.5)
very_low = -1e30


def visible(window_start, positions, first_row, width):
    columns = first_row + jnp.arange(width, dtype=jnp.int32)
    return (columns[None, :] >= window_start[:, None]) & (columns[None, :] <= positions[:, None])


def on_device(main_query, latent, log_sums, window_start, index_query, index_key, index_weight):
    query_rows, head_count, latent_width = main_query.shape
    index_width = index_query.shape[2]
    groups = lax.axis_size("ha")
    tokens = query_rows * lax.axis_size("pb")
    own_rows = query_rows // groups
    block_first = lax.axis_index("pb") * query_rows
    flat_query = main_query.reshape(query_rows * head_count, latent_width)
    latent_piece = lax.all_gather(latent, "pb", axis=0, tiled=True)
    keys_all = lax.all_gather(index_key, "pb", axis=0, tiled=True)

    local_index = lax.all_to_all(index_query, "ha", 0, 1, tiled=True)
    local_weight = lax.all_to_all(index_weight, "ha", 0, 1, tiled=True)
    index_heads = local_index.shape[1]
    row_first = block_first + lax.axis_index("ha") * own_rows
    own_positions = row_first + jnp.arange(own_rows, dtype=jnp.int32)
    own_start = lax.dynamic_slice_in_dim(window_start, lax.axis_index("ha") * own_rows, own_rows, 0)

    positions = block_first + jnp.arange(query_rows, dtype=jnp.int32)
    probs_part = jnp.zeros((query_rows, tokens), jnp.float32)
    block_size = math.gcd(tokens, 512)

    def one_block(block_index, probs_inner):
        offset = block_index * block_size
        latent_block = lax.dynamic_slice_in_dim(latent_piece, offset, block_size, 0)
        visible_mask = visible(window_start, positions, offset, block_size)
        scores = jnp.einsum(
            "rd,kd->rk", flat_query, latent_block, preferred_element_type=jnp.float32
        )
        scores = scores.reshape(query_rows, head_count, block_size) * main_scale
        head_mass = jnp.where(
            visible_mask, jnp.sum(jnp.exp(scores - log_sums[:, :, None]), axis=1), 0.0
        )
        return lax.dynamic_update_slice_in_dim(probs_inner, head_mass, offset, 1)

    probs_part = lax.fori_loop(0, tokens // block_size, one_block, probs_part)
    probs_all = lax.psum_scatter(probs_part, "ha", scatter_dimension=0, tiled=True)

    flat_index = local_index.reshape(own_rows * index_heads, index_width)
    active = jnp.einsum("rd,kd->rk", flat_index, keys_all, preferred_element_type=jnp.float32)
    active = active.reshape(own_rows, index_heads, tokens)
    relu_act = jnp.maximum(active, 0.0)
    logit_all = jnp.sum(local_weight[:, :, None] * relu_act, axis=1)

    visible_all = visible(own_start, own_positions, 0, tokens)
    target = probs_all / jnp.sum(probs_all, axis=1, keepdims=True)
    masked = jnp.where(visible_all, logit_all, very_low)
    row_top = jnp.max(masked, axis=1, keepdims=True)
    expo = jnp.where(visible_all, jnp.exp(masked - row_top), 0.0)
    logit_grad = jnp.where(visible_all, expo / jnp.sum(expo, axis=1, keepdims=True) - target, 0.0)

    weight_grad = jnp.sum(logit_grad[:, None, :] * relu_act, axis=2)
    coeffs = jnp.where(
        active > 0.0, logit_grad[:, None, :] * local_weight[:, :, None], 0.0
    ).astype(jnp.bfloat16)
    coeffs = coeffs.reshape(own_rows * index_heads, tokens)
    query_grad = jnp.dot(coeffs, keys_all, preferred_element_type=jnp.float32)
    key_grad = jnp.einsum("rk,rd->kd", coeffs, flat_index, preferred_element_type=jnp.float32)

    key_share = lax.psum_scatter(key_grad, "pb", scatter_dimension=0, tiled=True)
    key_output = lax.psum(key_share, "ha").astype(jnp.bfloat16)
    query_grad = query_grad.astype(jnp.bfloat16).reshape(own_rows, index_heads, index_width)
    query_output = lax.all_to_all(query_grad, "ha", 1, 0, tiled=True)
    weight_output = lax.all_to_all(weight_grad, "ha", 1, 0, tiled=True)
    return (query_output, key_output, weight_output)


def solution(mesh):
    return jax.shard_map(
        on_device,
        mesh=mesh,
        in_specs=(
            P("pb", "ha", None),
            P("pb", None),
            P("pb", "ha"),
            P("pb"),
            P("pb", "ha", None),
            P("pb", None),
            P("pb", "ha"),
        ),
        out_specs=(P("pb", "ha", None), P("pb", None), P("pb", "ha")),
        check_vma=False,
    )
```

```python
import functools
import math

import jax
import jax.numpy as jnp
from jax import lax
from jax.experimental import pallas as pl
from jax.experimental.pallas import tpu as pltpu
from jax.sharding import PartitionSpec as P

main_scale = 192.0 ** (-0.5)
very_low = -1e30
MESH = pl.DeviceIdType.MESH
AXES = ("pb", "ha")


def visible(window_start, positions, first_row, width):
    columns = first_row + jnp.arange(width, dtype=jnp.int32)
    return (columns[None, :] >= window_start[:, None]) & (columns[None, :] <= positions[:, None])


def device_of(axis, peer):
    return tuple(peer if name == axis else lax.axis_index(name) for name in AXES)


def exchange_kernel(axis, count, gather, *refs):
    x_refs, y_refs = refs[:count], refs[count : 2 * count]
    send_sem, recv_sem = refs[2 * count], refs[2 * count + 1]
    n = lax.axis_size(axis)
    me = lax.axis_index(axis)

    barrier = pltpu.get_barrier_semaphore()
    for step in range(1, n):
        peer = lax.rem(me + step, n)
        pl.semaphore_signal(barrier, inc=1, device_id=device_of(axis, peer), device_id_type=MESH)
    pl.semaphore_wait(barrier, n - 1)

    copies = []
    for step in range(1, n):
        peer = lax.rem(me + step, n)
        for i in range(count):
            source = x_refs[i] if gather else x_refs[i].at[peer]
            copy = pltpu.make_async_remote_copy(
                src_ref=source,
                dst_ref=y_refs[i].at[me],
                send_sem=send_sem.at[i * n + peer],
                recv_sem=recv_sem.at[i * n + me],
                device_id=device_of(axis, peer),
                device_id_type=MESH,
            )
            copy.start()
            copies.append(copy)
    for i in range(count):
        y_refs[i][me] = x_refs[i][...] if gather else x_refs[i][me]
    for step in range(1, n):
        source_device = lax.rem(me + n - step, n)
        for i in range(count):
            copies[(step - 1) * count + i].wait_send()
            incoming = pltpu.make_async_remote_copy(
                src_ref=y_refs[i].at[source_device],
                dst_ref=y_refs[i].at[source_device],
                send_sem=send_sem.at[i * n + source_device],
                recv_sem=recv_sem.at[i * n + source_device],
                device_id=device_of(axis, source_device),
                device_id_type=MESH,
            )
            incoming.wait_recv()


def exchange(arrays, axis, collective_id, gather=False):
    n = lax.axis_size(axis)
    count = len(arrays)
    out_shapes = [
        jax.ShapeDtypeStruct(((n,) + a.shape) if gather else a.shape, a.dtype) for a in arrays
    ]
    moved = sum(a.size * a.dtype.itemsize for a in arrays) * (n if gather else 1)
    return pl.pallas_call(
        functools.partial(exchange_kernel, axis, count, gather),
        out_shape=out_shapes,
        in_specs=[pl.BlockSpec(memory_space=pltpu.VMEM)] * count,
        out_specs=[pl.BlockSpec(memory_space=pltpu.VMEM)] * count,
        scratch_shapes=[
            pltpu.SemaphoreType.DMA((count * n,)),
            pltpu.SemaphoreType.DMA((count * n,)),
        ],
        compiler_params=pltpu.CompilerParams(collective_id=collective_id, has_side_effects=True),
        cost_estimate=pl.CostEstimate(flops=0, transcendentals=0, bytes_accessed=2 * moved),
    )(*arrays)


def on_device(main_query, latent, log_sums, window_start, index_query, index_key, index_weight):
    query_rows, head_count, latent_width = main_query.shape
    index_width = index_query.shape[2]
    part_heads = index_query.shape[1]
    groups = lax.axis_size("ha")
    blocks = lax.axis_size("pb")
    tokens = query_rows * blocks
    own_rows = query_rows // groups
    block_first = lax.axis_index("pb") * query_rows
    flat_query = main_query.reshape(query_rows * head_count, latent_width)
    latent_piece = lax.all_gather(latent, "pb", axis=0, tiled=True)
    keys_all = lax.all_gather(index_key, "pb", axis=0, tiled=True)

    index_parts, weight_parts = exchange(
        [
            index_query.reshape(groups, own_rows * part_heads, index_width),
            index_weight.reshape(groups, 1, own_rows * part_heads),
        ],
        "ha",
        0,
    )
    index_heads = part_heads * groups
    local_index = (
        index_parts.reshape(groups, own_rows, part_heads, index_width)
        .transpose(1, 0, 2, 3)
        .reshape(own_rows, index_heads, index_width)
    )
    local_weight = (
        weight_parts.reshape(groups, own_rows, part_heads).transpose(1, 0, 2).reshape(own_rows, index_heads)
    )
    row_first = block_first + lax.axis_index("ha") * own_rows
    own_positions = row_first + jnp.arange(own_rows, dtype=jnp.int32)
    own_start = lax.dynamic_slice_in_dim(window_start, lax.axis_index("ha") * own_rows, own_rows, 0)

    positions = block_first + jnp.arange(query_rows, dtype=jnp.int32)
    probs_part = jnp.zeros((query_rows, tokens), jnp.float32)
    block_size = math.gcd(tokens, 512)

    def one_block(block_index, probs_inner):
        offset = block_index * block_size
        latent_block = lax.dynamic_slice_in_dim(latent_piece, offset, block_size, 0)
        visible_mask = visible(window_start, positions, offset, block_size)
        scores = jnp.einsum(
            "rd,kd->rk", flat_query, latent_block, preferred_element_type=jnp.float32
        )
        scores = scores.reshape(query_rows, head_count, block_size) * main_scale
        head_mass = jnp.where(
            visible_mask, jnp.sum(jnp.exp(scores - log_sums[:, :, None]), axis=1), 0.0
        )
        return lax.dynamic_update_slice_in_dim(probs_inner, head_mass, offset, 1)

    probs_part = lax.fori_loop(0, tokens // block_size, one_block, probs_part)
    probs_parts = exchange([probs_part.reshape(groups, own_rows, tokens)], "ha", 1)[0]
    probs_all = jnp.sum(probs_parts, axis=0)

    flat_index = local_index.reshape(own_rows * index_heads, index_width)
    active = jnp.einsum("rd,kd->rk", flat_index, keys_all, preferred_element_type=jnp.float32)
    active = active.reshape(own_rows, index_heads, tokens)
    relu_act = jnp.maximum(active, 0.0)
    logit_all = jnp.sum(local_weight[:, :, None] * relu_act, axis=1)

    visible_all = visible(own_start, own_positions, 0, tokens)
    target = probs_all / jnp.sum(probs_all, axis=1, keepdims=True)
    masked = jnp.where(visible_all, logit_all, very_low)
    row_top = jnp.max(masked, axis=1, keepdims=True)
    expo = jnp.where(visible_all, jnp.exp(masked - row_top), 0.0)
    logit_grad = jnp.where(visible_all, expo / jnp.sum(expo, axis=1, keepdims=True) - target, 0.0)

    weight_grad = jnp.sum(logit_grad[:, None, :] * relu_act, axis=2)
    coeffs = jnp.where(
        active > 0.0, logit_grad[:, None, :] * local_weight[:, :, None], 0.0
    ).astype(jnp.bfloat16)
    coeffs = coeffs.reshape(own_rows * index_heads, tokens)
    query_grad = jnp.dot(coeffs, keys_all, preferred_element_type=jnp.float32)
    key_grad = jnp.einsum("rk,rd->kd", coeffs, flat_index, preferred_element_type=jnp.float32)

    query_grad = query_grad.astype(jnp.bfloat16).reshape(own_rows, groups, part_heads, index_width)
    query_back, weight_back = exchange(
        [
            query_grad.transpose(1, 0, 2, 3).reshape(groups, own_rows * part_heads, index_width),
            weight_grad.reshape(own_rows, groups, part_heads)
            .transpose(1, 0, 2)
            .reshape(groups, 1, own_rows * part_heads),
        ],
        "ha",
        2,
    )
    query_output = query_back.reshape(query_rows, part_heads, index_width)
    weight_output = weight_back.reshape(query_rows, part_heads)

    key_parts = exchange([key_grad.reshape(blocks, query_rows, index_width)], "pb", 3)[0]
    key_share = jnp.sum(key_parts, axis=0).reshape(groups, own_rows, index_width)
    key_rows = jnp.sum(exchange([key_share], "ha", 4)[0], axis=0)
    key_output = exchange([key_rows], "ha", 5, gather=True)[0]
    key_output = key_output.reshape(query_rows, index_width).astype(jnp.bfloat16)
    return (query_output, key_output, weight_output)


def solution(mesh):
    return jax.shard_map(
        on_device,
        mesh=mesh,
        in_specs=(
            P("pb", "ha", None),
            P("pb", None),
            P("pb", "ha"),
            P("pb"),
            P("pb", "ha", None),
            P("pb", None),
            P("pb", "ha"),
        ),
        out_specs=(P("pb", "ha", None), P("pb", None), P("pb", "ha")),
        check_vma=False,
    )
```

```python
import functools
import math

import jax
import jax.numpy as jnp
from jax import lax
from jax.experimental import pallas as pl
from jax.experimental.pallas import tpu as pltpu
from jax.sharding import PartitionSpec as P

main_scale = 192.0 ** (-0.5)
very_low = -1e30
MESH = pl.DeviceIdType.MESH
AXES = ("pb", "ha")


def visible(window_start, positions, first_row, width):
    columns = first_row + jnp.arange(width, dtype=jnp.int32)
    return (columns[None, :] >= window_start[:, None]) & (columns[None, :] <= positions[:, None])


def device_of(axis, peer):
    return tuple(peer if name == axis else lax.axis_index(name) for name in AXES)


def exchange_kernel(axis, count, gathers, *refs):
    x_refs, y_refs = refs[:count], refs[count : 2 * count]
    send_sem, recv_sem = refs[2 * count], refs[2 * count + 1]
    n = lax.axis_size(axis)
    me = lax.axis_index(axis)

    barrier = pltpu.get_barrier_semaphore()
    for step in range(1, n):
        peer = lax.rem(me + step, n)
        pl.semaphore_signal(barrier, inc=1, device_id=device_of(axis, peer), device_id_type=MESH)
    pl.semaphore_wait(barrier, n - 1)

    copies = []
    for step in range(1, n):
        peer = lax.rem(me + step, n)
        for i in range(count):
            source = x_refs[i] if gathers[i] else x_refs[i].at[peer]
            copy = pltpu.make_async_remote_copy(
                src_ref=source,
                dst_ref=y_refs[i].at[me],
                send_sem=send_sem.at[i * n + peer],
                recv_sem=recv_sem.at[i * n + me],
                device_id=device_of(axis, peer),
                device_id_type=MESH,
            )
            copy.start()
            copies.append(copy)
    for i in range(count):
        y_refs[i][me] = x_refs[i][...] if gathers[i] else x_refs[i][me]
    for step in range(1, n):
        source_device = lax.rem(me + n - step, n)
        for i in range(count):
            copies[(step - 1) * count + i].wait_send()
            incoming = pltpu.make_async_remote_copy(
                src_ref=y_refs[i].at[source_device],
                dst_ref=y_refs[i].at[source_device],
                send_sem=send_sem.at[i * n + source_device],
                recv_sem=recv_sem.at[i * n + source_device],
                device_id=device_of(axis, source_device),
                device_id_type=MESH,
            )
            incoming.wait_recv()


def exchange(arrays, axis, collective_id, gathers=None):
    n = lax.axis_size(axis)
    count = len(arrays)
    gathers = tuple(gathers or (False,) * count)
    out_shapes = [
        jax.ShapeDtypeStruct(((n,) + a.shape) if g else a.shape, a.dtype) for a, g in zip(arrays, gathers)
    ]
    moved = sum(a.size * a.dtype.itemsize * (n if g else 1) for a, g in zip(arrays, gathers))
    return pl.pallas_call(
        functools.partial(exchange_kernel, axis, count, gathers),
        out_shape=out_shapes,
        in_specs=[pl.BlockSpec(memory_space=pltpu.VMEM)] * count,
        out_specs=[pl.BlockSpec(memory_space=pltpu.VMEM)] * count,
        scratch_shapes=[
            pltpu.SemaphoreType.DMA((count * n,)),
            pltpu.SemaphoreType.DMA((count * n,)),
        ],
        compiler_params=pltpu.CompilerParams(collective_id=collective_id, has_side_effects=True),
        cost_estimate=pl.CostEstimate(flops=0, transcendentals=0, bytes_accessed=2 * moved),
    )(*arrays)


def head_mass_kernel(query_ref, latent_ref, sums_ref, start_ref, position_ref, out_ref):
    rows, width = out_ref.shape
    scores = lax.dot_general(
        query_ref[...], latent_ref[...], (((1,), (1,)), ((), ())), preferred_element_type=jnp.float32
    )
    mass = jnp.exp(scores * main_scale - sums_ref[...])
    mass = jnp.sum(mass.reshape(rows, mass.shape[0] // rows, width), axis=1)
    columns = pl.program_id(0) * width + lax.broadcasted_iota(jnp.int32, (rows, width), 1)
    seen = (columns >= start_ref[...]) & (columns <= position_ref[...])
    out_ref[...] = jnp.where(seen, mass, 0.0)


def head_mass(flat_query, latent_piece, flat_sums, window_start, positions):
    query_rows = window_start.shape[0]
    tokens, latent_width = latent_piece.shape
    width = math.gcd(tokens, 256)
    flat_rows = flat_query.shape[0]
    return pl.pallas_call(
        head_mass_kernel,
        out_shape=jax.ShapeDtypeStruct((query_rows, tokens), jnp.float32),
        grid=(tokens // width,),
        in_specs=[
            pl.BlockSpec((flat_rows, latent_width), lambda k: (0, 0)),
            pl.BlockSpec((width, latent_width), lambda k: (k, 0)),
            pl.BlockSpec((flat_rows, 1), lambda k: (0, 0)),
            pl.BlockSpec((query_rows, 1), lambda k: (0, 0)),
            pl.BlockSpec((query_rows, 1), lambda k: (0, 0)),
        ],
        out_specs=pl.BlockSpec((query_rows, width), lambda k: (0, k)),
        cost_estimate=pl.CostEstimate(
            flops=2 * flat_rows * tokens * latent_width,
            transcendentals=flat_rows * tokens,
            bytes_accessed=flat_query.size * 2 + latent_piece.size * 2 + query_rows * tokens * 4,
        ),
    )(flat_query, latent_piece, flat_sums, window_start[:, None], positions[:, None])


def on_device(main_query, latent, log_sums, window_start, index_query, index_key, index_weight):
    query_rows, head_count, latent_width = main_query.shape
    index_width = index_query.shape[2]
    part_heads = index_query.shape[1]
    groups = lax.axis_size("ha")
    blocks = lax.axis_size("pb")
    tokens = query_rows * blocks
    own_rows = query_rows // groups
    index_heads = part_heads * groups
    block_first = lax.axis_index("pb") * query_rows
    flat_query = main_query.reshape(query_rows * head_count, latent_width)
    latent_piece = lax.all_gather(latent, "pb", axis=0, tiled=True)
    keys_all = lax.all_gather(index_key, "pb", axis=0, tiled=True)

    positions = block_first + jnp.arange(query_rows, dtype=jnp.int32)
    probs_part = head_mass(
        flat_query, latent_piece, log_sums.reshape(query_rows * head_count, 1), window_start, positions
    )

    probs_parts, index_parts, weight_parts = exchange(
        [
            probs_part.reshape(groups, own_rows, tokens),
            index_query.reshape(groups, own_rows * part_heads, index_width),
            index_weight.reshape(groups, 1, own_rows * part_heads),
        ],
        "ha",
        0,
    )
    probs_all = jnp.sum(probs_parts, axis=0)
    local_index = (
        index_parts.reshape(groups, own_rows, part_heads, index_width)
        .transpose(1, 0, 2, 3)
        .reshape(own_rows, index_heads, index_width)
    )
    local_weight = (
        weight_parts.reshape(groups, own_rows, part_heads).transpose(1, 0, 2).reshape(own_rows, index_heads)
    )
    row_first = block_first + lax.axis_index("ha") * own_rows
    own_positions = row_first + jnp.arange(own_rows, dtype=jnp.int32)
    own_start = lax.dynamic_slice_in_dim(window_start, lax.axis_index("ha") * own_rows, own_rows, 0)

    flat_index = local_index.reshape(own_rows * index_heads, index_width)
    active = jnp.einsum("rd,kd->rk", flat_index, keys_all, preferred_element_type=jnp.float32)
    active = active.reshape(own_rows, index_heads, tokens)
    relu_act = jnp.maximum(active, 0.0)
    logit_all = jnp.sum(local_weight[:, :, None] * relu_act, axis=1)

    visible_all = visible(own_start, own_positions, 0, tokens)
    target = probs_all / jnp.sum(probs_all, axis=1, keepdims=True)
    masked = jnp.where(visible_all, logit_all, very_low)
    row_top = jnp.max(masked, axis=1, keepdims=True)
    expo = jnp.where(visible_all, jnp.exp(masked - row_top), 0.0)
    logit_grad = jnp.where(visible_all, expo / jnp.sum(expo, axis=1, keepdims=True) - target, 0.0)

    weight_grad = jnp.sum(logit_grad[:, None, :] * relu_act, axis=2)
    coeffs = jnp.where(
        active > 0.0, logit_grad[:, None, :] * local_weight[:, :, None], 0.0
    ).astype(jnp.bfloat16)
    coeffs = coeffs.reshape(own_rows * index_heads, tokens)
    query_grad = jnp.dot(coeffs, keys_all, preferred_element_type=jnp.float32)
    key_grad = jnp.einsum("rk,rd->kd", coeffs, flat_index, preferred_element_type=jnp.float32)

    key_parts = exchange([key_grad.reshape(blocks, query_rows, index_width)], "pb", 1)[0]
    key_share = jnp.sum(key_parts, axis=0).reshape(groups, own_rows, index_width)

    query_grad = query_grad.astype(jnp.bfloat16).reshape(own_rows, groups, part_heads, index_width)
    query_back, weight_back, key_rows = exchange(
        [
            query_grad.transpose(1, 0, 2, 3).reshape(groups, own_rows * part_heads, index_width),
            weight_grad.reshape(own_rows, groups, part_heads)
            .transpose(1, 0, 2)
            .reshape(groups, 1, own_rows * part_heads),
            key_share,
        ],
        "ha",
        2,
    )
    query_output = query_back.reshape(query_rows, part_heads, index_width)
    weight_output = weight_back.reshape(query_rows, part_heads)
    key_rows = jnp.sum(key_rows, axis=0)
    key_output = exchange([key_rows], "ha", 3, gathers=(True,))[0]
    key_output = key_output.reshape(query_rows, index_width).astype(jnp.bfloat16)
    return (query_output, key_output, weight_output)


def solution(mesh):
    return jax.shard_map(
        on_device,
        mesh=mesh,
        in_specs=(
            P("pb", "ha", None),
            P("pb", None),
            P("pb", "ha"),
            P("pb"),
            P("pb", "ha", None),
            P("pb", None),
            P("pb", "ha"),
        ),
        out_specs=(P("pb", "ha", None), P("pb", None), P("pb", "ha")),
        check_vma=False,
    )
```

```python
import functools
import math

import jax
import jax.numpy as jnp
from jax import lax
from jax.experimental import pallas as pl
from jax.experimental.pallas import tpu as pltpu
from jax.sharding import PartitionSpec as P

main_scale = 192.0 ** (-0.5)
very_low = -1e30
MESH = pl.DeviceIdType.MESH
AXES = ("pb", "ha")


def visible(window_start, positions, first_row, width):
    columns = first_row + jnp.arange(width, dtype=jnp.int32)
    return (columns[None, :] >= window_start[:, None]) & (columns[None, :] <= positions[:, None])


def device_of(axis, peer):
    return tuple(peer if name == axis else lax.axis_index(name) for name in AXES)


def exchange_kernel(items, *refs):
    count = len(items)
    x_refs, y_refs = refs[:count], refs[count : 2 * count]
    send_sem, recv_sem = refs[2 * count], refs[2 * count + 1]
    axes = sorted({axis for axis, _ in items})
    stride = max(lax.axis_size(axis) for axis in axes)

    barrier = pltpu.get_barrier_semaphore()
    for axis in axes:
        n = lax.axis_size(axis)
        me = lax.axis_index(axis)
        for step in range(1, n):
            peer = lax.rem(me + step, n)
            pl.semaphore_signal(barrier, inc=1, device_id=device_of(axis, peer), device_id_type=MESH)
    pl.semaphore_wait(barrier, sum(lax.axis_size(axis) - 1 for axis in axes))

    copies = {}
    for step in range(1, max(lax.axis_size(axis) for axis in axes)):
        for i, (axis, gather) in enumerate(items):
            n = lax.axis_size(axis)
            if step >= n:
                continue
            me = lax.axis_index(axis)
            peer = lax.rem(me + step, n)
            source = x_refs[i] if gather else x_refs[i].at[peer]
            copy = pltpu.make_async_remote_copy(
                src_ref=source,
                dst_ref=y_refs[i].at[me],
                send_sem=send_sem.at[i * stride + peer],
                recv_sem=recv_sem.at[i * stride + me],
                device_id=device_of(axis, peer),
                device_id_type=MESH,
            )
            copy.start()
            copies[(i, step)] = copy
    for i, (axis, gather) in enumerate(items):
        me = lax.axis_index(axis)
        y_refs[i][me] = x_refs[i][...] if gather else x_refs[i][me]
    for step in range(1, max(lax.axis_size(axis) for axis in axes)):
        for i, (axis, gather) in enumerate(items):
            n = lax.axis_size(axis)
            if step >= n:
                continue
            me = lax.axis_index(axis)
            source_device = lax.rem(me + n - step, n)
            copies[(i, step)].wait_send()
            incoming = pltpu.make_async_remote_copy(
                src_ref=y_refs[i].at[source_device],
                dst_ref=y_refs[i].at[source_device],
                send_sem=send_sem.at[i * stride + source_device],
                recv_sem=recv_sem.at[i * stride + source_device],
                device_id=device_of(axis, source_device),
                device_id_type=MESH,
            )
            incoming.wait_recv()


def exchange(arrays, items, collective_id):
    count = len(arrays)
    items = tuple(items)
    out_shapes = [
        jax.ShapeDtypeStruct(((lax.axis_size(axis),) + a.shape) if g else a.shape, a.dtype)
        for a, (axis, g) in zip(arrays, items)
    ]
    moved = sum(
        a.size * a.dtype.itemsize * (lax.axis_size(axis) if g else 1) for a, (axis, g) in zip(arrays, items)
    )
    slots = count * max(lax.axis_size(axis) for axis, _ in items)
    return pl.pallas_call(
        functools.partial(exchange_kernel, items),
        out_shape=out_shapes,
        in_specs=[pl.BlockSpec(memory_space=pltpu.VMEM)] * count,
        out_specs=[pl.BlockSpec(memory_space=pltpu.VMEM)] * count,
        scratch_shapes=[pltpu.SemaphoreType.DMA((slots,)), pltpu.SemaphoreType.DMA((slots,))],
        compiler_params=pltpu.CompilerParams(
            collective_id=collective_id, has_side_effects=True, vmem_limit_bytes=48 * 1024 * 1024
        ),
        cost_estimate=pl.CostEstimate(flops=0, transcendentals=0, bytes_accessed=2 * moved),
    )(*arrays)


def head_mass_kernel(query_ref, latent_ref, sums_ref, start_ref, position_ref, out_ref):
    rows, width = out_ref.shape
    scores = lax.dot_general(
        query_ref[...], latent_ref[...], (((1,), (1,)), ((), ())), preferred_element_type=jnp.float32
    )
    mass = jnp.exp(scores * main_scale - sums_ref[...])
    mass = jnp.sum(mass.reshape(rows, mass.shape[0] // rows, width), axis=1)
    columns = pl.program_id(0) * width + lax.broadcasted_iota(jnp.int32, (rows, width), 1)
    seen = (columns >= start_ref[...]) & (columns <= position_ref[...])
    out_ref[...] = jnp.where(seen, mass, 0.0)


def head_mass(flat_query, latent_piece, flat_sums, window_start, positions):
    query_rows = window_start.shape[0]
    tokens, latent_width = latent_piece.shape
    width = math.gcd(tokens, 256)
    flat_rows = flat_query.shape[0]
    return pl.pallas_call(
        head_mass_kernel,
        out_shape=jax.ShapeDtypeStruct((query_rows, tokens), jnp.float32),
        grid=(tokens // width,),
        in_specs=[
            pl.BlockSpec((flat_rows, latent_width), lambda k: (0, 0)),
            pl.BlockSpec((width, latent_width), lambda k: (k, 0)),
            pl.BlockSpec((flat_rows, 1), lambda k: (0, 0)),
            pl.BlockSpec((query_rows, 1), lambda k: (0, 0)),
            pl.BlockSpec((query_rows, 1), lambda k: (0, 0)),
        ],
        out_specs=pl.BlockSpec((query_rows, width), lambda k: (0, k)),
        cost_estimate=pl.CostEstimate(
            flops=2 * flat_rows * tokens * latent_width,
            transcendentals=flat_rows * tokens,
            bytes_accessed=flat_query.size * 2 + latent_piece.size * 2 + query_rows * tokens * 4,
        ),
    )(flat_query, latent_piece, flat_sums, window_start[:, None], positions[:, None])


def on_device(main_query, latent, log_sums, window_start, index_query, index_key, index_weight):
    query_rows, head_count, latent_width = main_query.shape
    index_width = index_query.shape[2]
    part_heads = index_query.shape[1]
    groups = lax.axis_size("ha")
    blocks = lax.axis_size("pb")
    tokens = query_rows * blocks
    own_rows = query_rows // groups
    index_heads = part_heads * groups
    all_heads = head_count * groups
    block_first = lax.axis_index("pb") * query_rows

    latent_parts, key_parts, query_parts, sums_parts, index_parts, weight_parts = exchange(
        [
            latent,
            index_key,
            main_query.reshape(groups, own_rows * head_count, latent_width),
            log_sums.reshape(groups, 1, own_rows * head_count),
            index_query.reshape(groups, own_rows * part_heads, index_width),
            index_weight.reshape(groups, 1, own_rows * part_heads),
        ],
        [("pb", True), ("pb", True), ("ha", False), ("ha", False), ("ha", False), ("ha", False)],
        0,
    )
    latent_piece = latent_parts.reshape(tokens, latent_width)
    keys_all = key_parts.reshape(tokens, index_width)
    local_query = (
        query_parts.reshape(groups, own_rows, head_count, latent_width)
        .transpose(1, 0, 2, 3)
        .reshape(own_rows * all_heads, latent_width)
    )
    local_sums = (
        sums_parts.reshape(groups, own_rows, head_count).transpose(1, 0, 2).reshape(own_rows * all_heads, 1)
    )
    local_index = (
        index_parts.reshape(groups, own_rows, part_heads, index_width)
        .transpose(1, 0, 2, 3)
        .reshape(own_rows, index_heads, index_width)
    )
    local_weight = (
        weight_parts.reshape(groups, own_rows, part_heads).transpose(1, 0, 2).reshape(own_rows, index_heads)
    )
    row_first = block_first + lax.axis_index("ha") * own_rows
    own_positions = row_first + jnp.arange(own_rows, dtype=jnp.int32)
    own_start = lax.dynamic_slice_in_dim(window_start, lax.axis_index("ha") * own_rows, own_rows, 0)

    probs_all = head_mass(local_query, latent_piece, local_sums, own_start, own_positions)

    flat_index = local_index.reshape(own_rows * index_heads, index_width)
    active = jnp.einsum("rd,kd->rk", flat_index, keys_all, preferred_element_type=jnp.float32)
    active = active.reshape(own_rows, index_heads, tokens)
    relu_act = jnp.maximum(active, 0.0)
    logit_all = jnp.sum(local_weight[:, :, None] * relu_act, axis=1)

    visible_all = visible(own_start, own_positions, 0, tokens)
    target = probs_all / jnp.sum(probs_all, axis=1, keepdims=True)
    masked = jnp.where(visible_all, logit_all, very_low)
    row_top = jnp.max(masked, axis=1, keepdims=True)
    expo = jnp.where(visible_all, jnp.exp(masked - row_top), 0.0)
    logit_grad = jnp.where(visible_all, expo / jnp.sum(expo, axis=1, keepdims=True) - target, 0.0)

    weight_grad = jnp.sum(logit_grad[:, None, :] * relu_act, axis=2)
    coeffs = jnp.where(
        active > 0.0, logit_grad[:, None, :] * local_weight[:, :, None], 0.0
    ).astype(jnp.bfloat16)
    coeffs = coeffs.reshape(own_rows * index_heads, tokens)
    query_grad = jnp.dot(coeffs, keys_all, preferred_element_type=jnp.float32)
    key_grad = jnp.einsum("rk,rd->kd", coeffs, flat_index, preferred_element_type=jnp.float32)

    query_grad = query_grad.astype(jnp.bfloat16).reshape(own_rows, groups, part_heads, index_width)
    key_parts, query_back, weight_back = exchange(
        [
            key_grad.reshape(blocks, query_rows, index_width),
            query_grad.transpose(1, 0, 2, 3).reshape(groups, own_rows * part_heads, index_width),
            weight_grad.reshape(own_rows, groups, part_heads)
            .transpose(1, 0, 2)
            .reshape(groups, 1, own_rows * part_heads),
        ],
        [("pb", False), ("ha", False), ("ha", False)],
        1,
    )
    query_output = query_back.reshape(query_rows, part_heads, index_width)
    weight_output = weight_back.reshape(query_rows, part_heads)
    key_share = jnp.sum(key_parts, axis=0).reshape(groups, own_rows, index_width)
    key_rows = jnp.sum(exchange([key_share], [("ha", False)], 2)[0], axis=0)
    key_output = exchange([key_rows], [("ha", True)], 3)[0]
    key_output = key_output.reshape(query_rows, index_width).astype(jnp.bfloat16)
    return (query_output, key_output, weight_output)


def solution(mesh):
    return jax.shard_map(
        on_device,
        mesh=mesh,
        in_specs=(
            P("pb", "ha", None),
            P("pb", None),
            P("pb", "ha"),
            P("pb"),
            P("pb", "ha", None),
            P("pb", None),
            P("pb", "ha"),
        ),
        out_specs=(P("pb", "ha", None), P("pb", None), P("pb", "ha")),
        check_vma=False,
    )
```

```python
import functools
import math

import jax
import jax.numpy as jnp
from jax import lax
from jax.experimental import pallas as pl
from jax.experimental.pallas import tpu as pltpu
from jax.sharding import PartitionSpec as P

main_scale = 192.0 ** (-0.5)
very_low = -1e30
MESH = pl.DeviceIdType.MESH
AXES = ("pb", "ha")


def visible(window_start, positions, first_row, width):
    columns = first_row + jnp.arange(width, dtype=jnp.int32)
    return (columns[None, :] >= window_start[:, None]) & (columns[None, :] <= positions[:, None])


def device_of(axis, peer):
    return tuple(peer if name == axis else lax.axis_index(name) for name in AXES)


def pair_peers(axis):
    n = lax.axis_size(axis)
    me = lax.axis_index(axis)
    sibling = me + 1 - 2 * lax.rem(me, 2)
    return sibling, [lax.rem(me + 2 * step, n) for step in range(1, n // 2)]


def barrier_peers(items):
    peers = []
    for axis in sorted({axis for axis, _ in items}):
        n = lax.axis_size(axis)
        me = lax.axis_index(axis)
        modes = {mode for item_axis, mode in items if item_axis == axis}
        if modes == {"pair"}:
            sibling, others = pair_peers(axis)
            peers += [(axis, sibling)] + [(axis, peer) for peer in others]
        else:
            peers += [(axis, lax.rem(me + step, n)) for step in range(1, n)]
    return peers


def exchange_kernel(items, *refs):
    count = len(items)
    x_refs, y_refs = refs[:count], refs[count : 2 * count]
    send_sem, recv_sem = refs[2 * count], refs[2 * count + 1]
    stride = max(lax.axis_size(axis) for axis, _ in items)
    forward_base = count * stride

    def remote(i, axis, source, slot, target, send_slot, recv_slot):
        return pltpu.make_async_remote_copy(
            src_ref=source,
            dst_ref=y_refs[i].at[slot],
            send_sem=send_sem.at[send_slot],
            recv_sem=recv_sem.at[recv_slot],
            device_id=device_of(axis, target),
            device_id_type=MESH,
        )

    barrier = pltpu.get_barrier_semaphore()
    peers = barrier_peers(items)
    for axis, peer in peers:
        pl.semaphore_signal(barrier, inc=1, device_id=device_of(axis, peer), device_id_type=MESH)
    pl.semaphore_wait(barrier, len(peers))

    sends = []
    for i, (axis, mode) in enumerate(items):
        n = lax.axis_size(axis)
        me = lax.axis_index(axis)
        if mode == "pair":
            sibling, others = pair_peers(axis)
            targets = [sibling] + others
        else:
            targets = [lax.rem(me + step, n) for step in range(1, n)]
        for peer in targets:
            source = x_refs[i].at[peer] if mode == "a2a" else x_refs[i]
            copy = remote(i, axis, source, me, peer, i * stride + peer, i * stride + me)
            copy.start()
            sends.append(copy)
    for i, (axis, mode) in enumerate(items):
        me = lax.axis_index(axis)
        y_refs[i][me] = x_refs[i][me] if mode == "a2a" else x_refs[i][...]

    forwards = []
    for i, (axis, mode) in enumerate(items):
        if mode != "pair":
            continue
        sibling, others = pair_peers(axis)
        for block in others:
            arrived = remote(i, axis, y_refs[i].at[block], block, block, i * stride + block, i * stride + block)
            arrived.wait_recv()
            copy = remote(
                i, axis, y_refs[i].at[block], block, sibling, forward_base + i * stride + block,
                i * stride + block,
            )
            copy.start()
            forwards.append(copy)

    for i, (axis, mode) in enumerate(items):
        n = lax.axis_size(axis)
        me = lax.axis_index(axis)
        if mode == "pair":
            sibling, _ = pair_peers(axis)
            blocks = [sibling] + [lax.rem(sibling + 2 * step, n) for step in range(1, n // 2)]
        else:
            blocks = [lax.rem(me + n - step, n) for step in range(1, n)]
        for block in blocks:
            incoming = remote(i, axis, y_refs[i].at[block], block, block, i * stride + block, i * stride + block)
            incoming.wait_recv()
    for copy in sends + forwards:
        copy.wait_send()


def exchange(arrays, items, collective_id):
    count = len(arrays)
    items = tuple(items)
    out_shapes = [
        jax.ShapeDtypeStruct(a.shape if mode == "a2a" else ((lax.axis_size(axis),) + a.shape), a.dtype)
        for a, (axis, mode) in zip(arrays, items)
    ]
    moved = sum(
        a.size * a.dtype.itemsize * (1 if mode == "a2a" else lax.axis_size(axis))
        for a, (axis, mode) in zip(arrays, items)
    )
    slots = count * max(lax.axis_size(axis) for axis, _ in items)
    return pl.pallas_call(
        functools.partial(exchange_kernel, items),
        out_shape=out_shapes,
        in_specs=[pl.BlockSpec(memory_space=pltpu.VMEM)] * count,
        out_specs=[pl.BlockSpec(memory_space=pltpu.VMEM)] * count,
        scratch_shapes=[pltpu.SemaphoreType.DMA((2 * slots,)), pltpu.SemaphoreType.DMA((slots,))],
        compiler_params=pltpu.CompilerParams(
            collective_id=collective_id, has_side_effects=True, vmem_limit_bytes=48 * 1024 * 1024
        ),
        cost_estimate=pl.CostEstimate(flops=0, transcendentals=0, bytes_accessed=2 * moved),
    )(*arrays)


def head_mass_kernel(query_ref, latent_ref, sums_ref, start_ref, position_ref, out_ref):
    rows, width = out_ref.shape
    scores = lax.dot_general(
        query_ref[...], latent_ref[...], (((1,), (1,)), ((), ())), preferred_element_type=jnp.float32
    )
    mass = jnp.exp(scores * main_scale - sums_ref[...])
    mass = jnp.sum(mass.reshape(rows, mass.shape[0] // rows, width), axis=1)
    columns = pl.program_id(0) * width + lax.broadcasted_iota(jnp.int32, (rows, width), 1)
    seen = (columns >= start_ref[...]) & (columns <= position_ref[...])
    out_ref[...] = jnp.where(seen, mass, 0.0)


def head_mass(flat_query, latent_piece, flat_sums, window_start, positions):
    query_rows = window_start.shape[0]
    tokens, latent_width = latent_piece.shape
    width = math.gcd(tokens, 256)
    flat_rows = flat_query.shape[0]
    return pl.pallas_call(
        head_mass_kernel,
        out_shape=jax.ShapeDtypeStruct((query_rows, tokens), jnp.float32),
        grid=(tokens // width,),
        in_specs=[
            pl.BlockSpec((flat_rows, latent_width), lambda k: (0, 0)),
            pl.BlockSpec((width, latent_width), lambda k: (k, 0)),
            pl.BlockSpec((flat_rows, 1), lambda k: (0, 0)),
            pl.BlockSpec((query_rows, 1), lambda k: (0, 0)),
            pl.BlockSpec((query_rows, 1), lambda k: (0, 0)),
        ],
        out_specs=pl.BlockSpec((query_rows, width), lambda k: (0, k)),
        cost_estimate=pl.CostEstimate(
            flops=2 * flat_rows * tokens * latent_width,
            transcendentals=flat_rows * tokens,
            bytes_accessed=flat_query.size * 2 + latent_piece.size * 2 + query_rows * tokens * 4,
        ),
    )(flat_query, latent_piece, flat_sums, window_start[:, None], positions[:, None])


def on_device(main_query, latent, log_sums, window_start, index_query, index_key, index_weight):
    query_rows, head_count, latent_width = main_query.shape
    index_width = index_query.shape[2]
    part_heads = index_query.shape[1]
    groups = lax.axis_size("ha")
    blocks = lax.axis_size("pb")
    tokens = query_rows * blocks
    own_rows = query_rows // groups
    index_heads = part_heads * groups
    all_heads = head_count * groups
    block_first = lax.axis_index("pb") * query_rows

    latent_parts, key_parts, query_parts, sums_parts, index_parts, weight_parts = exchange(
        [
            latent,
            index_key,
            main_query.reshape(groups, own_rows * head_count, latent_width),
            log_sums.reshape(groups, 1, own_rows * head_count),
            index_query.reshape(groups, own_rows * part_heads, index_width),
            index_weight.reshape(groups, 1, own_rows * part_heads),
        ],
        [("pb", "pair"), ("pb", "pair"), ("ha", "a2a"), ("ha", "a2a"), ("ha", "a2a"), ("ha", "a2a")],
        0,
    )
    latent_piece = latent_parts.reshape(tokens, latent_width)
    keys_all = key_parts.reshape(tokens, index_width)
    local_query = (
        query_parts.reshape(groups, own_rows, head_count, latent_width)
        .transpose(1, 0, 2, 3)
        .reshape(own_rows * all_heads, latent_width)
    )
    local_sums = (
        sums_parts.reshape(groups, own_rows, head_count).transpose(1, 0, 2).reshape(own_rows * all_heads, 1)
    )
    local_index = (
        index_parts.reshape(groups, own_rows, part_heads, index_width)
        .transpose(1, 0, 2, 3)
        .reshape(own_rows, index_heads, index_width)
    )
    local_weight = (
        weight_parts.reshape(groups, own_rows, part_heads).transpose(1, 0, 2).reshape(own_rows, index_heads)
    )
    row_first = block_first + lax.axis_index("ha") * own_rows
    own_positions = row_first + jnp.arange(own_rows, dtype=jnp.int32)
    own_start = lax.dynamic_slice_in_dim(window_start, lax.axis_index("ha") * own_rows, own_rows, 0)

    probs_all = head_mass(local_query, latent_piece, local_sums, own_start, own_positions)

    flat_index = local_index.reshape(own_rows * index_heads, index_width)
    active = jnp.einsum("rd,kd->rk", flat_index, keys_all, preferred_element_type=jnp.float32)
    active = active.reshape(own_rows, index_heads, tokens)
    relu_act = jnp.maximum(active, 0.0)
    logit_all = jnp.sum(local_weight[:, :, None] * relu_act, axis=1)

    visible_all = visible(own_start, own_positions, 0, tokens)
    target = probs_all / jnp.sum(probs_all, axis=1, keepdims=True)
    masked = jnp.where(visible_all, logit_all, very_low)
    row_top = jnp.max(masked, axis=1, keepdims=True)
    expo = jnp.where(visible_all, jnp.exp(masked - row_top), 0.0)
    logit_grad = jnp.where(visible_all, expo / jnp.sum(expo, axis=1, keepdims=True) - target, 0.0)

    weight_grad = jnp.sum(logit_grad[:, None, :] * relu_act, axis=2)
    coeffs = jnp.where(
        active > 0.0, logit_grad[:, None, :] * local_weight[:, :, None], 0.0
    ).astype(jnp.bfloat16)
    coeffs = coeffs.reshape(own_rows * index_heads, tokens)
    query_grad = jnp.dot(coeffs, keys_all, preferred_element_type=jnp.float32)
    key_grad = jnp.einsum("rk,rd->kd", coeffs, flat_index, preferred_element_type=jnp.float32)

    query_grad = query_grad.astype(jnp.bfloat16).reshape(own_rows, groups, part_heads, index_width)
    key_parts, query_back, weight_back = exchange(
        [
            key_grad.reshape(blocks, query_rows, index_width),
            query_grad.transpose(1, 0, 2, 3).reshape(groups, own_rows * part_heads, index_width),
            weight_grad.reshape(own_rows, groups, part_heads)
            .transpose(1, 0, 2)
            .reshape(groups, 1, own_rows * part_heads),
        ],
        [("pb", "a2a"), ("ha", "a2a"), ("ha", "a2a")],
        1,
    )
    query_output = query_back.reshape(query_rows, part_heads, index_width)
    weight_output = weight_back.reshape(query_rows, part_heads)
    key_share = jnp.sum(key_parts, axis=0).reshape(groups, own_rows, index_width)
    key_rows = jnp.sum(exchange([key_share], [("ha", "a2a")], 2)[0], axis=0)
    key_output = exchange([key_rows], [("ha", "gather")], 3)[0]
    key_output = key_output.reshape(query_rows, index_width).astype(jnp.bfloat16)
    return (query_output, key_output, weight_output)


def solution(mesh):
    return jax.shard_map(
        on_device,
        mesh=mesh,
        in_specs=(
            P("pb", "ha", None),
            P("pb", None),
            P("pb", "ha"),
            P("pb"),
            P("pb", "ha", None),
            P("pb", None),
            P("pb", "ha"),
        ),
        out_specs=(P("pb", "ha", None), P("pb", None), P("pb", "ha")),
        check_vma=False,
    )
```

```python
import functools
import math

import jax
import jax.numpy as jnp
from jax import lax
from jax.experimental import pallas as pl
from jax.experimental.pallas import tpu as pltpu
from jax.sharding import PartitionSpec as P

main_scale = 192.0 ** (-0.5)
very_low = -1e30
MESH = pl.DeviceIdType.MESH
AXES = ("pb", "ha")


def visible(window_start, positions, first_row, width):
    columns = first_row + jnp.arange(width, dtype=jnp.int32)
    return (columns[None, :] >= window_start[:, None]) & (columns[None, :] <= positions[:, None])


def device_of(axis, peer):
    return tuple(peer if name == axis else lax.axis_index(name) for name in AXES)


def pair_peers(axis):
    n = lax.axis_size(axis)
    me = lax.axis_index(axis)
    sibling = me + 1 - 2 * lax.rem(me, 2)
    return sibling, [lax.rem(me + 2 * step, n) for step in range(1, n // 2)]


def barrier_peers(items):
    peers = []
    for axis in sorted({axis for axis, _, _ in items}):
        n = lax.axis_size(axis)
        me = lax.axis_index(axis)
        modes = {mode for item_axis, mode, _ in items if item_axis == axis}
        sibling, others = pair_peers(axis)
        if modes == {"sib"}:
            peers += [(axis, sibling)]
        elif modes == {"same"}:
            peers += [(axis, peer) for peer in others]
        elif modes == {"pair"}:
            peers += [(axis, sibling)] + [(axis, peer) for peer in others]
        else:
            peers += [(axis, lax.rem(me + step, n)) for step in range(1, n)]
    return peers


def plan(axis, mode):
    n = lax.axis_size(axis)
    me = lax.axis_index(axis)
    sibling, others = pair_peers(axis)
    if mode == "a2a":
        return (
            [(lax.rem(me + s, n), lax.rem(me + s, n), me) for s in range(1, n)],
            [(lax.rem(me + n - s, n), lax.rem(me + n - s, n)) for s in range(1, n)],
        )
    if mode == "gather":
        return (
            [(lax.rem(me + s, n), None, me) for s in range(1, n)],
            [(lax.rem(me + n - s, n), lax.rem(me + n - s, n)) for s in range(1, n)],
        )
    if mode == "sib":
        parity = lax.rem(sibling, 2)
        return (
            [(sibling, 2 * j + parity, j) for j in range(n // 2)],
            [(sibling, j) for j in range(n // 2)],
        )
    if mode == "same":
        return (
            [(peer, peer // 2, me // 2) for peer in others],
            [(lax.rem(me + n - 2 * s, n), lax.rem(me + n - 2 * s, n) // 2) for s in range(1, n // 2)],
        )
    return (
        [(peer, None, me) for peer in [sibling] + others],
        [(sibling, sibling)] + [(lax.rem(sibling + 2 * s, n),) * 2 for s in range(1, n // 2)],
    )


def exchange_kernel(items, *refs):
    count = len(items)
    x_refs, y_refs = refs[:count], refs[count : 2 * count]
    send_sem, recv_sem, local_sem = refs[2 * count : 2 * count + 3]
    stride = max(lax.axis_size(axis) for axis, _, _ in items)
    forward_base = count * stride

    def remote(i, axis, source, slot, target, send_slot, recv_slot):
        return pltpu.make_async_remote_copy(
            src_ref=source,
            dst_ref=y_refs[i].at[slot],
            send_sem=send_sem.at[send_slot],
            recv_sem=recv_sem.at[recv_slot],
            device_id=device_of(axis, target),
            device_id_type=MESH,
        )

    barrier = pltpu.get_barrier_semaphore()
    peers = barrier_peers(items)
    for axis, peer in peers:
        pl.semaphore_signal(barrier, inc=1, device_id=device_of(axis, peer), device_id_type=MESH)
    pl.semaphore_wait(barrier, len(peers))

    sends = []
    for i, (axis, mode, _) in enumerate(items):
        for peer, chunk, slot in plan(axis, mode)[0]:
            source = x_refs[i] if chunk is None else x_refs[i].at[chunk]
            send_slot = i * stride + (chunk if mode == "sib" else peer)
            copy = remote(i, axis, source, slot, peer, send_slot, i * stride + slot)
            copy.start()
            sends.append(copy)
    locals_ = []
    for i, (axis, mode, _) in enumerate(items):
        me = lax.axis_index(axis)
        if mode == "sib":
            continue
        if mode == "same":
            own = (x_refs[i].at[me // 2], y_refs[i].at[me // 2])
        elif mode == "a2a":
            own = (x_refs[i].at[me], y_refs[i].at[me])
        else:
            own = (x_refs[i], y_refs[i].at[me])
        copy = pltpu.make_async_copy(own[0], own[1], local_sem.at[i])
        copy.start()
        locals_.append(copy)

    forwards = []
    for i, (axis, mode, _) in enumerate(items):
        if mode != "pair":
            continue
        sibling, others = pair_peers(axis)
        for block in others:
            arrived = remote(i, axis, y_refs[i].at[block], block, block, i * stride + block, i * stride + block)
            arrived.wait_recv()
            copy = remote(
                i, axis, y_refs[i].at[block], block, sibling, forward_base + i * stride + block,
                i * stride + block,
            )
            copy.start()
            forwards.append(copy)

    for i, (axis, mode, _) in enumerate(items):
        for peer, slot in plan(axis, mode)[1]:
            incoming = remote(i, axis, y_refs[i].at[slot], slot, peer, i * stride + slot, i * stride + slot)
            incoming.wait_recv()
    for copy in sends + forwards:
        copy.wait_send()
    for copy in locals_:
        copy.wait()


def exchange(arrays, items, collective_id):
    count = len(arrays)
    items = tuple(items)

    def out_shape(a, axis, mode):
        n = lax.axis_size(axis)
        if mode == "a2a":
            return a.shape
        if mode in ("sib", "same"):
            return (n // 2,) + a.shape[1:]
        return (n,) + a.shape

    out_shapes = [jax.ShapeDtypeStruct(out_shape(a, axis, mode), a.dtype) for a, (axis, mode, _) in zip(arrays, items)]
    moved = sum(math.prod(o.shape) * a.dtype.itemsize for a, o in zip(arrays, out_shapes))
    slots = count * max(lax.axis_size(axis) for axis, _, _ in items)
    space = [pl.BlockSpec(memory_space=pl.ANY if hbm else pltpu.VMEM) for _, _, hbm in items]
    return pl.pallas_call(
        functools.partial(exchange_kernel, items),
        out_shape=out_shapes,
        in_specs=space,
        out_specs=[pl.BlockSpec(memory_space=pltpu.VMEM)] * count,
        scratch_shapes=[
            pltpu.SemaphoreType.DMA((2 * slots,)),
            pltpu.SemaphoreType.DMA((slots,)),
            pltpu.SemaphoreType.DMA((count,)),
        ],
        compiler_params=pltpu.CompilerParams(
            collective_id=collective_id, has_side_effects=True, vmem_limit_bytes=48 * 1024 * 1024
        ),
        cost_estimate=pl.CostEstimate(flops=0, transcendentals=0, bytes_accessed=2 * moved),
    )(*arrays)


def head_mass_kernel(query_ref, latent_ref, sums_ref, start_ref, position_ref, out_ref):
    rows, width = out_ref.shape
    scores = lax.dot_general(
        query_ref[...], latent_ref[...], (((1,), (1,)), ((), ())), preferred_element_type=jnp.float32
    )
    mass = jnp.exp(scores * main_scale - sums_ref[...])
    mass = jnp.sum(mass.reshape(rows, mass.shape[0] // rows, width), axis=1)
    columns = pl.program_id(0) * width + lax.broadcasted_iota(jnp.int32, (rows, width), 1)
    seen = (columns >= start_ref[...]) & (columns <= position_ref[...])
    out_ref[...] = jnp.where(seen, mass, 0.0)


def head_mass(flat_query, latent_piece, flat_sums, window_start, positions):
    query_rows = window_start.shape[0]
    tokens, latent_width = latent_piece.shape
    width = math.gcd(tokens, 256)
    flat_rows = flat_query.shape[0]
    return pl.pallas_call(
        head_mass_kernel,
        out_shape=jax.ShapeDtypeStruct((query_rows, tokens), jnp.float32),
        grid=(tokens // width,),
        in_specs=[
            pl.BlockSpec((flat_rows, latent_width), lambda k: (0, 0)),
            pl.BlockSpec((width, latent_width), lambda k: (k, 0)),
            pl.BlockSpec((flat_rows, 1), lambda k: (0, 0)),
            pl.BlockSpec((query_rows, 1), lambda k: (0, 0)),
            pl.BlockSpec((query_rows, 1), lambda k: (0, 0)),
        ],
        out_specs=pl.BlockSpec((query_rows, width), lambda k: (0, k)),
        cost_estimate=pl.CostEstimate(
            flops=2 * flat_rows * tokens * latent_width,
            transcendentals=flat_rows * tokens,
            bytes_accessed=flat_query.size * 2 + latent_piece.size * 2 + query_rows * tokens * 4,
        ),
    )(flat_query, latent_piece, flat_sums, window_start[:, None], positions[:, None])


def on_device(main_query, latent, log_sums, window_start, index_query, index_key, index_weight):
    query_rows, head_count, latent_width = main_query.shape
    index_width = index_query.shape[2]
    part_heads = index_query.shape[1]
    groups = lax.axis_size("ha")
    blocks = lax.axis_size("pb")
    tokens = query_rows * blocks
    own_rows = query_rows // groups
    index_heads = part_heads * groups
    all_heads = head_count * groups
    block_first = lax.axis_index("pb") * query_rows

    latent_parts, key_parts, query_parts, sums_parts, index_parts, weight_parts = exchange(
        [
            latent,
            index_key,
            main_query.reshape(groups, own_rows * head_count, latent_width),
            log_sums.reshape(groups, 1, own_rows * head_count),
            index_query.reshape(groups, own_rows * part_heads, index_width),
            index_weight.reshape(groups, 1, own_rows * part_heads),
        ],
        [
            ("pb", "pair", False),
            ("pb", "pair", False),
            ("ha", "a2a", True),
            ("ha", "a2a", False),
            ("ha", "a2a", False),
            ("ha", "a2a", False),
        ],
        0,
    )
    latent_piece = latent_parts.reshape(tokens, latent_width)
    keys_all = key_parts.reshape(tokens, index_width)
    local_query = (
        query_parts.reshape(groups, own_rows, head_count, latent_width)
        .transpose(1, 0, 2, 3)
        .reshape(own_rows * all_heads, latent_width)
    )
    local_sums = (
        sums_parts.reshape(groups, own_rows, head_count).transpose(1, 0, 2).reshape(own_rows * all_heads, 1)
    )
    local_index = (
        index_parts.reshape(groups, own_rows, part_heads, index_width)
        .transpose(1, 0, 2, 3)
        .reshape(own_rows, index_heads, index_width)
    )
    local_weight = (
        weight_parts.reshape(groups, own_rows, part_heads).transpose(1, 0, 2).reshape(own_rows, index_heads)
    )
    row_first = block_first + lax.axis_index("ha") * own_rows
    own_positions = row_first + jnp.arange(own_rows, dtype=jnp.int32)
    own_start = lax.dynamic_slice_in_dim(window_start, lax.axis_index("ha") * own_rows, own_rows, 0)

    probs_all = head_mass(local_query, latent_piece, local_sums, own_start, own_positions)

    flat_index = local_index.reshape(own_rows * index_heads, index_width)
    active = jnp.einsum("rd,kd->rk", flat_index, keys_all, preferred_element_type=jnp.float32)
    active = active.reshape(own_rows, index_heads, tokens)
    relu_act = jnp.maximum(active, 0.0)
    logit_all = jnp.sum(local_weight[:, :, None] * relu_act, axis=1)

    visible_all = visible(own_start, own_positions, 0, tokens)
    target = probs_all / jnp.sum(probs_all, axis=1, keepdims=True)
    masked = jnp.where(visible_all, logit_all, very_low)
    row_top = jnp.max(masked, axis=1, keepdims=True)
    expo = jnp.where(visible_all, jnp.exp(masked - row_top), 0.0)
    logit_grad = jnp.where(visible_all, expo / jnp.sum(expo, axis=1, keepdims=True) - target, 0.0)

    weight_grad = jnp.sum(logit_grad[:, None, :] * relu_act, axis=2)
    coeffs = jnp.where(
        active > 0.0, logit_grad[:, None, :] * local_weight[:, :, None], 0.0
    ).astype(jnp.bfloat16)
    coeffs = coeffs.reshape(own_rows * index_heads, tokens)
    query_grad = jnp.dot(coeffs, keys_all, preferred_element_type=jnp.float32)
    key_grad = jnp.einsum("rk,rd->kd", coeffs, flat_index, preferred_element_type=jnp.float32)

    query_grad = query_grad.astype(jnp.bfloat16).reshape(own_rows, groups, part_heads, index_width)
    key_grad = key_grad.reshape(blocks, query_rows, index_width)
    sibling_part = exchange([key_grad], [("pb", "sib", False)], 1)[0]
    parity = lax.rem(lax.axis_index("pb"), 2)
    own_part = lax.dynamic_index_in_dim(
        key_grad.reshape(blocks // 2, 2, query_rows, index_width), parity, axis=1, keepdims=False
    )
    key_parts, query_back, weight_back = exchange(
        [
            own_part + sibling_part,
            query_grad.transpose(1, 0, 2, 3).reshape(groups, own_rows * part_heads, index_width),
            weight_grad.reshape(own_rows, groups, part_heads)
            .transpose(1, 0, 2)
            .reshape(groups, 1, own_rows * part_heads),
        ],
        [("pb", "same", False), ("ha", "a2a", False), ("ha", "a2a", False)],
        4,
    )
    query_output = query_back.reshape(query_rows, part_heads, index_width)
    weight_output = weight_back.reshape(query_rows, part_heads)
    key_share = jnp.sum(key_parts, axis=0).reshape(groups, own_rows, index_width)
    key_rows = jnp.sum(exchange([key_share], [("ha", "a2a", False)], 2)[0], axis=0)
    key_output = exchange([key_rows], [("ha", "gather", False)], 3)[0]
    key_output = key_output.reshape(query_rows, index_width).astype(jnp.bfloat16)
    return (query_output, key_output, weight_output)


def solution(mesh):
    return jax.shard_map(
        on_device,
        mesh=mesh,
        in_specs=(
            P("pb", "ha", None),
            P("pb", None),
            P("pb", "ha"),
            P("pb"),
            P("pb", "ha", None),
            P("pb", None),
            P("pb", "ha"),
        ),
        out_specs=(P("pb", "ha", None), P("pb", None), P("pb", "ha")),
        check_vma=False,
    )
```

```python
import functools
import math

import jax
import jax.numpy as jnp
from jax import lax
from jax.experimental import pallas as pl
from jax.experimental.pallas import tpu as pltpu
from jax.sharding import PartitionSpec as P

main_scale = 192.0 ** (-0.5)
very_low = -1e30
MESH = pl.DeviceIdType.MESH
AXES = ("pb", "ha")


def visible(window_start, positions, first_row, width):
    columns = first_row + jnp.arange(width, dtype=jnp.int32)
    return (columns[None, :] >= window_start[:, None]) & (columns[None, :] <= positions[:, None])


def device_of(axis, peer):
    return tuple(peer if name == axis else lax.axis_index(name) for name in AXES)


def pair_peers(axis):
    n = lax.axis_size(axis)
    me = lax.axis_index(axis)
    sibling = me + 1 - 2 * lax.rem(me, 2)
    return sibling, [lax.rem(me + 2 * step, n) for step in range(1, n // 2)]


def barrier_peers(items):
    peers = []
    for axis in sorted({axis for axis, _, _ in items}):
        n = lax.axis_size(axis)
        me = lax.axis_index(axis)
        modes = {mode for item_axis, mode, _ in items if item_axis == axis}
        sibling, others = pair_peers(axis)
        if modes == {"sib"}:
            peers += [(axis, sibling)]
        elif modes == {"same"}:
            peers += [(axis, peer) for peer in others]
        elif modes == {"pair"}:
            peers += [(axis, sibling)] + [(axis, peer) for peer in others]
        else:
            peers += [(axis, lax.rem(me + step, n)) for step in range(1, n)]
    return peers


def plan(axis, mode):
    n = lax.axis_size(axis)
    me = lax.axis_index(axis)
    sibling, others = pair_peers(axis)
    if mode == "a2a":
        return (
            [(lax.rem(me + s, n), lax.rem(me + s, n), me) for s in range(1, n)],
            [(lax.rem(me + n - s, n), lax.rem(me + n - s, n)) for s in range(1, n)],
        )
    if mode == "gather":
        return (
            [(lax.rem(me + s, n), None, me) for s in range(1, n)],
            [(lax.rem(me + n - s, n), lax.rem(me + n - s, n)) for s in range(1, n)],
        )
    if mode == "sib":
        parity = lax.rem(sibling, 2)
        return (
            [(sibling, 2 * j + parity, j) for j in range(n // 2)],
            [(sibling, j) for j in range(n // 2)],
        )
    if mode == "same":
        return (
            [(peer, peer // 2, me // 2) for peer in others],
            [(lax.rem(me + n - 2 * s, n), lax.rem(me + n - 2 * s, n) // 2) for s in range(1, n // 2)],
        )
    return (
        [(peer, None, me) for peer in [sibling] + others],
        [(sibling, sibling)] + [(lax.rem(sibling + 2 * s, n),) * 2 for s in range(1, n // 2)],
    )


def exchange_kernel(items, *refs):
    count = len(items)
    x_refs, y_refs = refs[:count], refs[count : 2 * count]
    send_sem, recv_sem, local_sem = refs[2 * count : 2 * count + 3]
    stride = max(lax.axis_size(axis) for axis, _, _ in items)
    forward_base = count * stride

    def remote(i, axis, source, slot, target, send_slot, recv_slot):
        return pltpu.make_async_remote_copy(
            src_ref=source,
            dst_ref=y_refs[i].at[slot],
            send_sem=send_sem.at[send_slot],
            recv_sem=recv_sem.at[recv_slot],
            device_id=device_of(axis, target),
            device_id_type=MESH,
        )

    barrier = pltpu.get_barrier_semaphore()
    peers = barrier_peers(items)
    for axis, peer in peers:
        pl.semaphore_signal(barrier, inc=1, device_id=device_of(axis, peer), device_id_type=MESH)
    pl.semaphore_wait(barrier, len(peers))

    sends = []
    for i, (axis, mode, _) in enumerate(items):
        for peer, chunk, slot in plan(axis, mode)[0]:
            source = x_refs[i] if chunk is None else x_refs[i].at[chunk]
            send_slot = i * stride + (chunk if mode == "sib" else peer)
            copy = remote(i, axis, source, slot, peer, send_slot, i * stride + slot)
            copy.start()
            sends.append(copy)
    locals_ = []
    for i, (axis, mode, _) in enumerate(items):
        me = lax.axis_index(axis)
        if mode == "sib":
            continue
        if mode == "same":
            own = (x_refs[i].at[me // 2], y_refs[i].at[me // 2])
        elif mode == "a2a":
            own = (x_refs[i].at[me], y_refs[i].at[me])
        else:
            own = (x_refs[i], y_refs[i].at[me])
        copy = pltpu.make_async_copy(own[0], own[1], local_sem.at[i])
        copy.start()
        locals_.append(copy)

    forwards = []
    for i, (axis, mode, _) in enumerate(items):
        if mode != "pair":
            continue
        sibling, others = pair_peers(axis)
        for block in others:
            arrived = remote(i, axis, y_refs[i].at[block], block, block, i * stride + block, i * stride + block)
            arrived.wait_recv()
            copy = remote(
                i, axis, y_refs[i].at[block], block, sibling, forward_base + i * stride + block,
                i * stride + block,
            )
            copy.start()
            forwards.append(copy)

    for i, (axis, mode, _) in enumerate(items):
        for peer, slot in plan(axis, mode)[1]:
            incoming = remote(i, axis, y_refs[i].at[slot], slot, peer, i * stride + slot, i * stride + slot)
            incoming.wait_recv()
    for copy in sends + forwards:
        copy.wait_send()
    for copy in locals_:
        copy.wait()


def exchange(arrays, items, collective_id):
    count = len(arrays)
    items = tuple(items)

    def out_shape(a, axis, mode):
        n = lax.axis_size(axis)
        if mode == "a2a":
            return a.shape
        if mode in ("sib", "same"):
            return (n // 2,) + a.shape[1:]
        return (n,) + a.shape

    out_shapes = [jax.ShapeDtypeStruct(out_shape(a, axis, mode), a.dtype) for a, (axis, mode, _) in zip(arrays, items)]
    moved = sum(math.prod(o.shape) * a.dtype.itemsize for a, o in zip(arrays, out_shapes))
    slots = count * max(lax.axis_size(axis) for axis, _, _ in items)
    space = [pl.BlockSpec(memory_space=pl.ANY if hbm else pltpu.VMEM) for _, _, hbm in items]
    return pl.pallas_call(
        functools.partial(exchange_kernel, items),
        out_shape=out_shapes,
        in_specs=space,
        out_specs=[pl.BlockSpec(memory_space=pltpu.VMEM)] * count,
        scratch_shapes=[
            pltpu.SemaphoreType.DMA((2 * slots,)),
            pltpu.SemaphoreType.DMA((slots,)),
            pltpu.SemaphoreType.DMA((count,)),
        ],
        compiler_params=pltpu.CompilerParams(
            collective_id=collective_id, has_side_effects=True, vmem_limit_bytes=48 * 1024 * 1024
        ),
        cost_estimate=pl.CostEstimate(flops=0, transcendentals=0, bytes_accessed=2 * moved),
    )(*arrays)


def head_mass_kernel(query_ref, latent_ref, sums_ref, start_ref, position_ref, out_ref):
    rows, width = out_ref.shape
    scores = lax.dot_general(
        query_ref[...], latent_ref[...], (((1,), (1,)), ((), ())), preferred_element_type=jnp.float32
    )
    mass = jnp.exp(scores * main_scale - sums_ref[...])
    mass = jnp.sum(mass.reshape(rows, mass.shape[0] // rows, width), axis=1)
    columns = pl.program_id(0) * width + lax.broadcasted_iota(jnp.int32, (rows, width), 1)
    seen = (columns >= start_ref[...]) & (columns <= position_ref[...])
    out_ref[...] = jnp.where(seen, mass, 0.0)


def head_mass(flat_query, latent_piece, flat_sums, window_start, positions):
    query_rows = window_start.shape[0]
    tokens, latent_width = latent_piece.shape
    width = math.gcd(tokens, 256)
    flat_rows = flat_query.shape[0]
    return pl.pallas_call(
        head_mass_kernel,
        out_shape=jax.ShapeDtypeStruct((query_rows, tokens), jnp.float32),
        grid=(tokens // width,),
        in_specs=[
            pl.BlockSpec((flat_rows, latent_width), lambda k: (0, 0)),
            pl.BlockSpec((width, latent_width), lambda k: (k, 0)),
            pl.BlockSpec((flat_rows, 1), lambda k: (0, 0)),
            pl.BlockSpec((query_rows, 1), lambda k: (0, 0)),
            pl.BlockSpec((query_rows, 1), lambda k: (0, 0)),
        ],
        out_specs=pl.BlockSpec((query_rows, width), lambda k: (0, k)),
        cost_estimate=pl.CostEstimate(
            flops=2 * flat_rows * tokens * latent_width,
            transcendentals=flat_rows * tokens,
            bytes_accessed=flat_query.size * 2 + latent_piece.size * 2 + query_rows * tokens * 4,
        ),
    )(flat_query, latent_piece, flat_sums, window_start[:, None], positions[:, None])


def on_device(main_query, latent, log_sums, window_start, index_query, index_key, index_weight):
    query_rows, head_count, latent_width = main_query.shape
    index_width = index_query.shape[2]
    part_heads = index_query.shape[1]
    groups = lax.axis_size("ha")
    blocks = lax.axis_size("pb")
    tokens = query_rows * blocks
    own_rows = query_rows // groups
    index_heads = part_heads * groups
    all_heads = head_count * groups
    block_first = lax.axis_index("pb") * query_rows

    latent_parts, key_parts, query_parts, sums_parts, index_parts, weight_parts = exchange(
        [
            latent,
            index_key,
            main_query.reshape(groups, own_rows * head_count, latent_width),
            log_sums.reshape(groups, 1, own_rows * head_count),
            index_query.reshape(groups, own_rows * part_heads, index_width),
            index_weight.reshape(groups, 1, own_rows * part_heads),
        ],
        [
            ("pb", "pair", False),
            ("pb", "pair", False),
            ("ha", "a2a", True),
            ("ha", "a2a", False),
            ("ha", "a2a", False),
            ("ha", "a2a", False),
        ],
        0,
    )
    latent_piece = latent_parts.reshape(tokens, latent_width)
    keys_all = key_parts.reshape(tokens, index_width)
    local_query = (
        query_parts.reshape(groups, own_rows, head_count, latent_width)
        .transpose(1, 0, 2, 3)
        .reshape(own_rows * all_heads, latent_width)
    )
    local_sums = (
        sums_parts.reshape(groups, own_rows, head_count).transpose(1, 0, 2).reshape(own_rows * all_heads, 1)
    )
    local_index = (
        index_parts.reshape(groups, own_rows, part_heads, index_width)
        .transpose(1, 0, 2, 3)
        .reshape(own_rows, index_heads, index_width)
    )
    local_weight = (
        weight_parts.reshape(groups, own_rows, part_heads).transpose(1, 0, 2).reshape(own_rows, index_heads)
    )
    row_first = block_first + lax.axis_index("ha") * own_rows
    own_positions = row_first + jnp.arange(own_rows, dtype=jnp.int32)
    own_start = lax.dynamic_slice_in_dim(window_start, lax.axis_index("ha") * own_rows, own_rows, 0)

    probs_all = head_mass(local_query, latent_piece, local_sums, own_start, own_positions)

    flat_index = local_index.reshape(own_rows * index_heads, index_width)
    active = jnp.einsum("rd,kd->rk", flat_index, keys_all, preferred_element_type=jnp.float32)
    active = active.reshape(own_rows, index_heads, tokens)
    relu_act = jnp.maximum(active, 0.0)
    logit_all = jnp.sum(local_weight[:, :, None] * relu_act, axis=1)

    visible_all = visible(own_start, own_positions, 0, tokens)
    target = probs_all / jnp.sum(probs_all, axis=1, keepdims=True)
    masked = jnp.where(visible_all, logit_all, very_low)
    row_top = jnp.max(masked, axis=1, keepdims=True)
    expo = jnp.where(visible_all, jnp.exp(masked - row_top), 0.0)
    logit_grad = jnp.where(visible_all, expo / jnp.sum(expo, axis=1, keepdims=True) - target, 0.0)

    weight_grad = jnp.sum(logit_grad[:, None, :] * relu_act, axis=2)
    coeffs = jnp.where(
        active > 0.0, logit_grad[:, None, :] * local_weight[:, :, None], 0.0
    ).astype(jnp.bfloat16)
    coeffs = coeffs.reshape(own_rows * index_heads, tokens)
    query_grad = jnp.dot(coeffs, keys_all, preferred_element_type=jnp.float32)
    key_grad = jnp.einsum("rk,rd->kd", coeffs, flat_index, preferred_element_type=jnp.float32)

    query_grad = query_grad.astype(jnp.bfloat16).reshape(own_rows, groups, part_heads, index_width)
    key_grad = key_grad.reshape(blocks, query_rows, index_width)
    sibling_part = exchange([key_grad], [("pb", "sib", False)], 1)[0]
    parity = lax.rem(lax.axis_index("pb"), 2)
    own_part = lax.dynamic_index_in_dim(
        key_grad.reshape(blocks // 2, 2, query_rows, index_width), parity, axis=1, keepdims=False
    )
    key_parts = exchange([own_part + sibling_part], [("pb", "same", False)], 4)[0]
    key_share = jnp.sum(key_parts, axis=0).reshape(groups, own_rows, index_width)
    key_rows, query_back, weight_back = exchange(
        [
            key_share,
            query_grad.transpose(1, 0, 2, 3).reshape(groups, own_rows * part_heads, index_width),
            weight_grad.reshape(own_rows, groups, part_heads)
            .transpose(1, 0, 2)
            .reshape(groups, 1, own_rows * part_heads),
        ],
        [("ha", "a2a", False), ("ha", "a2a", False), ("ha", "a2a", False)],
        2,
    )
    query_output = query_back.reshape(query_rows, part_heads, index_width)
    weight_output = weight_back.reshape(query_rows, part_heads)
    key_output = exchange([jnp.sum(key_rows, axis=0)], [("ha", "gather", False)], 3)[0]
    key_output = key_output.reshape(query_rows, index_width).astype(jnp.bfloat16)
    return (query_output, key_output, weight_output)


def solution(mesh):
    return jax.shard_map(
        on_device,
        mesh=mesh,
        in_specs=(
            P("pb", "ha", None),
            P("pb", None),
            P("pb", "ha"),
            P("pb"),
            P("pb", "ha", None),
            P("pb", None),
            P("pb", "ha"),
        ),
        out_specs=(P("pb", "ha", None), P("pb", None), P("pb", "ha")),
        check_vma=False,
    )
```

```python
import functools
import math

import jax
import jax.numpy as jnp
from jax import lax
from jax.experimental import pallas as pl
from jax.experimental.pallas import tpu as pltpu
from jax.sharding import PartitionSpec as P

main_scale = 192.0 ** (-0.5)
very_low = -1e30
MESH = pl.DeviceIdType.MESH
AXES = ("pb", "ha")


def visible(window_start, positions, first_row, width):
    columns = first_row + jnp.arange(width, dtype=jnp.int32)
    return (columns[None, :] >= window_start[:, None]) & (columns[None, :] <= positions[:, None])


def device_of(axis, peer):
    return tuple(peer if name == axis else lax.axis_index(name) for name in AXES)


def pair_peers(axis):
    n = lax.axis_size(axis)
    me = lax.axis_index(axis)
    sibling = me + 1 - 2 * lax.rem(me, 2)
    return sibling, [lax.rem(me + 2 * step, n) for step in range(1, n // 2)]


def barrier_peers(items):
    peers = []
    for axis in sorted({axis for axis, _, _ in items}):
        n = lax.axis_size(axis)
        me = lax.axis_index(axis)
        modes = {mode for item_axis, mode, _ in items if item_axis == axis}
        sibling, others = pair_peers(axis)
        if modes == {"sib"}:
            peers += [(axis, sibling)]
        elif modes == {"same"}:
            peers += [(axis, peer) for peer in others]
        elif modes == {"pair"}:
            peers += [(axis, sibling)] + [(axis, peer) for peer in others]
        else:
            peers += [(axis, lax.rem(me + step, n)) for step in range(1, n)]
    return peers


def plan(axis, mode):
    n = lax.axis_size(axis)
    me = lax.axis_index(axis)
    sibling, others = pair_peers(axis)
    always = None
    if mode == "a2a":
        return (
            [(lax.rem(me + s, n), lax.rem(me + s, n), me, always) for s in range(1, n)],
            [(lax.rem(me + n - s, n), lax.rem(me + n - s, n), always) for s in range(1, n)],
        )
    if mode == "gather":
        return (
            [(lax.rem(me + s, n), None, me, always) for s in range(1, n)],
            [(lax.rem(me + n - s, n), lax.rem(me + n - s, n), always) for s in range(1, n)],
        )
    if mode == "sib":
        parity = lax.rem(sibling, 2)
        return (
            [(sibling, 2 * j + parity, j, always) for j in range(n // 2)],
            [(sibling, j, always) for j in range(n // 2)],
        )
    if mode == "same":
        sources = [lax.rem(me + n - 2 * s, n) for s in range(1, n // 2)]
        return (
            [(peer, peer // 2, me // 2, peer // 2 < me // 2) for peer in others],
            [(peer, peer // 2, peer // 2 > me // 2) for peer in sources],
        )
    sources = [lax.rem(sibling + 2 * s, n) for s in range(1, n // 2)]
    return (
        [(sibling, None, me, always)] + [(peer, None, me, peer // 2 > me // 2) for peer in others],
        [(sibling, sibling, always)] + [(peer, peer, peer // 2 < me // 2) for peer in sources],
    )


def when(condition, body):
    if condition is None:
        body()
    else:
        pl.when(condition)(body)


def exchange_kernel(items, *refs):
    count = len(items)
    x_refs, y_refs = refs[:count], refs[count : 2 * count]
    send_sem, recv_sem, local_sem = refs[2 * count : 2 * count + 3]
    stride = max(lax.axis_size(axis) for axis, _, _ in items)
    forward_base = count * stride

    def remote(i, axis, source, slot, target, send_slot, recv_slot):
        return pltpu.make_async_remote_copy(
            src_ref=source,
            dst_ref=y_refs[i].at[slot],
            send_sem=send_sem.at[send_slot],
            recv_sem=recv_sem.at[recv_slot],
            device_id=device_of(axis, target),
            device_id_type=MESH,
        )

    barrier = pltpu.get_barrier_semaphore()
    peers = barrier_peers(items)
    for axis, peer in peers:
        pl.semaphore_signal(barrier, inc=1, device_id=device_of(axis, peer), device_id_type=MESH)
    pl.semaphore_wait(barrier, len(peers))

    sends = []
    for i, (axis, mode, _) in enumerate(items):
        for peer, chunk, slot, condition in plan(axis, mode)[0]:
            source = x_refs[i] if chunk is None else x_refs[i].at[chunk]
            send_slot = i * stride + (chunk if mode == "sib" else peer)
            copy = remote(i, axis, source, slot, peer, send_slot, i * stride + slot)
            when(condition, copy.start)
            sends.append((copy, condition))
    locals_ = []
    for i, (axis, mode, _) in enumerate(items):
        me = lax.axis_index(axis)
        n = lax.axis_size(axis)
        if mode == "sib":
            continue
        if mode == "same":
            own = (x_refs[i].at[me // 2], y_refs[i].at[me // 2])
            for j in range(n // 2):
                def clear(j=j):
                    y_refs[i][j] = jnp.zeros(y_refs[i].shape[1:], y_refs[i].dtype)
                when(j < me // 2, clear)
        elif mode == "a2a":
            own = (x_refs[i].at[me], y_refs[i].at[me])
        else:
            own = (x_refs[i], y_refs[i].at[me])
            if mode == "pair":
                for block in range(n):
                    def clear(block=block):
                        y_refs[i][block] = jnp.zeros(y_refs[i].shape[1:], y_refs[i].dtype)
                    when(block // 2 > me // 2, clear)
        copy = pltpu.make_async_copy(own[0], own[1], local_sem.at[i])
        copy.start()
        locals_.append(copy)

    forwards = []
    for i, (axis, mode, _) in enumerate(items):
        if mode != "pair":
            continue
        me = lax.axis_index(axis)
        sibling, others = pair_peers(axis)
        for block in others:
            arrived = remote(i, axis, y_refs[i].at[block], block, block, i * stride + block, i * stride + block)
            copy = remote(
                i, axis, y_refs[i].at[block], block, sibling, forward_base + i * stride + block,
                i * stride + block,
            )

            def relay(arrived=arrived, copy=copy):
                arrived.wait_recv()
                copy.start()

            when(block // 2 < me // 2, relay)
            forwards.append((copy, block // 2 < me // 2))

    for i, (axis, mode, _) in enumerate(items):
        for peer, slot, condition in plan(axis, mode)[1]:
            incoming = remote(i, axis, y_refs[i].at[slot], slot, peer, i * stride + slot, i * stride + slot)
            when(condition, incoming.wait_recv)
    for copy, condition in sends + forwards:
        when(condition, copy.wait_send)
    for copy in locals_:
        copy.wait()


def exchange(arrays, items, collective_id):
    count = len(arrays)
    items = tuple(items)

    def out_shape(a, axis, mode):
        n = lax.axis_size(axis)
        if mode == "a2a":
            return a.shape
        if mode in ("sib", "same"):
            return (n // 2,) + a.shape[1:]
        return (n,) + a.shape

    out_shapes = [jax.ShapeDtypeStruct(out_shape(a, axis, mode), a.dtype) for a, (axis, mode, _) in zip(arrays, items)]
    moved = sum(math.prod(o.shape) * a.dtype.itemsize for a, o in zip(arrays, out_shapes))
    slots = count * max(lax.axis_size(axis) for axis, _, _ in items)
    space = [pl.BlockSpec(memory_space=pl.ANY if hbm else pltpu.VMEM) for _, _, hbm in items]
    return pl.pallas_call(
        functools.partial(exchange_kernel, items),
        out_shape=out_shapes,
        in_specs=space,
        out_specs=[pl.BlockSpec(memory_space=pltpu.VMEM)] * count,
        scratch_shapes=[
            pltpu.SemaphoreType.DMA((2 * slots,)),
            pltpu.SemaphoreType.DMA((slots,)),
            pltpu.SemaphoreType.DMA((count,)),
        ],
        compiler_params=pltpu.CompilerParams(
            collective_id=collective_id, has_side_effects=True, vmem_limit_bytes=48 * 1024 * 1024
        ),
        cost_estimate=pl.CostEstimate(flops=0, transcendentals=0, bytes_accessed=2 * moved),
    )(*arrays)


def head_mass_kernel(query_ref, latent_ref, sums_ref, start_ref, position_ref, out_ref):
    rows, width = out_ref.shape
    scores = lax.dot_general(
        query_ref[...], latent_ref[...], (((1,), (1,)), ((), ())), preferred_element_type=jnp.float32
    )
    mass = jnp.exp(scores * main_scale - sums_ref[...])
    mass = jnp.sum(mass.reshape(rows, mass.shape[0] // rows, width), axis=1)
    columns = pl.program_id(0) * width + lax.broadcasted_iota(jnp.int32, (rows, width), 1)
    seen = (columns >= start_ref[...]) & (columns <= position_ref[...])
    out_ref[...] = jnp.where(seen, mass, 0.0)


def head_mass(flat_query, latent_piece, flat_sums, window_start, positions):
    query_rows = window_start.shape[0]
    tokens, latent_width = latent_piece.shape
    width = math.gcd(tokens, 256)
    flat_rows = flat_query.shape[0]
    return pl.pallas_call(
        head_mass_kernel,
        out_shape=jax.ShapeDtypeStruct((query_rows, tokens), jnp.float32),
        grid=(tokens // width,),
        in_specs=[
            pl.BlockSpec((flat_rows, latent_width), lambda k: (0, 0)),
            pl.BlockSpec((width, latent_width), lambda k: (k, 0)),
            pl.BlockSpec((flat_rows, 1), lambda k: (0, 0)),
            pl.BlockSpec((query_rows, 1), lambda k: (0, 0)),
            pl.BlockSpec((query_rows, 1), lambda k: (0, 0)),
        ],
        out_specs=pl.BlockSpec((query_rows, width), lambda k: (0, k)),
        cost_estimate=pl.CostEstimate(
            flops=2 * flat_rows * tokens * latent_width,
            transcendentals=flat_rows * tokens,
            bytes_accessed=flat_query.size * 2 + latent_piece.size * 2 + query_rows * tokens * 4,
        ),
    )(flat_query, latent_piece, flat_sums, window_start[:, None], positions[:, None])


def on_device(main_query, latent, log_sums, window_start, index_query, index_key, index_weight):
    query_rows, head_count, latent_width = main_query.shape
    index_width = index_query.shape[2]
    part_heads = index_query.shape[1]
    groups = lax.axis_size("ha")
    blocks = lax.axis_size("pb")
    tokens = query_rows * blocks
    own_rows = query_rows // groups
    index_heads = part_heads * groups
    all_heads = head_count * groups
    block_first = lax.axis_index("pb") * query_rows

    latent_parts, key_parts, query_parts, sums_parts, index_parts, weight_parts = exchange(
        [
            latent,
            index_key,
            main_query.reshape(groups, own_rows * head_count, latent_width),
            log_sums.reshape(groups, 1, own_rows * head_count),
            index_query.reshape(groups, own_rows * part_heads, index_width),
            index_weight.reshape(groups, 1, own_rows * part_heads),
        ],
        [
            ("pb", "pair", False),
            ("pb", "pair", False),
            ("ha", "a2a", True),
            ("ha", "a2a", False),
            ("ha", "a2a", False),
            ("ha", "a2a", False),
        ],
        0,
    )
    latent_piece = latent_parts.reshape(tokens, latent_width)
    keys_all = key_parts.reshape(tokens, index_width)
    local_query = (
        query_parts.reshape(groups, own_rows, head_count, latent_width)
        .transpose(1, 0, 2, 3)
        .reshape(own_rows * all_heads, latent_width)
    )
    local_sums = (
        sums_parts.reshape(groups, own_rows, head_count).transpose(1, 0, 2).reshape(own_rows * all_heads, 1)
    )
    local_index = (
        index_parts.reshape(groups, own_rows, part_heads, index_width)
        .transpose(1, 0, 2, 3)
        .reshape(own_rows, index_heads, index_width)
    )
    local_weight = (
        weight_parts.reshape(groups, own_rows, part_heads).transpose(1, 0, 2).reshape(own_rows, index_heads)
    )
    row_first = block_first + lax.axis_index("ha") * own_rows
    own_positions = row_first + jnp.arange(own_rows, dtype=jnp.int32)
    own_start = lax.dynamic_slice_in_dim(window_start, lax.axis_index("ha") * own_rows, own_rows, 0)

    probs_all = head_mass(local_query, latent_piece, local_sums, own_start, own_positions)

    flat_index = local_index.reshape(own_rows * index_heads, index_width)
    active = jnp.einsum("rd,kd->rk", flat_index, keys_all, preferred_element_type=jnp.float32)
    active = active.reshape(own_rows, index_heads, tokens)
    relu_act = jnp.maximum(active, 0.0)
    logit_all = jnp.sum(local_weight[:, :, None] * relu_act, axis=1)

    visible_all = visible(own_start, own_positions, 0, tokens)
    target = probs_all / jnp.sum(probs_all, axis=1, keepdims=True)
    masked = jnp.where(visible_all, logit_all, very_low)
    row_top = jnp.max(masked, axis=1, keepdims=True)
    expo = jnp.where(visible_all, jnp.exp(masked - row_top), 0.0)
    logit_grad = jnp.where(visible_all, expo / jnp.sum(expo, axis=1, keepdims=True) - target, 0.0)

    weight_grad = jnp.sum(logit_grad[:, None, :] * relu_act, axis=2)
    coeffs = jnp.where(
        active > 0.0, logit_grad[:, None, :] * local_weight[:, :, None], 0.0
    ).astype(jnp.bfloat16)
    coeffs = coeffs.reshape(own_rows * index_heads, tokens)
    query_grad = jnp.dot(coeffs, keys_all, preferred_element_type=jnp.float32)
    key_grad = jnp.einsum("rk,rd->kd", coeffs, flat_index, preferred_element_type=jnp.float32)

    query_grad = query_grad.astype(jnp.bfloat16).reshape(own_rows, groups, part_heads, index_width)
    key_grad = key_grad.reshape(blocks, query_rows, index_width)
    sibling_part = exchange([key_grad], [("pb", "sib", False)], 1)[0]
    parity = lax.rem(lax.axis_index("pb"), 2)
    own_part = lax.dynamic_index_in_dim(
        key_grad.reshape(blocks // 2, 2, query_rows, index_width), parity, axis=1, keepdims=False
    )
    key_parts = exchange([own_part + sibling_part], [("pb", "same", False)], 4)[0]
    key_share = jnp.sum(key_parts, axis=0).reshape(groups, own_rows, index_width)
    key_rows, query_back, weight_back = exchange(
        [
            key_share,
            query_grad.transpose(1, 0, 2, 3).reshape(groups, own_rows * part_heads, index_width),
            weight_grad.reshape(own_rows, groups, part_heads)
            .transpose(1, 0, 2)
            .reshape(groups, 1, own_rows * part_heads),
        ],
        [("ha", "a2a", False), ("ha", "a2a", False), ("ha", "a2a", False)],
        2,
    )
    query_output = query_back.reshape(query_rows, part_heads, index_width)
    weight_output = weight_back.reshape(query_rows, part_heads)
    key_output = exchange([jnp.sum(key_rows, axis=0)], [("ha", "gather", False)], 3)[0]
    key_output = key_output.reshape(query_rows, index_width).astype(jnp.bfloat16)
    return (query_output, key_output, weight_output)


def solution(mesh):
    return jax.shard_map(
        on_device,
        mesh=mesh,
        in_specs=(
            P("pb", "ha", None),
            P("pb", None),
            P("pb", "ha"),
            P("pb"),
            P("pb", "ha", None),
            P("pb", None),
            P("pb", "ha"),
        ),
        out_specs=(P("pb", "ha", None), P("pb", None), P("pb", "ha")),
        check_vma=False,
    )
```

```python
import functools
import math

import jax
import jax.numpy as jnp
from jax import lax
from jax.experimental import pallas as pl
from jax.experimental.pallas import tpu as pltpu
from jax.sharding import PartitionSpec as P

main_scale = 192.0 ** (-0.5)
very_low = -1e30
MESH = pl.DeviceIdType.MESH
AXES = ("pb", "ha")


def visible(window_start, positions, first_row, width):
    columns = first_row + jnp.arange(width, dtype=jnp.int32)
    return (columns[None, :] >= window_start[:, None]) & (columns[None, :] <= positions[:, None])


def device_of(axis, peer):
    return tuple(peer if name == axis else lax.axis_index(name) for name in AXES)


def pair_peers(axis):
    n = lax.axis_size(axis)
    me = lax.axis_index(axis)
    sibling = me + 1 - 2 * lax.rem(me, 2)
    return sibling, [lax.rem(me + 2 * step, n) for step in range(1, n // 2)]


def barrier_peers(items):
    peers = []
    for axis in sorted({axis for axis, _, _ in items}):
        n = lax.axis_size(axis)
        me = lax.axis_index(axis)
        modes = {mode for item_axis, mode, _ in items if item_axis == axis}
        sibling, others = pair_peers(axis)
        if modes == {"sib"}:
            peers += [(axis, sibling)]
        elif modes == {"same"}:
            peers += [(axis, peer) for peer in others]
        elif modes == {"pair"}:
            peers += [(axis, sibling)] + [(axis, peer) for peer in others]
        else:
            peers += [(axis, lax.rem(me + step, n)) for step in range(1, n)]
    return peers


def plan(axis, mode):
    n = lax.axis_size(axis)
    me = lax.axis_index(axis)
    sibling, others = pair_peers(axis)
    always = None
    if mode == "a2a":
        return (
            [(lax.rem(me + s, n), lax.rem(me + s, n), me, always) for s in range(1, n)],
            [(lax.rem(me + n - s, n), lax.rem(me + n - s, n), always) for s in range(1, n)],
        )
    if mode == "gather":
        return (
            [(lax.rem(me + s, n), None, me, always) for s in range(1, n)],
            [(lax.rem(me + n - s, n), lax.rem(me + n - s, n), always) for s in range(1, n)],
        )
    if mode == "sib":
        parity = lax.rem(sibling, 2)
        return (
            [(sibling, 2 * j + parity, j, always) for j in range(n // 2)],
            [(sibling, j, always) for j in range(n // 2)],
        )
    if mode == "same":
        sources = [lax.rem(me + n - 2 * s, n) for s in range(1, n // 2)]
        return (
            [(peer, peer // 2, me // 2, peer // 2 < me // 2) for peer in others],
            [(peer, peer // 2, peer // 2 > me // 2) for peer in sources],
        )
    sources = [lax.rem(sibling + 2 * s, n) for s in range(1, n // 2)]
    return (
        [(sibling, None, me, always)] + [(peer, None, me, peer // 2 > me // 2) for peer in others],
        [(sibling, sibling, always)] + [(peer, peer, peer // 2 < me // 2) for peer in sources],
    )


def when(condition, body):
    if condition is None:
        body()
    else:
        pl.when(condition)(body)


def exchange_kernel(items, *refs):
    count = len(items)
    x_refs, y_refs = refs[:count], refs[count : 2 * count]
    send_sem, recv_sem, local_sem = refs[2 * count : 2 * count + 3]
    stride = max(lax.axis_size(axis) for axis, _, _ in items)
    forward_base = count * stride

    def remote(i, axis, source, slot, target, send_slot, recv_slot):
        return pltpu.make_async_remote_copy(
            src_ref=source,
            dst_ref=y_refs[i].at[slot],
            send_sem=send_sem.at[send_slot],
            recv_sem=recv_sem.at[recv_slot],
            device_id=device_of(axis, target),
            device_id_type=MESH,
        )

    barrier = pltpu.get_barrier_semaphore()
    peers = barrier_peers(items)
    for axis, peer in peers:
        pl.semaphore_signal(barrier, inc=1, device_id=device_of(axis, peer), device_id_type=MESH)
    pl.semaphore_wait(barrier, len(peers))

    sends = []
    order = sorted(range(count), key=lambda i: items[i][0] != "ha")
    for i in order:
        axis, mode, _ = items[i]
        for peer, chunk, slot, condition in plan(axis, mode)[0]:
            source = x_refs[i] if chunk is None else x_refs[i].at[chunk]
            send_slot = i * stride + (chunk if mode == "sib" else peer)
            copy = remote(i, axis, source, slot, peer, send_slot, i * stride + slot)
            when(condition, copy.start)
            sends.append((copy, condition))
    locals_ = []
    for i, (axis, mode, _) in enumerate(items):
        me = lax.axis_index(axis)
        n = lax.axis_size(axis)
        if mode == "sib":
            continue
        if mode == "same":
            own = (x_refs[i].at[me // 2], y_refs[i].at[me // 2])
            for j in range(n // 2):
                def clear(j=j):
                    y_refs[i][j] = jnp.zeros(y_refs[i].shape[1:], y_refs[i].dtype)
                when(j < me // 2, clear)
        elif mode == "a2a":
            own = (x_refs[i].at[me], y_refs[i].at[me])
        else:
            own = (x_refs[i], y_refs[i].at[me])
            if mode == "pair":
                for block in range(n):
                    def clear(block=block):
                        y_refs[i][block] = jnp.zeros(y_refs[i].shape[1:], y_refs[i].dtype)
                    when(block // 2 > me // 2, clear)
        copy = pltpu.make_async_copy(own[0], own[1], local_sem.at[i])
        copy.start()
        locals_.append(copy)

    forwards = []
    for i, (axis, mode, _) in enumerate(items):
        if mode != "pair":
            continue
        me = lax.axis_index(axis)
        sibling, others = pair_peers(axis)
        for block in others:
            arrived = remote(i, axis, y_refs[i].at[block], block, block, i * stride + block, i * stride + block)
            copy = remote(
                i, axis, y_refs[i].at[block], block, sibling, forward_base + i * stride + block,
                i * stride + block,
            )

            def relay(arrived=arrived, copy=copy):
                arrived.wait_recv()
                copy.start()

            when(block // 2 < me // 2, relay)
            forwards.append((copy, block // 2 < me // 2))

    for i, (axis, mode, _) in enumerate(items):
        for peer, slot, condition in plan(axis, mode)[1]:
            incoming = remote(i, axis, y_refs[i].at[slot], slot, peer, i * stride + slot, i * stride + slot)
            when(condition, incoming.wait_recv)
    for copy, condition in sends + forwards:
        when(condition, copy.wait_send)
    for copy in locals_:
        copy.wait()


def exchange(arrays, items, collective_id):
    count = len(arrays)
    items = tuple(items)

    def out_shape(a, axis, mode):
        n = lax.axis_size(axis)
        if mode == "a2a":
            return a.shape
        if mode in ("sib", "same"):
            return (n // 2,) + a.shape[1:]
        return (n,) + a.shape

    out_shapes = [jax.ShapeDtypeStruct(out_shape(a, axis, mode), a.dtype) for a, (axis, mode, _) in zip(arrays, items)]
    moved = sum(math.prod(o.shape) * a.dtype.itemsize for a, o in zip(arrays, out_shapes))
    slots = count * max(lax.axis_size(axis) for axis, _, _ in items)
    space = [pl.BlockSpec(memory_space=pl.ANY if hbm else pltpu.VMEM) for _, _, hbm in items]
    return pl.pallas_call(
        functools.partial(exchange_kernel, items),
        out_shape=out_shapes,
        in_specs=space,
        out_specs=[pl.BlockSpec(memory_space=pltpu.VMEM)] * count,
        scratch_shapes=[
            pltpu.SemaphoreType.DMA((2 * slots,)),
            pltpu.SemaphoreType.DMA((slots,)),
            pltpu.SemaphoreType.DMA((count,)),
        ],
        compiler_params=pltpu.CompilerParams(
            collective_id=collective_id, has_side_effects=True, vmem_limit_bytes=48 * 1024 * 1024
        ),
        cost_estimate=pl.CostEstimate(flops=0, transcendentals=0, bytes_accessed=2 * moved),
    )(*arrays)


def head_mass_kernel(query_ref, latent_ref, sums_ref, start_ref, position_ref, out_ref):
    rows, width = out_ref.shape
    scores = lax.dot_general(
        query_ref[...], latent_ref[...], (((1,), (1,)), ((), ())), preferred_element_type=jnp.float32
    )
    mass = jnp.exp(scores * main_scale - sums_ref[...])
    mass = jnp.sum(mass.reshape(rows, mass.shape[0] // rows, width), axis=1)
    columns = pl.program_id(0) * width + lax.broadcasted_iota(jnp.int32, (rows, width), 1)
    seen = (columns >= start_ref[...]) & (columns <= position_ref[...])
    out_ref[...] = jnp.where(seen, mass, 0.0)


def head_mass(flat_query, latent_piece, flat_sums, window_start, positions):
    query_rows = window_start.shape[0]
    tokens, latent_width = latent_piece.shape
    width = math.gcd(tokens, 512)
    flat_rows = flat_query.shape[0]
    return pl.pallas_call(
        head_mass_kernel,
        out_shape=jax.ShapeDtypeStruct((query_rows, tokens), jnp.float32),
        grid=(tokens // width,),
        in_specs=[
            pl.BlockSpec((flat_rows, latent_width), lambda k: (0, 0)),
            pl.BlockSpec((width, latent_width), lambda k: (k, 0)),
            pl.BlockSpec((flat_rows, 1), lambda k: (0, 0)),
            pl.BlockSpec((query_rows, 1), lambda k: (0, 0)),
            pl.BlockSpec((query_rows, 1), lambda k: (0, 0)),
        ],
        out_specs=pl.BlockSpec((query_rows, width), lambda k: (0, k)),
        cost_estimate=pl.CostEstimate(
            flops=2 * flat_rows * tokens * latent_width,
            transcendentals=flat_rows * tokens,
            bytes_accessed=flat_query.size * 2 + latent_piece.size * 2 + query_rows * tokens * 4,
        ),
    )(flat_query, latent_piece, flat_sums, window_start[:, None], positions[:, None])


def on_device(main_query, latent, log_sums, window_start, index_query, index_key, index_weight):
    query_rows, head_count, latent_width = main_query.shape
    index_width = index_query.shape[2]
    part_heads = index_query.shape[1]
    groups = lax.axis_size("ha")
    blocks = lax.axis_size("pb")
    tokens = query_rows * blocks
    own_rows = query_rows // groups
    index_heads = part_heads * groups
    all_heads = head_count * groups
    block_first = lax.axis_index("pb") * query_rows

    latent_parts, key_parts, query_parts, sums_parts, index_parts, weight_parts = exchange(
        [
            latent,
            index_key,
            main_query.reshape(groups, own_rows * head_count, latent_width),
            log_sums.reshape(groups, 1, own_rows * head_count),
            index_query.reshape(groups, own_rows * part_heads, index_width),
            index_weight.reshape(groups, 1, own_rows * part_heads),
        ],
        [
            ("pb", "pair", False),
            ("pb", "pair", False),
            ("ha", "a2a", True),
            ("ha", "a2a", False),
            ("ha", "a2a", False),
            ("ha", "a2a", False),
        ],
        0,
    )
    latent_piece = latent_parts.reshape(tokens, latent_width)
    keys_all = key_parts.reshape(tokens, index_width)
    local_query = (
        query_parts.reshape(groups, own_rows, head_count, latent_width)
        .transpose(1, 0, 2, 3)
        .reshape(own_rows * all_heads, latent_width)
    )
    local_sums = (
        sums_parts.reshape(groups, own_rows, head_count).transpose(1, 0, 2).reshape(own_rows * all_heads, 1)
    )
    local_index = (
        index_parts.reshape(groups, own_rows, part_heads, index_width)
        .transpose(1, 0, 2, 3)
        .reshape(own_rows, index_heads, index_width)
    )
    local_weight = (
        weight_parts.reshape(groups, own_rows, part_heads).transpose(1, 0, 2).reshape(own_rows, index_heads)
    )
    row_first = block_first + lax.axis_index("ha") * own_rows
    own_positions = row_first + jnp.arange(own_rows, dtype=jnp.int32)
    own_start = lax.dynamic_slice_in_dim(window_start, lax.axis_index("ha") * own_rows, own_rows, 0)

    probs_all = head_mass(local_query, latent_piece, local_sums, own_start, own_positions)

    flat_index = local_index.reshape(own_rows * index_heads, index_width)
    active = jnp.einsum("rd,kd->rk", flat_index, keys_all, preferred_element_type=jnp.float32)
    active = active.reshape(own_rows, index_heads, tokens)
    relu_act = jnp.maximum(active, 0.0)
    logit_all = jnp.sum(local_weight[:, :, None] * relu_act, axis=1)

    visible_all = visible(own_start, own_positions, 0, tokens)
    target = probs_all / jnp.sum(probs_all, axis=1, keepdims=True)
    masked = jnp.where(visible_all, logit_all, very_low)
    row_top = jnp.max(masked, axis=1, keepdims=True)
    expo = jnp.where(visible_all, jnp.exp(masked - row_top), 0.0)
    logit_grad = jnp.where(visible_all, expo / jnp.sum(expo, axis=1, keepdims=True) - target, 0.0)

    weight_grad = jnp.sum(logit_grad[:, None, :] * relu_act, axis=2)
    coeffs = jnp.where(
        active > 0.0, logit_grad[:, None, :] * local_weight[:, :, None], 0.0
    ).astype(jnp.bfloat16)
    coeffs = coeffs.reshape(own_rows * index_heads, tokens)
    query_grad = jnp.dot(coeffs, keys_all, preferred_element_type=jnp.float32)
    key_grad = jnp.einsum("rk,rd->kd", coeffs, flat_index, preferred_element_type=jnp.float32)

    query_grad = query_grad.astype(jnp.bfloat16).reshape(own_rows, groups, part_heads, index_width)
    key_grad = key_grad.reshape(blocks, query_rows, index_width)
    sibling_part = exchange([key_grad], [("pb", "sib", False)], 1)[0]
    parity = lax.rem(lax.axis_index("pb"), 2)
    own_part = lax.dynamic_index_in_dim(
        key_grad.reshape(blocks // 2, 2, query_rows, index_width), parity, axis=1, keepdims=False
    )
    key_parts = exchange([own_part + sibling_part], [("pb", "same", False)], 4)[0]
    key_share = jnp.sum(key_parts, axis=0).reshape(groups, own_rows, index_width)
    key_rows, query_back, weight_back = exchange(
        [
            key_share,
            query_grad.transpose(1, 0, 2, 3).reshape(groups, own_rows * part_heads, index_width),
            weight_grad.reshape(own_rows, groups, part_heads)
            .transpose(1, 0, 2)
            .reshape(groups, 1, own_rows * part_heads),
        ],
        [("ha", "a2a", False), ("ha", "a2a", False), ("ha", "a2a", False)],
        2,
    )
    query_output = query_back.reshape(query_rows, part_heads, index_width)
    weight_output = weight_back.reshape(query_rows, part_heads)
    key_output = exchange([jnp.sum(key_rows, axis=0)], [("ha", "gather", False)], 3)[0]
    key_output = key_output.reshape(query_rows, index_width).astype(jnp.bfloat16)
    return (query_output, key_output, weight_output)


def solution(mesh):
    return jax.shard_map(
        on_device,
        mesh=mesh,
        in_specs=(
            P("pb", "ha", None),
            P("pb", None),
            P("pb", "ha"),
            P("pb"),
            P("pb", "ha", None),
            P("pb", None),
            P("pb", "ha"),
        ),
        out_specs=(P("pb", "ha", None), P("pb", None), P("pb", "ha")),
        check_vma=False,
    )
```

```python
import functools
import math

import jax
import jax.numpy as jnp
from jax import lax
from jax.experimental import pallas as pl
from jax.experimental.pallas import tpu as pltpu
from jax.sharding import PartitionSpec as P

main_scale = 192.0 ** (-0.5)
very_low = -1e30
MESH = pl.DeviceIdType.MESH
AXES = ("pb", "ha")


def visible(window_start, positions, first_row, width):
    columns = first_row + jnp.arange(width, dtype=jnp.int32)
    return (columns[None, :] >= window_start[:, None]) & (columns[None, :] <= positions[:, None])


def device_of(axis, peer):
    return tuple(peer if name == axis else lax.axis_index(name) for name in AXES)


def pair_peers(axis):
    n = lax.axis_size(axis)
    me = lax.axis_index(axis)
    sibling = me + 1 - 2 * lax.rem(me, 2)
    return sibling, [lax.rem(me + 2 * step, n) for step in range(1, n // 2)]


def barrier_peers(items):
    peers = []
    for axis in sorted({axis for axis, _, _ in items}):
        n = lax.axis_size(axis)
        me = lax.axis_index(axis)
        modes = {mode for item_axis, mode, _ in items if item_axis == axis}
        sibling, others = pair_peers(axis)
        if modes == {"sib"}:
            peers += [(axis, sibling)]
        elif modes == {"same"}:
            peers += [(axis, peer) for peer in others]
        elif modes == {"pair"}:
            peers += [(axis, sibling)] + [(axis, peer) for peer in others]
        else:
            peers += [(axis, lax.rem(me + step, n)) for step in range(1, n)]
    return peers


def plan(axis, mode):
    n = lax.axis_size(axis)
    me = lax.axis_index(axis)
    sibling, others = pair_peers(axis)
    always = None
    if mode == "a2a":
        return (
            [(lax.rem(me + s, n), lax.rem(me + s, n), me, always) for s in range(1, n)],
            [(lax.rem(me + n - s, n), lax.rem(me + n - s, n), always) for s in range(1, n)],
        )
    if mode == "gather":
        return (
            [(lax.rem(me + s, n), None, me, always) for s in range(1, n)],
            [(lax.rem(me + n - s, n), lax.rem(me + n - s, n), always) for s in range(1, n)],
        )
    if mode == "sib":
        parity = lax.rem(sibling, 2)
        return (
            [(sibling, 2 * j + parity, j, always) for j in range(n // 2)],
            [(sibling, j, always) for j in range(n // 2)],
        )
    if mode == "same":
        sources = [lax.rem(me + n - 2 * s, n) for s in range(1, n // 2)]
        return (
            [(peer, peer // 2, me // 2, peer // 2 < me // 2) for peer in others],
            [(peer, peer // 2, peer // 2 > me // 2) for peer in sources],
        )
    sources = [lax.rem(sibling + 2 * s, n) for s in range(1, n // 2)]
    return (
        [(sibling, None, me, always)] + [(peer, None, me, peer // 2 > me // 2) for peer in others],
        [(sibling, sibling, always)] + [(peer, peer, peer // 2 < me // 2) for peer in sources],
    )


def when(condition, body):
    if condition is None:
        body()
    else:
        pl.when(condition)(body)


def exchange_kernel(items, *refs):
    count = len(items)
    x_refs, y_refs = refs[:count], refs[count : 2 * count]
    send_sem, recv_sem, local_sem = refs[2 * count : 2 * count + 3]
    stride = max(lax.axis_size(axis) for axis, _, _ in items)
    forward_base = count * stride

    def remote(i, axis, source, slot, target, send_slot, recv_slot):
        return pltpu.make_async_remote_copy(
            src_ref=source,
            dst_ref=y_refs[i].at[slot],
            send_sem=send_sem.at[send_slot],
            recv_sem=recv_sem.at[recv_slot],
            device_id=device_of(axis, target),
            device_id_type=MESH,
        )

    barrier = pltpu.get_barrier_semaphore()
    peers = barrier_peers(items)
    for axis, peer in peers:
        pl.semaphore_signal(barrier, inc=1, device_id=device_of(axis, peer), device_id_type=MESH)
    if peers:
        pl.semaphore_wait(barrier, len(peers))

    sends = []
    order = sorted(range(count), key=lambda i: items[i][0] != "ha")
    for i in order:
        axis, mode, _ = items[i]
        for peer, chunk, slot, condition in plan(axis, mode)[0]:
            source = x_refs[i] if chunk is None else x_refs[i].at[chunk]
            send_slot = i * stride + (chunk if mode == "sib" else peer)
            copy = remote(i, axis, source, slot, peer, send_slot, i * stride + slot)
            when(condition, copy.start)
            sends.append((copy, condition))
    locals_ = []
    for i, (axis, mode, _) in enumerate(items):
        me = lax.axis_index(axis)
        n = lax.axis_size(axis)
        if mode == "sib":
            continue
        if mode == "same":
            own = (x_refs[i].at[me // 2], y_refs[i].at[me // 2])
            for j in range(n // 2):
                def clear(j=j):
                    y_refs[i][j] = jnp.zeros(y_refs[i].shape[1:], y_refs[i].dtype)
                when(j < me // 2, clear)
        elif mode == "a2a":
            own = (x_refs[i].at[me], y_refs[i].at[me])
        else:
            own = (x_refs[i], y_refs[i].at[me])
            if mode == "pair":
                for block in range(n):
                    def clear(block=block):
                        y_refs[i][block] = jnp.zeros(y_refs[i].shape[1:], y_refs[i].dtype)
                    when(block // 2 > me // 2, clear)
        copy = pltpu.make_async_copy(own[0], own[1], local_sem.at[i])
        copy.start()
        locals_.append(copy)

    forwards = []
    for i, (axis, mode, _) in enumerate(items):
        if mode != "pair":
            continue
        me = lax.axis_index(axis)
        sibling, others = pair_peers(axis)
        for block in others:
            arrived = remote(i, axis, y_refs[i].at[block], block, block, i * stride + block, i * stride + block)
            copy = remote(
                i, axis, y_refs[i].at[block], block, sibling, forward_base + i * stride + block,
                i * stride + block,
            )

            def relay(arrived=arrived, copy=copy):
                arrived.wait_recv()
                copy.start()

            when(block // 2 < me // 2, relay)
            forwards.append((copy, block // 2 < me // 2))

    for i, (axis, mode, _) in enumerate(items):
        for peer, slot, condition in plan(axis, mode)[1]:
            incoming = remote(i, axis, y_refs[i].at[slot], slot, peer, i * stride + slot, i * stride + slot)
            when(condition, incoming.wait_recv)
    for copy, condition in sends + forwards:
        when(condition, copy.wait_send)
    for copy in locals_:
        copy.wait()


def exchange(arrays, items, collective_id):
    count = len(arrays)
    items = tuple(items)

    def out_shape(a, axis, mode):
        n = lax.axis_size(axis)
        if mode == "a2a":
            return a.shape
        if mode in ("sib", "same"):
            return (n // 2,) + a.shape[1:]
        return (n,) + a.shape

    out_shapes = [jax.ShapeDtypeStruct(out_shape(a, axis, mode), a.dtype) for a, (axis, mode, _) in zip(arrays, items)]
    moved = sum(math.prod(o.shape) * a.dtype.itemsize for a, o in zip(arrays, out_shapes))
    slots = count * max(lax.axis_size(axis) for axis, _, _ in items)
    space = [pl.BlockSpec(memory_space=pl.ANY if hbm else pltpu.VMEM) for _, _, hbm in items]
    return pl.pallas_call(
        functools.partial(exchange_kernel, items),
        out_shape=out_shapes,
        in_specs=space,
        out_specs=[pl.BlockSpec(memory_space=pltpu.VMEM)] * count,
        scratch_shapes=[
            pltpu.SemaphoreType.DMA((2 * slots,)),
            pltpu.SemaphoreType.DMA((slots,)),
            pltpu.SemaphoreType.DMA((count,)),
        ],
        compiler_params=pltpu.CompilerParams(
            collective_id=collective_id, has_side_effects=True, vmem_limit_bytes=48 * 1024 * 1024
        ),
        cost_estimate=pl.CostEstimate(flops=0, transcendentals=0, bytes_accessed=2 * moved),
    )(*arrays)


def head_mass_kernel(query_rows, starts_ref, query_ref, latent_ref, sums_ref, out_ref):
    rows, width = out_ref.shape
    scores = lax.dot_general(
        query_ref[...], latent_ref[...], (((1,), (1,)), ((), ())), preferred_element_type=jnp.float32
    )
    mass = jnp.exp(scores * main_scale - sums_ref[...])
    mass = jnp.sum(mass.reshape(rows, mass.shape[0] // rows, width), axis=1)
    own_first = lax.axis_index("ha") * rows
    row_ids = lax.broadcasted_iota(jnp.int32, (rows, width), 0)
    starts = jnp.zeros((rows, width), jnp.int32)
    for row in range(rows):
        starts = jnp.where(row_ids == row, starts_ref[own_first + row], starts)
    positions = lax.axis_index("pb") * query_rows + own_first + row_ids
    columns = pl.program_id(0) * width + lax.broadcasted_iota(jnp.int32, (rows, width), 1)
    seen = (columns >= starts) & (columns <= positions)
    out_ref[...] = jnp.where(seen, mass, 0.0)


def head_mass(flat_query, latent_piece, flat_sums, window_start, rows):
    query_rows = window_start.shape[0]
    tokens, latent_width = latent_piece.shape
    width = math.gcd(tokens, 512)
    flat_rows = flat_query.shape[0]
    return pl.pallas_call(
        functools.partial(head_mass_kernel, query_rows),
        out_shape=jax.ShapeDtypeStruct((rows, tokens), jnp.float32),
        grid_spec=pltpu.PrefetchScalarGridSpec(
            num_scalar_prefetch=1,
            grid=(tokens // width,),
            in_specs=[
                pl.BlockSpec((flat_rows, latent_width), lambda k, starts: (0, 0)),
                pl.BlockSpec((width, latent_width), lambda k, starts: (k, 0)),
                pl.BlockSpec((flat_rows, 1), lambda k, starts: (0, 0)),
            ],
            out_specs=pl.BlockSpec((rows, width), lambda k, starts: (0, k)),
        ),
        cost_estimate=pl.CostEstimate(
            flops=2 * flat_rows * tokens * latent_width,
            transcendentals=flat_rows * tokens,
            bytes_accessed=flat_query.size * 2 + latent_piece.size * 2 + rows * tokens * 4,
        ),
    )(window_start, flat_query, latent_piece, flat_sums)


def on_device(main_query, latent, log_sums, window_start, index_query, index_key, index_weight):
    query_rows, head_count, latent_width = main_query.shape
    index_width = index_query.shape[2]
    part_heads = index_query.shape[1]
    groups = lax.axis_size("ha")
    blocks = lax.axis_size("pb")
    tokens = query_rows * blocks
    own_rows = query_rows // groups
    index_heads = part_heads * groups
    all_heads = head_count * groups
    block_first = lax.axis_index("pb") * query_rows

    latent_parts, key_parts, query_parts, sums_parts, index_parts, weight_parts = exchange(
        [
            latent,
            index_key,
            main_query.reshape(groups, own_rows * head_count, latent_width),
            log_sums.reshape(groups, 1, own_rows * head_count),
            index_query.reshape(groups, own_rows * part_heads, index_width),
            index_weight.reshape(groups, 1, own_rows * part_heads),
        ],
        [
            ("pb", "pair", False),
            ("pb", "pair", False),
            ("ha", "a2a", True),
            ("ha", "a2a", False),
            ("ha", "a2a", False),
            ("ha", "a2a", False),
        ],
        0,
    )
    latent_piece = latent_parts.reshape(tokens, latent_width)
    keys_all = key_parts.reshape(tokens, index_width)
    local_query = (
        query_parts.reshape(groups, own_rows, head_count, latent_width)
        .transpose(1, 0, 2, 3)
        .reshape(own_rows * all_heads, latent_width)
    )
    local_sums = (
        sums_parts.reshape(groups, own_rows, head_count).transpose(1, 0, 2).reshape(own_rows * all_heads, 1)
    )
    local_index = (
        index_parts.reshape(groups, own_rows, part_heads, index_width)
        .transpose(1, 0, 2, 3)
        .reshape(own_rows, index_heads, index_width)
    )
    local_weight = (
        weight_parts.reshape(groups, own_rows, part_heads).transpose(1, 0, 2).reshape(own_rows, index_heads)
    )
    row_first = block_first + lax.axis_index("ha") * own_rows
    own_positions = row_first + jnp.arange(own_rows, dtype=jnp.int32)
    own_start = lax.dynamic_slice_in_dim(window_start, lax.axis_index("ha") * own_rows, own_rows, 0)

    probs_all = head_mass(local_query, latent_piece, local_sums, window_start, own_rows)

    flat_index = local_index.reshape(own_rows * index_heads, index_width)
    active = jnp.einsum("rd,kd->rk", flat_index, keys_all, preferred_element_type=jnp.float32)
    active = active.reshape(own_rows, index_heads, tokens)
    relu_act = jnp.maximum(active, 0.0)
    logit_all = jnp.sum(local_weight[:, :, None] * relu_act, axis=1)

    visible_all = visible(own_start, own_positions, 0, tokens)
    target = probs_all / jnp.sum(probs_all, axis=1, keepdims=True)
    masked = jnp.where(visible_all, logit_all, very_low)
    row_top = jnp.max(masked, axis=1, keepdims=True)
    expo = jnp.where(visible_all, jnp.exp(masked - row_top), 0.0)
    logit_grad = jnp.where(visible_all, expo / jnp.sum(expo, axis=1, keepdims=True) - target, 0.0)

    weight_grad = jnp.sum(logit_grad[:, None, :] * relu_act, axis=2)
    coeffs = jnp.where(
        active > 0.0, logit_grad[:, None, :] * local_weight[:, :, None], 0.0
    ).astype(jnp.bfloat16)
    coeffs = coeffs.reshape(own_rows * index_heads, tokens)
    query_grad = jnp.dot(coeffs, keys_all, preferred_element_type=jnp.float32)
    key_grad = jnp.einsum("rk,rd->kd", coeffs, flat_index, preferred_element_type=jnp.float32)

    query_grad = query_grad.astype(jnp.bfloat16).reshape(own_rows, groups, part_heads, index_width)
    key_grad = key_grad.reshape(blocks, query_rows, index_width)
    sibling_part = exchange([key_grad], [("pb", "sib", False)], 1)[0]
    parity = lax.rem(lax.axis_index("pb"), 2)
    own_part = lax.dynamic_index_in_dim(
        key_grad.reshape(blocks // 2, 2, query_rows, index_width), parity, axis=1, keepdims=False
    )
    key_parts = exchange([own_part + sibling_part], [("pb", "same", False)], 4)[0]
    key_share = jnp.sum(key_parts, axis=0).reshape(groups, own_rows, index_width)
    key_rows, query_back, weight_back = exchange(
        [
            key_share,
            query_grad.transpose(1, 0, 2, 3).reshape(groups, own_rows * part_heads, index_width),
            weight_grad.reshape(own_rows, groups, part_heads)
            .transpose(1, 0, 2)
            .reshape(groups, 1, own_rows * part_heads),
        ],
        [("ha", "a2a", False), ("ha", "a2a", False), ("ha", "a2a", False)],
        2,
    )
    query_output = query_back.reshape(query_rows, part_heads, index_width)
    weight_output = weight_back.reshape(query_rows, part_heads)
    key_output = exchange([jnp.sum(key_rows, axis=0)], [("ha", "gather", False)], 3)[0]
    key_output = key_output.reshape(query_rows, index_width).astype(jnp.bfloat16)
    return (query_output, key_output, weight_output)


def solution(mesh):
    return jax.shard_map(
        on_device,
        mesh=mesh,
        in_specs=(
            P("pb", "ha", None),
            P("pb", None),
            P("pb", "ha"),
            P("pb"),
            P("pb", "ha", None),
            P("pb", None),
            P("pb", "ha"),
        ),
        out_specs=(P("pb", "ha", None), P("pb", None), P("pb", "ha")),
        check_vma=False,
    )
```

```python
import functools
import math

import jax
import jax.numpy as jnp
from jax import lax
from jax.experimental import pallas as pl
from jax.experimental.pallas import tpu as pltpu
from jax.sharding import PartitionSpec as P

main_scale = 192.0 ** (-0.5)
very_low = -1e30
MESH = pl.DeviceIdType.MESH
AXES = ("pb", "ha")


def visible(window_start, positions, first_row, width):
    columns = first_row + jnp.arange(width, dtype=jnp.int32)
    return (columns[None, :] >= window_start[:, None]) & (columns[None, :] <= positions[:, None])


def device_of(axis, peer):
    return tuple(peer if name == axis else lax.axis_index(name) for name in AXES)


def pair_peers(axis):
    n = lax.axis_size(axis)
    me = lax.axis_index(axis)
    sibling = me + 1 - 2 * lax.rem(me, 2)
    return sibling, [lax.rem(me + 2 * step, n) for step in range(1, n // 2)]


def barrier_peers(items):
    peers = []
    for axis in sorted({axis for axis, _, _ in items}):
        n = lax.axis_size(axis)
        me = lax.axis_index(axis)
        modes = {mode for item_axis, mode, _ in items if item_axis == axis}
        sibling, others = pair_peers(axis)
        if modes == {"sib"}:
            peers += [(axis, sibling)]
        elif modes == {"same"}:
            peers += [(axis, peer) for peer in others]
        elif modes == {"pair"}:
            peers += [(axis, sibling)] + [(axis, peer) for peer in others]
        else:
            peers += [(axis, lax.rem(me + step, n)) for step in range(1, n)]
    return peers


def plan(axis, mode):
    n = lax.axis_size(axis)
    me = lax.axis_index(axis)
    sibling, others = pair_peers(axis)
    always = None
    if mode == "a2a":
        return (
            [(lax.rem(me + s, n), lax.rem(me + s, n), me, always) for s in range(1, n)],
            [(lax.rem(me + n - s, n), lax.rem(me + n - s, n), always) for s in range(1, n)],
        )
    if mode == "gather":
        return (
            [(lax.rem(me + s, n), None, me, always) for s in range(1, n)],
            [(lax.rem(me + n - s, n), lax.rem(me + n - s, n), always) for s in range(1, n)],
        )
    if mode == "sib":
        parity = lax.rem(sibling, 2)
        return (
            [(sibling, 2 * j + parity, j, always) for j in range(n // 2)],
            [(sibling, j, always) for j in range(n // 2)],
        )
    if mode == "same":
        sources = [lax.rem(me + n - 2 * s, n) for s in range(1, n // 2)]
        return (
            [(peer, peer // 2, me // 2, peer // 2 < me // 2) for peer in others],
            [(peer, peer // 2, peer // 2 > me // 2) for peer in sources],
        )
    sources = [lax.rem(sibling + 2 * s, n) for s in range(1, n // 2)]
    return (
        [(sibling, None, me, always)] + [(peer, None, me, peer // 2 > me // 2) for peer in others],
        [(sibling, sibling, always)] + [(peer, peer, peer // 2 < me // 2) for peer in sources],
    )


def when(condition, body):
    if condition is None:
        body()
    else:
        pl.when(condition)(body)


def exchange_kernel(items, *refs):
    count = len(items)
    x_refs, y_refs = refs[:count], refs[count : 2 * count]
    send_sem, recv_sem, local_sem = refs[2 * count : 2 * count + 3]
    stride = max(lax.axis_size(axis) for axis, _, _ in items)
    forward_base = count * stride

    def remote(i, axis, source, slot, target, send_slot, recv_slot):
        return pltpu.make_async_remote_copy(
            src_ref=source,
            dst_ref=y_refs[i].at[slot],
            send_sem=send_sem.at[send_slot],
            recv_sem=recv_sem.at[recv_slot],
            device_id=device_of(axis, target),
            device_id_type=MESH,
        )

    barrier = pltpu.get_barrier_semaphore()
    peers = barrier_peers(items)
    for axis, peer in peers:
        pl.semaphore_signal(barrier, inc=1, device_id=device_of(axis, peer), device_id_type=MESH)
    if peers:
        pl.semaphore_wait(barrier, len(peers))

    sends = []
    order = sorted(range(count), key=lambda i: items[i][0] != "ha")
    for i in order:
        axis, mode, _ = items[i]
        for peer, chunk, slot, condition in plan(axis, mode)[0]:
            source = x_refs[i] if chunk is None else x_refs[i].at[chunk]
            send_slot = i * stride + (chunk if mode == "sib" else peer)
            copy = remote(i, axis, source, slot, peer, send_slot, i * stride + slot)
            when(condition, copy.start)
            sends.append((copy, condition))
    locals_ = []
    for i, (axis, mode, _) in enumerate(items):
        me = lax.axis_index(axis)
        n = lax.axis_size(axis)
        if mode == "sib":
            continue
        if mode == "same":
            own = (x_refs[i].at[me // 2], y_refs[i].at[me // 2])
            for j in range(n // 2):
                def clear(j=j):
                    y_refs[i][j] = jnp.zeros(y_refs[i].shape[1:], y_refs[i].dtype)
                when(j < me // 2, clear)
        elif mode == "a2a":
            own = (x_refs[i].at[me], y_refs[i].at[me])
        else:
            own = (x_refs[i], y_refs[i].at[me])
            if mode == "pair":
                for block in range(n):
                    def clear(block=block):
                        y_refs[i][block] = jnp.zeros(y_refs[i].shape[1:], y_refs[i].dtype)
                    when(block // 2 > me // 2, clear)
        copy = pltpu.make_async_copy(own[0], own[1], local_sem.at[i])
        copy.start()
        locals_.append(copy)

    forwards = []
    for i, (axis, mode, _) in enumerate(items):
        if mode != "pair":
            continue
        me = lax.axis_index(axis)
        sibling, others = pair_peers(axis)
        for block in others:
            arrived = remote(i, axis, y_refs[i].at[block], block, block, i * stride + block, i * stride + block)
            copy = remote(
                i, axis, y_refs[i].at[block], block, sibling, forward_base + i * stride + block,
                i * stride + block,
            )

            def relay(arrived=arrived, copy=copy):
                arrived.wait_recv()
                copy.start()

            when(block // 2 < me // 2, relay)
            forwards.append((copy, block // 2 < me // 2))

    for i, (axis, mode, _) in enumerate(items):
        for peer, slot, condition in plan(axis, mode)[1]:
            incoming = remote(i, axis, y_refs[i].at[slot], slot, peer, i * stride + slot, i * stride + slot)
            when(condition, incoming.wait_recv)
    for copy, condition in sends + forwards:
        when(condition, copy.wait_send)
    for copy in locals_:
        copy.wait()


def exchange(arrays, items, collective_id):
    count = len(arrays)
    items = tuple(items)

    def out_shape(a, axis, mode):
        n = lax.axis_size(axis)
        if mode == "a2a":
            return a.shape
        if mode in ("sib", "same"):
            return (n // 2,) + a.shape[1:]
        return (n,) + a.shape

    out_shapes = [jax.ShapeDtypeStruct(out_shape(a, axis, mode), a.dtype) for a, (axis, mode, _) in zip(arrays, items)]
    moved = sum(math.prod(o.shape) * a.dtype.itemsize for a, o in zip(arrays, out_shapes))
    slots = count * max(lax.axis_size(axis) for axis, _, _ in items)
    space = [pl.BlockSpec(memory_space=pl.ANY if hbm else pltpu.VMEM) for _, _, hbm in items]
    return pl.pallas_call(
        functools.partial(exchange_kernel, items),
        out_shape=out_shapes,
        in_specs=space,
        out_specs=[pl.BlockSpec(memory_space=pltpu.VMEM)] * count,
        scratch_shapes=[
            pltpu.SemaphoreType.DMA((2 * slots,)),
            pltpu.SemaphoreType.DMA((slots,)),
            pltpu.SemaphoreType.DMA((count,)),
        ],
        compiler_params=pltpu.CompilerParams(
            collective_id=collective_id, has_side_effects=True, vmem_limit_bytes=48 * 1024 * 1024
        ),
        cost_estimate=pl.CostEstimate(flops=0, transcendentals=0, bytes_accessed=2 * moved),
    )(*arrays)


def head_mass_kernel(query_rows, sources, starts_ref, query_ref, latent_ref, sums_ref, out_ref):
    rows, width = out_ref.shape
    scores = lax.dot_general(
        query_ref[...], latent_ref[...], (((1,), (1,)), ((), ())), preferred_element_type=jnp.float32
    )
    mass = jnp.exp(scores * main_scale - sums_ref[...])
    heads = mass.shape[0] // (rows * sources)
    mass = jnp.sum(mass.reshape(sources, rows, heads, width), axis=(0, 2))
    own_first = lax.axis_index("ha") * rows
    row_ids = lax.broadcasted_iota(jnp.int32, (rows, width), 0)
    starts = jnp.zeros((rows, width), jnp.int32)
    for row in range(rows):
        starts = jnp.where(row_ids == row, starts_ref[own_first + row], starts)
    positions = lax.axis_index("pb") * query_rows + own_first + row_ids
    columns = pl.program_id(0) * width + lax.broadcasted_iota(jnp.int32, (rows, width), 1)
    seen = (columns >= starts) & (columns <= positions)
    out_ref[...] = jnp.where(seen, mass, 0.0)


def head_mass(flat_query, latent_piece, flat_sums, window_start, rows, sources):
    query_rows = window_start.shape[0]
    tokens, latent_width = latent_piece.shape
    width = math.gcd(tokens, 512)
    flat_rows = flat_query.shape[0]
    return pl.pallas_call(
        functools.partial(head_mass_kernel, query_rows, sources),
        out_shape=jax.ShapeDtypeStruct((rows, tokens), jnp.float32),
        grid_spec=pltpu.PrefetchScalarGridSpec(
            num_scalar_prefetch=1,
            grid=(tokens // width,),
            in_specs=[
                pl.BlockSpec((flat_rows, latent_width), lambda k, starts: (0, 0)),
                pl.BlockSpec((width, latent_width), lambda k, starts: (k, 0)),
                pl.BlockSpec((flat_rows, 1), lambda k, starts: (0, 0)),
            ],
            out_specs=pl.BlockSpec((rows, width), lambda k, starts: (0, k)),
        ),
        cost_estimate=pl.CostEstimate(
            flops=2 * flat_rows * tokens * latent_width,
            transcendentals=flat_rows * tokens,
            bytes_accessed=flat_query.size * 2 + latent_piece.size * 2 + rows * tokens * 4,
        ),
    )(window_start, flat_query, latent_piece, flat_sums)


def on_device(main_query, latent, log_sums, window_start, index_query, index_key, index_weight):
    query_rows, head_count, latent_width = main_query.shape
    index_width = index_query.shape[2]
    part_heads = index_query.shape[1]
    groups = lax.axis_size("ha")
    blocks = lax.axis_size("pb")
    tokens = query_rows * blocks
    own_rows = query_rows // groups
    index_heads = part_heads * groups
    all_heads = head_count * groups
    block_first = lax.axis_index("pb") * query_rows

    latent_parts, key_parts, query_parts, sums_parts, index_parts, weight_parts = exchange(
        [
            latent,
            index_key,
            main_query.reshape(groups, own_rows * head_count, latent_width),
            log_sums.reshape(groups, 1, own_rows * head_count),
            index_query.reshape(groups, own_rows * part_heads, index_width),
            index_weight.reshape(groups, 1, own_rows * part_heads),
        ],
        [
            ("pb", "pair", False),
            ("pb", "pair", False),
            ("ha", "a2a", True),
            ("ha", "a2a", False),
            ("ha", "a2a", False),
            ("ha", "a2a", False),
        ],
        0,
    )
    latent_piece = latent_parts.reshape(tokens, latent_width)
    keys_all = key_parts.reshape(tokens, index_width)
    local_query = query_parts.reshape(own_rows * all_heads, latent_width)
    local_sums = sums_parts.reshape(own_rows * all_heads, 1)
    local_index = (
        index_parts.reshape(groups, own_rows, part_heads, index_width)
        .transpose(1, 0, 2, 3)
        .reshape(own_rows, index_heads, index_width)
    )
    local_weight = (
        weight_parts.reshape(groups, own_rows, part_heads).transpose(1, 0, 2).reshape(own_rows, index_heads)
    )
    row_first = block_first + lax.axis_index("ha") * own_rows
    own_positions = row_first + jnp.arange(own_rows, dtype=jnp.int32)
    own_start = lax.dynamic_slice_in_dim(window_start, lax.axis_index("ha") * own_rows, own_rows, 0)

    probs_all = head_mass(local_query, latent_piece, local_sums, window_start, own_rows, groups)

    flat_index = local_index.reshape(own_rows * index_heads, index_width)
    active = jnp.einsum("rd,kd->rk", flat_index, keys_all, preferred_element_type=jnp.float32)
    active = active.reshape(own_rows, index_heads, tokens)
    relu_act = jnp.maximum(active, 0.0)
    logit_all = jnp.sum(local_weight[:, :, None] * relu_act, axis=1)

    visible_all = visible(own_start, own_positions, 0, tokens)
    target = probs_all / jnp.sum(probs_all, axis=1, keepdims=True)
    masked = jnp.where(visible_all, logit_all, very_low)
    row_top = jnp.max(masked, axis=1, keepdims=True)
    expo = jnp.where(visible_all, jnp.exp(masked - row_top), 0.0)
    logit_grad = jnp.where(visible_all, expo / jnp.sum(expo, axis=1, keepdims=True) - target, 0.0)

    weight_grad = jnp.sum(logit_grad[:, None, :] * relu_act, axis=2)
    coeffs = jnp.where(
        active > 0.0, logit_grad[:, None, :] * local_weight[:, :, None], 0.0
    ).astype(jnp.bfloat16)
    coeffs = coeffs.reshape(own_rows * index_heads, tokens)
    query_grad = jnp.dot(coeffs, keys_all, preferred_element_type=jnp.float32)
    key_grad = jnp.einsum("rk,rd->kd", coeffs, flat_index, preferred_element_type=jnp.float32)

    query_grad = query_grad.astype(jnp.bfloat16).reshape(own_rows, groups, part_heads, index_width)
    key_grad = key_grad.reshape(blocks, query_rows, index_width)
    sibling_part = exchange([key_grad], [("pb", "sib", False)], 1)[0]
    parity = lax.rem(lax.axis_index("pb"), 2)
    own_part = lax.dynamic_index_in_dim(
        key_grad.reshape(blocks // 2, 2, query_rows, index_width), parity, axis=1, keepdims=False
    )
    key_parts = exchange([own_part + sibling_part], [("pb", "same", False)], 4)[0]
    key_share = jnp.sum(key_parts, axis=0).reshape(groups, own_rows, index_width)
    key_rows, query_back, weight_back = exchange(
        [
            key_share,
            query_grad.transpose(1, 0, 2, 3).reshape(groups, own_rows * part_heads, index_width),
            weight_grad.reshape(own_rows, groups, part_heads)
            .transpose(1, 0, 2)
            .reshape(groups, 1, own_rows * part_heads),
        ],
        [("ha", "a2a", False), ("ha", "a2a", False), ("ha", "a2a", False)],
        2,
    )
    query_output = query_back.reshape(query_rows, part_heads, index_width)
    weight_output = weight_back.reshape(query_rows, part_heads)
    key_output = exchange([jnp.sum(key_rows, axis=0)], [("ha", "gather", False)], 3)[0]
    key_output = key_output.reshape(query_rows, index_width).astype(jnp.bfloat16)
    return (query_output, key_output, weight_output)


def solution(mesh):
    return jax.shard_map(
        on_device,
        mesh=mesh,
        in_specs=(
            P("pb", "ha", None),
            P("pb", None),
            P("pb", "ha"),
            P("pb"),
            P("pb", "ha", None),
            P("pb", None),
            P("pb", "ha"),
        ),
        out_specs=(P("pb", "ha", None), P("pb", None), P("pb", "ha")),
        check_vma=False,
    )
```

```python
import functools
import math

import jax
import jax.numpy as jnp
from jax import lax
from jax.experimental import pallas as pl
from jax.experimental.pallas import tpu as pltpu
from jax.sharding import PartitionSpec as P

main_scale = 192.0 ** (-0.5)
very_low = -1e30
MESH = pl.DeviceIdType.MESH
AXES = ("pb", "ha")


def visible(window_start, positions, first_row, width):
    columns = first_row + jnp.arange(width, dtype=jnp.int32)
    return (columns[None, :] >= window_start[:, None]) & (columns[None, :] <= positions[:, None])


def device_of(axis, peer):
    return tuple(peer if name == axis else lax.axis_index(name) for name in AXES)


def pair_peers(axis):
    n = lax.axis_size(axis)
    me = lax.axis_index(axis)
    sibling = me + 1 - 2 * lax.rem(me, 2)
    return sibling, [lax.rem(me + 2 * step, n) for step in range(1, n // 2)]


def barrier_peers(items):
    peers = []
    for axis in sorted({axis for axis, _, _ in items}):
        n = lax.axis_size(axis)
        me = lax.axis_index(axis)
        modes = {mode for item_axis, mode, _ in items if item_axis == axis}
        sibling, others = pair_peers(axis)
        if modes == {"sib"}:
            peers += [(axis, sibling)]
        elif modes == {"same"}:
            peers += [(axis, peer) for peer in others]
        elif modes == {"pair"}:
            peers += [(axis, sibling)] + [(axis, peer) for peer in others]
        else:
            peers += [(axis, lax.rem(me + step, n)) for step in range(1, n)]
    return peers


def plan(axis, mode):
    n = lax.axis_size(axis)
    me = lax.axis_index(axis)
    sibling, others = pair_peers(axis)
    always = None
    if mode == "a2a":
        return (
            [(lax.rem(me + s, n), lax.rem(me + s, n), me, always) for s in range(1, n)],
            [(lax.rem(me + n - s, n), lax.rem(me + n - s, n), always) for s in range(1, n)],
        )
    if mode == "gather":
        return (
            [(lax.rem(me + s, n), None, me, always) for s in range(1, n)],
            [(lax.rem(me + n - s, n), lax.rem(me + n - s, n), always) for s in range(1, n)],
        )
    if mode == "sib":
        parity = lax.rem(sibling, 2)
        return (
            [(sibling, 2 * j + parity, j, always) for j in range(n // 2)],
            [(sibling, j, always) for j in range(n // 2)],
        )
    if mode == "same":
        sources = [lax.rem(me + n - 2 * s, n) for s in range(1, n // 2)]
        return (
            [(peer, peer // 2, me // 2, peer // 2 < me // 2) for peer in others],
            [(peer, peer // 2, peer // 2 > me // 2) for peer in sources],
        )
    sources = [lax.rem(sibling + 2 * s, n) for s in range(1, n // 2)]
    return (
        [(sibling, None, me, always)] + [(peer, None, me, peer // 2 > me // 2) for peer in others],
        [(sibling, sibling, always)] + [(peer, peer, peer // 2 < me // 2) for peer in sources],
    )


def when(condition, body):
    if condition is None:
        body()
    else:
        pl.when(condition)(body)


def exchange_kernel(items, *refs):
    count = len(items)
    x_refs, y_refs = refs[:count], refs[count : 2 * count]
    send_sem, recv_sem, local_sem = refs[2 * count : 2 * count + 3]
    stride = max(lax.axis_size(axis) for axis, _, _ in items)
    forward_base = count * stride

    def remote(i, axis, source, slot, target, send_slot, recv_slot):
        return pltpu.make_async_remote_copy(
            src_ref=source,
            dst_ref=y_refs[i].at[slot],
            send_sem=send_sem.at[send_slot],
            recv_sem=recv_sem.at[recv_slot],
            device_id=device_of(axis, target),
            device_id_type=MESH,
        )

    barrier = pltpu.get_barrier_semaphore()
    peers = barrier_peers(items)
    for axis, peer in peers:
        pl.semaphore_signal(barrier, inc=1, device_id=device_of(axis, peer), device_id_type=MESH)
    if peers:
        pl.semaphore_wait(barrier, len(peers))

    sends = []
    order = sorted(range(count), key=lambda i: items[i][0] != "ha")
    for i in order:
        axis, mode, _ = items[i]
        for peer, chunk, slot, condition in plan(axis, mode)[0]:
            source = x_refs[i] if chunk is None else x_refs[i].at[chunk]
            send_slot = i * stride + (chunk if mode == "sib" else peer)
            copy = remote(i, axis, source, slot, peer, send_slot, i * stride + slot)
            when(condition, copy.start)
            sends.append((copy, condition))
    locals_ = []
    for i, (axis, mode, _) in enumerate(items):
        me = lax.axis_index(axis)
        n = lax.axis_size(axis)
        if mode == "sib":
            continue
        if mode == "same":
            own = (x_refs[i].at[me // 2], y_refs[i].at[me // 2])
            for j in range(n // 2):
                def clear(j=j):
                    y_refs[i][j] = jnp.zeros(y_refs[i].shape[1:], y_refs[i].dtype)
                when(j < me // 2, clear)
        elif mode == "a2a":
            own = (x_refs[i].at[me], y_refs[i].at[me])
        else:
            own = (x_refs[i], y_refs[i].at[me])
            if mode == "pair":
                for block in range(n):
                    def clear(block=block):
                        y_refs[i][block] = jnp.zeros(y_refs[i].shape[1:], y_refs[i].dtype)
                    when(block // 2 > me // 2, clear)
        copy = pltpu.make_async_copy(own[0], own[1], local_sem.at[i])
        copy.start()
        locals_.append(copy)

    forwards = []
    for i, (axis, mode, _) in enumerate(items):
        if mode != "pair":
            continue
        me = lax.axis_index(axis)
        sibling, others = pair_peers(axis)
        for block in others:
            arrived = remote(i, axis, y_refs[i].at[block], block, block, i * stride + block, i * stride + block)
            copy = remote(
                i, axis, y_refs[i].at[block], block, sibling, forward_base + i * stride + block,
                i * stride + block,
            )

            def relay(arrived=arrived, copy=copy):
                arrived.wait_recv()
                copy.start()

            when(block // 2 < me // 2, relay)
            forwards.append((copy, block // 2 < me // 2))

    for i, (axis, mode, _) in enumerate(items):
        for peer, slot, condition in plan(axis, mode)[1]:
            incoming = remote(i, axis, y_refs[i].at[slot], slot, peer, i * stride + slot, i * stride + slot)
            when(condition, incoming.wait_recv)
    for copy, condition in sends + forwards:
        when(condition, copy.wait_send)
    for copy in locals_:
        copy.wait()


def exchange(arrays, items, collective_id):
    count = len(arrays)
    items = tuple(items)

    def out_shape(a, axis, mode):
        n = lax.axis_size(axis)
        if mode == "a2a":
            return a.shape
        if mode in ("sib", "same"):
            return (n // 2,) + a.shape[1:]
        return (n,) + a.shape

    out_shapes = [jax.ShapeDtypeStruct(out_shape(a, axis, mode), a.dtype) for a, (axis, mode, _) in zip(arrays, items)]
    moved = sum(math.prod(o.shape) * a.dtype.itemsize for a, o in zip(arrays, out_shapes))
    slots = count * max(lax.axis_size(axis) for axis, _, _ in items)
    space = [pl.BlockSpec(memory_space=pl.ANY if hbm else pltpu.VMEM) for _, _, hbm in items]
    return pl.pallas_call(
        functools.partial(exchange_kernel, items),
        out_shape=out_shapes,
        in_specs=space,
        out_specs=[pl.BlockSpec(memory_space=pltpu.VMEM)] * count,
        scratch_shapes=[
            pltpu.SemaphoreType.DMA((2 * slots,)),
            pltpu.SemaphoreType.DMA((slots,)),
            pltpu.SemaphoreType.DMA((count,)),
        ],
        compiler_params=pltpu.CompilerParams(
            collective_id=collective_id, has_side_effects=True, vmem_limit_bytes=48 * 1024 * 1024
        ),
        cost_estimate=pl.CostEstimate(flops=0, transcendentals=0, bytes_accessed=2 * moved),
    )(*arrays)


def head_mass_kernel(query_rows, starts_ref, query_ref, latent_ref, sums_ref, out_ref):
    rows, width = out_ref.shape
    scores = lax.dot_general(
        query_ref[...], latent_ref[...], (((1,), (1,)), ((), ())), preferred_element_type=jnp.float32
    )
    mass = jnp.exp(scores * main_scale - sums_ref[...])
    mass = jnp.sum(mass.reshape(rows, mass.shape[0] // rows, width), axis=1)
    own_first = lax.axis_index("ha") * rows
    row_ids = lax.broadcasted_iota(jnp.int32, (rows, width), 0)
    starts = jnp.zeros((rows, width), jnp.int32)
    for row in range(rows):
        starts = jnp.where(row_ids == row, starts_ref[own_first + row], starts)
    positions = lax.axis_index("pb") * query_rows + own_first + row_ids
    columns = pl.program_id(0) * width + lax.broadcasted_iota(jnp.int32, (rows, width), 1)
    seen = (columns >= starts) & (columns <= positions)
    out_ref[...] = jnp.where(seen, mass, 0.0)


def head_mass(flat_query, latent_piece, flat_sums, window_start, rows):
    query_rows = window_start.shape[0]
    tokens, latent_width = latent_piece.shape
    width = math.gcd(tokens, 512)
    flat_rows = flat_query.shape[0]
    return pl.pallas_call(
        functools.partial(head_mass_kernel, query_rows),
        out_shape=jax.ShapeDtypeStruct((rows, tokens), jnp.float32),
        grid_spec=pltpu.PrefetchScalarGridSpec(
            num_scalar_prefetch=1,
            grid=(tokens // width,),
            in_specs=[
                pl.BlockSpec((flat_rows, latent_width), lambda k, starts: (0, 0)),
                pl.BlockSpec((width, latent_width), lambda k, starts: (k, 0)),
                pl.BlockSpec((flat_rows, 1), lambda k, starts: (0, 0)),
            ],
            out_specs=pl.BlockSpec((rows, width), lambda k, starts: (0, k)),
        ),
        cost_estimate=pl.CostEstimate(
            flops=2 * flat_rows * tokens * latent_width,
            transcendentals=flat_rows * tokens,
            bytes_accessed=flat_query.size * 2 + latent_piece.size * 2 + rows * tokens * 4,
        ),
    )(window_start, flat_query, latent_piece, flat_sums)


def indexer_kernel(query_rows, starts_ref, index_ref, keys_ref, weight_ref, probs_ref, qgrad_ref, wgrad_ref,
                   kgrad_ref):
    rows, tokens = probs_ref.shape
    flat = index_ref.shape[0]
    heads = flat // rows
    index = index_ref[...]
    keys = keys_ref[...]
    weight = weight_ref[...]
    active = lax.dot_general(index, keys, (((1,), (1,)), ((), ())), preferred_element_type=jnp.float32)
    relu_act = jnp.maximum(active, 0.0)
    logits = jnp.sum((weight * relu_act).reshape(rows, heads, tokens), axis=1)

    own_first = lax.axis_index("ha") * rows
    row_ids = lax.broadcasted_iota(jnp.int32, (rows, tokens), 0)
    starts = jnp.zeros((rows, tokens), jnp.int32)
    for row in range(rows):
        starts = jnp.where(row_ids == row, starts_ref[own_first + row], starts)
    positions = lax.axis_index("pb") * query_rows + own_first + row_ids
    columns = lax.broadcasted_iota(jnp.int32, (rows, tokens), 1)
    seen = (columns >= starts) & (columns <= positions)

    probs = probs_ref[...]
    target = probs / jnp.sum(probs, axis=1, keepdims=True)
    masked = jnp.where(seen, logits, very_low)
    row_top = jnp.max(masked, axis=1, keepdims=True)
    expo = jnp.where(seen, jnp.exp(masked - row_top), 0.0)
    grad = jnp.where(seen, expo / jnp.sum(expo, axis=1, keepdims=True) - target, 0.0)
    grad = jnp.broadcast_to(grad[:, None, :], (rows, heads, tokens)).reshape(flat, tokens)

    wgrad_ref[...] = jnp.sum(grad * relu_act, axis=1, keepdims=True)
    coeffs = jnp.where(active > 0.0, grad * weight, 0.0).astype(jnp.bfloat16)
    qgrad_ref[...] = jnp.dot(coeffs, keys, preferred_element_type=jnp.float32).astype(qgrad_ref.dtype)
    kgrad_ref[...] = lax.dot_general(
        coeffs, index, (((0,), (0,)), ((), ())), preferred_element_type=jnp.float32
    )


def indexer_grads(flat_index, keys_all, flat_weight, probs_all, window_start):
    flat, width = flat_index.shape
    rows, tokens = probs_all.shape
    vmem = pltpu.MemorySpace.VMEM
    return pl.pallas_call(
        functools.partial(indexer_kernel, window_start.shape[0]),
        out_shape=(
            jax.ShapeDtypeStruct((flat, width), jnp.bfloat16),
            jax.ShapeDtypeStruct((flat, 1), jnp.float32),
            jax.ShapeDtypeStruct((tokens, width), jnp.float32),
        ),
        in_specs=[pl.BlockSpec(memory_space=pltpu.SMEM)] + [pl.BlockSpec(memory_space=vmem)] * 4,
        out_specs=[pl.BlockSpec(memory_space=vmem)] * 3,
        compiler_params=pltpu.CompilerParams(vmem_limit_bytes=56 * 1024 * 1024),
        cost_estimate=pl.CostEstimate(
            flops=6 * flat * tokens * width, transcendentals=rows * tokens,
            bytes_accessed=(flat + tokens) * width * 2 + tokens * width * 4,
        ),
    )(window_start, flat_index, keys_all, flat_weight, probs_all)


def on_device(main_query, latent, log_sums, window_start, index_query, index_key, index_weight):
    query_rows, head_count, latent_width = main_query.shape
    index_width = index_query.shape[2]
    part_heads = index_query.shape[1]
    groups = lax.axis_size("ha")
    blocks = lax.axis_size("pb")
    tokens = query_rows * blocks
    own_rows = query_rows // groups
    index_heads = part_heads * groups
    all_heads = head_count * groups
    block_first = lax.axis_index("pb") * query_rows

    latent_parts, key_parts, query_parts, sums_parts, index_parts, weight_parts = exchange(
        [
            latent,
            index_key,
            main_query.reshape(groups, own_rows * head_count, latent_width),
            log_sums.reshape(groups, 1, own_rows * head_count),
            index_query.reshape(groups, own_rows * part_heads, index_width),
            index_weight.reshape(groups, 1, own_rows * part_heads),
        ],
        [
            ("pb", "pair", False),
            ("pb", "pair", False),
            ("ha", "a2a", True),
            ("ha", "a2a", False),
            ("ha", "a2a", False),
            ("ha", "a2a", False),
        ],
        0,
    )
    latent_piece = latent_parts.reshape(tokens, latent_width)
    keys_all = key_parts.reshape(tokens, index_width)
    local_query = (
        query_parts.reshape(groups, own_rows, head_count, latent_width)
        .transpose(1, 0, 2, 3)
        .reshape(own_rows * all_heads, latent_width)
    )
    local_sums = (
        sums_parts.reshape(groups, own_rows, head_count).transpose(1, 0, 2).reshape(own_rows * all_heads, 1)
    )
    local_index = (
        index_parts.reshape(groups, own_rows, part_heads, index_width)
        .transpose(1, 0, 2, 3)
        .reshape(own_rows, index_heads, index_width)
    )
    local_weight = (
        weight_parts.reshape(groups, own_rows, part_heads).transpose(1, 0, 2).reshape(own_rows, index_heads)
    )
    row_first = block_first + lax.axis_index("ha") * own_rows
    own_positions = row_first + jnp.arange(own_rows, dtype=jnp.int32)
    own_start = lax.dynamic_slice_in_dim(window_start, lax.axis_index("ha") * own_rows, own_rows, 0)

    probs_all = head_mass(local_query, latent_piece, local_sums, window_start, own_rows)

    flat_index = local_index.reshape(own_rows * index_heads, index_width)
    query_grad, weight_grad, key_grad = indexer_grads(
        flat_index, keys_all, local_weight.reshape(own_rows * index_heads, 1), probs_all, window_start
    )
    weight_grad = weight_grad.reshape(own_rows, index_heads)

    query_grad = query_grad.astype(jnp.bfloat16).reshape(own_rows, groups, part_heads, index_width)
    key_grad = key_grad.reshape(blocks, query_rows, index_width)
    sibling_part = exchange([key_grad], [("pb", "sib", False)], 1)[0]
    parity = lax.rem(lax.axis_index("pb"), 2)
    own_part = lax.dynamic_index_in_dim(
        key_grad.reshape(blocks // 2, 2, query_rows, index_width), parity, axis=1, keepdims=False
    )
    key_parts = exchange([own_part + sibling_part], [("pb", "same", False)], 4)[0]
    key_share = jnp.sum(key_parts, axis=0).reshape(groups, own_rows, index_width)
    key_rows, query_back, weight_back = exchange(
        [
            key_share,
            query_grad.transpose(1, 0, 2, 3).reshape(groups, own_rows * part_heads, index_width),
            weight_grad.reshape(own_rows, groups, part_heads)
            .transpose(1, 0, 2)
            .reshape(groups, 1, own_rows * part_heads),
        ],
        [("ha", "a2a", False), ("ha", "a2a", False), ("ha", "a2a", False)],
        2,
    )
    query_output = query_back.reshape(query_rows, part_heads, index_width)
    weight_output = weight_back.reshape(query_rows, part_heads)
    key_output = exchange([jnp.sum(key_rows, axis=0)], [("ha", "gather", False)], 3)[0]
    key_output = key_output.reshape(query_rows, index_width).astype(jnp.bfloat16)
    return (query_output, key_output, weight_output)


def solution(mesh):
    return jax.shard_map(
        on_device,
        mesh=mesh,
        in_specs=(
            P("pb", "ha", None),
            P("pb", None),
            P("pb", "ha"),
            P("pb"),
            P("pb", "ha", None),
            P("pb", None),
            P("pb", "ha"),
        ),
        out_specs=(P("pb", "ha", None), P("pb", None), P("pb", "ha")),
        check_vma=False,
    )
```

```python
import functools
import math

import jax
import jax.numpy as jnp
from jax import lax
from jax.experimental import pallas as pl
from jax.experimental.pallas import tpu as pltpu
from jax.sharding import PartitionSpec as P

main_scale = 192.0 ** (-0.5)
very_low = -1e30
MESH = pl.DeviceIdType.MESH
AXES = ("pb", "ha")


def visible(window_start, positions, first_row, width):
    columns = first_row + jnp.arange(width, dtype=jnp.int32)
    return (columns[None, :] >= window_start[:, None]) & (columns[None, :] <= positions[:, None])


def device_of(axis, peer):
    return tuple(peer if name == axis else lax.axis_index(name) for name in AXES)


def pair_peers(axis):
    n = lax.axis_size(axis)
    me = lax.axis_index(axis)
    sibling = me + 1 - 2 * lax.rem(me, 2)
    return sibling, [lax.rem(me + 2 * step, n) for step in range(1, n // 2)]


def barrier_peers(items):
    peers = []
    for axis in sorted({axis for axis, _, _ in items}):
        n = lax.axis_size(axis)
        me = lax.axis_index(axis)
        modes = {mode for item_axis, mode, _ in items if item_axis == axis}
        sibling, others = pair_peers(axis)
        if modes == {"sib"}:
            peers += [(axis, sibling)]
        elif modes == {"same"}:
            peers += [(axis, peer) for peer in others]
        elif modes == {"pair"}:
            peers += [(axis, sibling)] + [(axis, peer) for peer in others]
        else:
            peers += [(axis, lax.rem(me + step, n)) for step in range(1, n)]
    return peers


def plan(axis, mode):
    n = lax.axis_size(axis)
    me = lax.axis_index(axis)
    sibling, others = pair_peers(axis)
    always = None
    if mode == "a2a":
        return (
            [(lax.rem(me + s, n), lax.rem(me + s, n), me, always) for s in range(1, n)],
            [(lax.rem(me + n - s, n), lax.rem(me + n - s, n), always) for s in range(1, n)],
        )
    if mode == "gather":
        return (
            [(lax.rem(me + s, n), None, me, always) for s in range(1, n)],
            [(lax.rem(me + n - s, n), lax.rem(me + n - s, n), always) for s in range(1, n)],
        )
    if mode == "sib":
        parity = lax.rem(sibling, 2)
        return (
            [(sibling, 2 * j + parity, j, always) for j in range(n // 2)],
            [(sibling, j, always) for j in range(n // 2)],
        )
    if mode == "same":
        sources = [lax.rem(me + n - 2 * s, n) for s in range(1, n // 2)]
        return (
            [(peer, peer // 2, me // 2, peer // 2 < me // 2) for peer in others],
            [(peer, peer // 2, peer // 2 > me // 2) for peer in sources],
        )
    sources = [lax.rem(sibling + 2 * s, n) for s in range(1, n // 2)]
    return (
        [(sibling, None, me, always)] + [(peer, None, me, peer // 2 > me // 2) for peer in others],
        [(sibling, sibling, always)] + [(peer, peer, peer // 2 < me // 2) for peer in sources],
    )


def when(condition, body):
    if condition is None:
        body()
    else:
        pl.when(condition)(body)


def exchange_kernel(items, *refs):
    count = len(items)
    x_refs, y_refs = refs[:count], refs[count : 2 * count]
    send_sem, recv_sem, local_sem = refs[2 * count : 2 * count + 3]
    stride = max(lax.axis_size(axis) for axis, _, _ in items)
    forward_base = count * stride

    def remote(i, axis, source, slot, target, send_slot, recv_slot):
        return pltpu.make_async_remote_copy(
            src_ref=source,
            dst_ref=y_refs[i].at[slot],
            send_sem=send_sem.at[send_slot],
            recv_sem=recv_sem.at[recv_slot],
            device_id=device_of(axis, target),
            device_id_type=MESH,
        )

    barrier = pltpu.get_barrier_semaphore()
    peers = barrier_peers(items)
    for axis, peer in peers:
        pl.semaphore_signal(barrier, inc=1, device_id=device_of(axis, peer), device_id_type=MESH)
    if peers:
        pl.semaphore_wait(barrier, len(peers))

    sends = []
    order = sorted(range(count), key=lambda i: items[i][0] != "ha")
    for i in order:
        axis, mode, _ = items[i]
        for peer, chunk, slot, condition in plan(axis, mode)[0]:
            source = x_refs[i] if chunk is None else x_refs[i].at[chunk]
            send_slot = i * stride + (chunk if mode == "sib" else peer)
            copy = remote(i, axis, source, slot, peer, send_slot, i * stride + slot)
            when(condition, copy.start)
            sends.append((copy, condition))
    locals_ = []
    for i, (axis, mode, _) in enumerate(items):
        me = lax.axis_index(axis)
        n = lax.axis_size(axis)
        if mode == "sib":
            continue
        if mode == "same":
            own = (x_refs[i].at[me // 2], y_refs[i].at[me // 2])
            for j in range(n // 2):
                def clear(j=j):
                    y_refs[i][j] = jnp.zeros(y_refs[i].shape[1:], y_refs[i].dtype)
                when(j < me // 2, clear)
        elif mode == "a2a":
            own = (x_refs[i].at[me], y_refs[i].at[me])
        else:
            own = (x_refs[i], y_refs[i].at[me])
            if mode == "pair":
                for block in range(n):
                    def clear(block=block):
                        y_refs[i][block] = jnp.zeros(y_refs[i].shape[1:], y_refs[i].dtype)
                    when(block // 2 > me // 2, clear)
        copy = pltpu.make_async_copy(own[0], own[1], local_sem.at[i])
        copy.start()
        locals_.append(copy)

    forwards = []
    for i, (axis, mode, _) in enumerate(items):
        if mode != "pair":
            continue
        me = lax.axis_index(axis)
        sibling, others = pair_peers(axis)
        for block in others:
            arrived = remote(i, axis, y_refs[i].at[block], block, block, i * stride + block, i * stride + block)
            copy = remote(
                i, axis, y_refs[i].at[block], block, sibling, forward_base + i * stride + block,
                i * stride + block,
            )

            def relay(arrived=arrived, copy=copy):
                arrived.wait_recv()
                copy.start()

            when(block // 2 < me // 2, relay)
            forwards.append((copy, block // 2 < me // 2))

    for i, (axis, mode, _) in enumerate(items):
        for peer, slot, condition in plan(axis, mode)[1]:
            incoming = remote(i, axis, y_refs[i].at[slot], slot, peer, i * stride + slot, i * stride + slot)
            when(condition, incoming.wait_recv)
    for copy, condition in sends + forwards:
        when(condition, copy.wait_send)
    for copy in locals_:
        copy.wait()


def exchange(arrays, items, collective_id):
    count = len(arrays)
    items = tuple(items)

    def out_shape(a, axis, mode):
        n = lax.axis_size(axis)
        if mode == "a2a":
            return a.shape
        if mode in ("sib", "same"):
            return (n // 2,) + a.shape[1:]
        return (n,) + a.shape

    out_shapes = [jax.ShapeDtypeStruct(out_shape(a, axis, mode), a.dtype) for a, (axis, mode, _) in zip(arrays, items)]
    moved = sum(math.prod(o.shape) * a.dtype.itemsize for a, o in zip(arrays, out_shapes))
    slots = count * max(lax.axis_size(axis) for axis, _, _ in items)
    space = [pl.BlockSpec(memory_space=pl.ANY if hbm else pltpu.VMEM) for _, _, hbm in items]
    return pl.pallas_call(
        functools.partial(exchange_kernel, items),
        out_shape=out_shapes,
        in_specs=space,
        out_specs=[pl.BlockSpec(memory_space=pltpu.VMEM)] * count,
        scratch_shapes=[
            pltpu.SemaphoreType.DMA((2 * slots,)),
            pltpu.SemaphoreType.DMA((slots,)),
            pltpu.SemaphoreType.DMA((count,)),
        ],
        compiler_params=pltpu.CompilerParams(
            collective_id=collective_id, has_side_effects=True, vmem_limit_bytes=48 * 1024 * 1024
        ),
        cost_estimate=pl.CostEstimate(flops=0, transcendentals=0, bytes_accessed=2 * moved),
    )(*arrays)


def head_mass_kernel(query_rows, sources, starts_ref, query_ref, latent_ref, sums_ref, out_ref):
    rows, width = out_ref.shape
    scores = lax.dot_general(
        query_ref[...], latent_ref[...], (((1,), (1,)), ((), ())), preferred_element_type=jnp.float32
    )
    mass = jnp.exp(scores * main_scale - sums_ref[...])
    heads = mass.shape[0] // (rows * sources)
    mass = jnp.sum(mass.reshape(sources, rows, heads, width), axis=(0, 2))
    own_first = lax.axis_index("ha") * rows
    row_ids = lax.broadcasted_iota(jnp.int32, (rows, width), 0)
    starts = jnp.zeros((rows, width), jnp.int32)
    for row in range(rows):
        starts = jnp.where(row_ids == row, starts_ref[own_first + row], starts)
    positions = lax.axis_index("pb") * query_rows + own_first + row_ids
    columns = pl.program_id(0) * width + lax.broadcasted_iota(jnp.int32, (rows, width), 1)
    seen = (columns >= starts) & (columns <= positions)
    out_ref[...] = jnp.where(seen, mass, 0.0)


def head_mass(flat_query, latent_piece, flat_sums, window_start, rows, sources):
    query_rows = window_start.shape[0]
    tokens, latent_width = latent_piece.shape
    width = math.gcd(tokens, 512)
    flat_rows = flat_query.shape[0]
    return pl.pallas_call(
        functools.partial(head_mass_kernel, query_rows, sources),
        out_shape=jax.ShapeDtypeStruct((rows, tokens), jnp.float32),
        grid_spec=pltpu.PrefetchScalarGridSpec(
            num_scalar_prefetch=1,
            grid=(tokens // width,),
            in_specs=[
                pl.BlockSpec((flat_rows, latent_width), lambda k, starts: (0, 0)),
                pl.BlockSpec((width, latent_width), lambda k, starts: (k, 0)),
                pl.BlockSpec((flat_rows, 1), lambda k, starts: (0, 0)),
            ],
            out_specs=pl.BlockSpec((rows, width), lambda k, starts: (0, k)),
        ),
        cost_estimate=pl.CostEstimate(
            flops=2 * flat_rows * tokens * latent_width,
            transcendentals=flat_rows * tokens,
            bytes_accessed=flat_query.size * 2 + latent_piece.size * 2 + rows * tokens * 4,
        ),
    )(window_start, flat_query, latent_piece, flat_sums)


def indexer_kernel(query_rows, starts_ref, index_ref, keys_ref, weight_ref, probs_ref, qgrad_ref, wgrad_ref,
                   kgrad_ref):
    rows, tokens = probs_ref.shape
    flat = index_ref.shape[0]
    heads = flat // rows
    index = index_ref[...]
    keys = keys_ref[...]
    weight = weight_ref[...]
    active = lax.dot_general(index, keys, (((1,), (1,)), ((), ())), preferred_element_type=jnp.float32)
    relu_act = jnp.maximum(active, 0.0)
    logits = jnp.sum((weight * relu_act).reshape(rows, heads, tokens), axis=1)

    own_first = lax.axis_index("ha") * rows
    row_ids = lax.broadcasted_iota(jnp.int32, (rows, tokens), 0)
    starts = jnp.zeros((rows, tokens), jnp.int32)
    for row in range(rows):
        starts = jnp.where(row_ids == row, starts_ref[own_first + row], starts)
    positions = lax.axis_index("pb") * query_rows + own_first + row_ids
    columns = lax.broadcasted_iota(jnp.int32, (rows, tokens), 1)
    seen = (columns >= starts) & (columns <= positions)

    probs = probs_ref[...]
    target = probs / jnp.sum(probs, axis=1, keepdims=True)
    masked = jnp.where(seen, logits, very_low)
    row_top = jnp.max(masked, axis=1, keepdims=True)
    expo = jnp.where(seen, jnp.exp(masked - row_top), 0.0)
    grad = jnp.where(seen, expo / jnp.sum(expo, axis=1, keepdims=True) - target, 0.0)
    grad = jnp.broadcast_to(grad[:, None, :], (rows, heads, tokens)).reshape(flat, tokens)

    wgrad_ref[...] = jnp.sum(grad * relu_act, axis=1, keepdims=True)
    coeffs = jnp.where(active > 0.0, grad * weight, 0.0).astype(jnp.bfloat16)
    qgrad_ref[...] = jnp.dot(coeffs, keys, preferred_element_type=jnp.float32).astype(qgrad_ref.dtype)
    kgrad_ref[...] = lax.dot_general(
        coeffs, index, (((0,), (0,)), ((), ())), preferred_element_type=jnp.float32
    )


def indexer_grads(flat_index, keys_all, flat_weight, probs_all, window_start):
    flat, width = flat_index.shape
    rows, tokens = probs_all.shape
    vmem = pltpu.MemorySpace.VMEM
    return pl.pallas_call(
        functools.partial(indexer_kernel, window_start.shape[0]),
        out_shape=(
            jax.ShapeDtypeStruct((flat, width), jnp.bfloat16),
            jax.ShapeDtypeStruct((flat, 1), jnp.float32),
            jax.ShapeDtypeStruct((tokens, width), jnp.float32),
        ),
        in_specs=[pl.BlockSpec(memory_space=pltpu.SMEM)] + [pl.BlockSpec(memory_space=vmem)] * 4,
        out_specs=[pl.BlockSpec(memory_space=vmem)] * 3,
        compiler_params=pltpu.CompilerParams(vmem_limit_bytes=56 * 1024 * 1024),
        cost_estimate=pl.CostEstimate(
            flops=6 * flat * tokens * width, transcendentals=rows * tokens,
            bytes_accessed=(flat + tokens) * width * 2 + tokens * width * 4,
        ),
    )(window_start, flat_index, keys_all, flat_weight, probs_all)


def on_device(main_query, latent, log_sums, window_start, index_query, index_key, index_weight):
    query_rows, head_count, latent_width = main_query.shape
    index_width = index_query.shape[2]
    part_heads = index_query.shape[1]
    groups = lax.axis_size("ha")
    blocks = lax.axis_size("pb")
    tokens = query_rows * blocks
    own_rows = query_rows // groups
    index_heads = part_heads * groups
    all_heads = head_count * groups
    block_first = lax.axis_index("pb") * query_rows

    latent_parts, key_parts, query_parts, sums_parts, index_parts, weight_parts = exchange(
        [
            latent,
            index_key,
            main_query.reshape(groups, own_rows * head_count, latent_width),
            log_sums.reshape(groups, 1, own_rows * head_count),
            index_query.reshape(groups, own_rows * part_heads, index_width),
            index_weight.reshape(groups, 1, own_rows * part_heads),
        ],
        [
            ("pb", "pair", False),
            ("pb", "pair", False),
            ("ha", "a2a", True),
            ("ha", "a2a", False),
            ("ha", "a2a", False),
            ("ha", "a2a", False),
        ],
        0,
    )
    latent_piece = latent_parts.reshape(tokens, latent_width)
    keys_all = key_parts.reshape(tokens, index_width)
    local_query = query_parts.reshape(own_rows * all_heads, latent_width)
    local_sums = sums_parts.reshape(own_rows * all_heads, 1)
    local_index = (
        index_parts.reshape(groups, own_rows, part_heads, index_width)
        .transpose(1, 0, 2, 3)
        .reshape(own_rows, index_heads, index_width)
    )
    local_weight = (
        weight_parts.reshape(groups, own_rows, part_heads).transpose(1, 0, 2).reshape(own_rows, index_heads)
    )
    row_first = block_first + lax.axis_index("ha") * own_rows
    own_positions = row_first + jnp.arange(own_rows, dtype=jnp.int32)
    own_start = lax.dynamic_slice_in_dim(window_start, lax.axis_index("ha") * own_rows, own_rows, 0)

    probs_all = head_mass(local_query, latent_piece, local_sums, window_start, own_rows, groups)

    flat_index = local_index.reshape(own_rows * index_heads, index_width)
    query_grad, weight_grad, key_grad = indexer_grads(
        flat_index, keys_all, local_weight.reshape(own_rows * index_heads, 1), probs_all, window_start
    )
    weight_grad = weight_grad.reshape(own_rows, index_heads)

    query_grad = query_grad.astype(jnp.bfloat16).reshape(own_rows, groups, part_heads, index_width)
    key_grad = key_grad.reshape(blocks, query_rows, index_width)
    sibling_part = exchange([key_grad], [("pb", "sib", False)], 1)[0]
    parity = lax.rem(lax.axis_index("pb"), 2)
    own_part = lax.dynamic_index_in_dim(
        key_grad.reshape(blocks // 2, 2, query_rows, index_width), parity, axis=1, keepdims=False
    )
    key_parts = exchange([own_part + sibling_part], [("pb", "same", False)], 4)[0]
    key_share = jnp.sum(key_parts, axis=0).reshape(groups, own_rows, index_width)
    key_rows, query_back, weight_back = exchange(
        [
            key_share,
            query_grad.transpose(1, 0, 2, 3).reshape(groups, own_rows * part_heads, index_width),
            weight_grad.reshape(own_rows, groups, part_heads)
            .transpose(1, 0, 2)
            .reshape(groups, 1, own_rows * part_heads),
        ],
        [("ha", "a2a", False), ("ha", "a2a", False), ("ha", "a2a", False)],
        2,
    )
    query_output = query_back.reshape(query_rows, part_heads, index_width)
    weight_output = weight_back.reshape(query_rows, part_heads)
    key_output = exchange([jnp.sum(key_rows, axis=0)], [("ha", "gather", False)], 3)[0]
    key_output = key_output.reshape(query_rows, index_width).astype(jnp.bfloat16)
    return (query_output, key_output, weight_output)


def solution(mesh):
    return jax.shard_map(
        on_device,
        mesh=mesh,
        in_specs=(
            P("pb", "ha", None),
            P("pb", None),
            P("pb", "ha"),
            P("pb"),
            P("pb", "ha", None),
            P("pb", None),
            P("pb", "ha"),
        ),
        out_specs=(P("pb", "ha", None), P("pb", None), P("pb", "ha")),
        check_vma=False,
    )
```

```python
import functools
import math

import jax
import jax.numpy as jnp
from jax import lax
from jax.experimental import pallas as pl
from jax.experimental.pallas import tpu as pltpu
from jax.sharding import PartitionSpec as P

main_scale = 192.0 ** (-0.5)
very_low = -1e30
MESH = pl.DeviceIdType.MESH
AXES = ("pb", "ha")


def visible(window_start, positions, first_row, width):
    columns = first_row + jnp.arange(width, dtype=jnp.int32)
    return (columns[None, :] >= window_start[:, None]) & (columns[None, :] <= positions[:, None])


def device_of(axis, peer):
    return tuple(peer if name == axis else lax.axis_index(name) for name in AXES)


def pair_peers(axis):
    n = lax.axis_size(axis)
    me = lax.axis_index(axis)
    sibling = me + 1 - 2 * lax.rem(me, 2)
    return sibling, [lax.rem(me + 2 * step, n) for step in range(1, n // 2)]


def barrier_peers(items):
    peers = []
    for axis in sorted({axis for axis, _, _ in items}):
        n = lax.axis_size(axis)
        me = lax.axis_index(axis)
        modes = {mode for item_axis, mode, _ in items if item_axis == axis}
        sibling, others = pair_peers(axis)
        if modes == {"sib"}:
            peers += [(axis, sibling)]
        elif modes == {"same"}:
            peers += [(axis, peer) for peer in others]
        elif modes == {"pair"}:
            peers += [(axis, sibling)] + [(axis, peer) for peer in others]
        else:
            peers += [(axis, lax.rem(me + step, n)) for step in range(1, n)]
    return peers


def plan(axis, mode):
    n = lax.axis_size(axis)
    me = lax.axis_index(axis)
    sibling, others = pair_peers(axis)
    always = None
    if mode == "a2a":
        return (
            [(lax.rem(me + s, n), lax.rem(me + s, n), me, always) for s in range(1, n)],
            [(lax.rem(me + n - s, n), lax.rem(me + n - s, n), always) for s in range(1, n)],
        )
    if mode == "gather":
        return (
            [(lax.rem(me + s, n), None, me, always) for s in range(1, n)],
            [(lax.rem(me + n - s, n), lax.rem(me + n - s, n), always) for s in range(1, n)],
        )
    if mode == "sib":
        parity = lax.rem(sibling, 2)
        return (
            [(sibling, 2 * j + parity, j, always) for j in range(n // 2)],
            [(sibling, j, always) for j in range(n // 2)],
        )
    if mode == "same":
        sources = [lax.rem(me + n - 2 * s, n) for s in range(1, n // 2)]
        return (
            [(peer, peer // 2, me // 2, peer // 2 < me // 2) for peer in others],
            [(peer, peer // 2, peer // 2 > me // 2) for peer in sources],
        )
    sources = [lax.rem(sibling + 2 * s, n) for s in range(1, n // 2)]
    return (
        [(sibling, None, me, always)] + [(peer, None, me, peer // 2 > me // 2) for peer in others],
        [(sibling, sibling, always)] + [(peer, peer, peer // 2 < me // 2) for peer in sources],
    )


def when(condition, body):
    if condition is None:
        body()
    else:
        pl.when(condition)(body)


def exchange_kernel(items, *refs):
    count = len(items)
    x_refs, y_refs = refs[:count], refs[count : 2 * count]
    send_sem, recv_sem, local_sem = refs[2 * count : 2 * count + 3]
    stride = max(lax.axis_size(axis) for axis, _, _ in items)
    forward_base = count * stride

    def remote(i, axis, source, slot, target, send_slot, recv_slot):
        return pltpu.make_async_remote_copy(
            src_ref=source,
            dst_ref=y_refs[i].at[slot],
            send_sem=send_sem.at[send_slot],
            recv_sem=recv_sem.at[recv_slot],
            device_id=device_of(axis, target),
            device_id_type=MESH,
        )

    barrier = pltpu.get_barrier_semaphore()
    peers = barrier_peers(items)
    for axis, peer in peers:
        pl.semaphore_signal(barrier, inc=1, device_id=device_of(axis, peer), device_id_type=MESH)
    if peers:
        pl.semaphore_wait(barrier, len(peers))

    sends = []
    order = sorted(range(count), key=lambda i: items[i][0] != "ha")
    for i in order:
        axis, mode, _ = items[i]
        for peer, chunk, slot, condition in plan(axis, mode)[0]:
            source = x_refs[i] if chunk is None else x_refs[i].at[chunk]
            send_slot = i * stride + (chunk if mode == "sib" else peer)
            copy = remote(i, axis, source, slot, peer, send_slot, i * stride + slot)
            when(condition, copy.start)
            sends.append((copy, condition))
    locals_ = []
    for i, (axis, mode, _) in enumerate(items):
        me = lax.axis_index(axis)
        n = lax.axis_size(axis)
        if mode == "sib":
            continue
        if mode == "same":
            own = (x_refs[i].at[me // 2], y_refs[i].at[me // 2])
            for j in range(n // 2):
                def clear(j=j):
                    y_refs[i][j] = jnp.zeros(y_refs[i].shape[1:], y_refs[i].dtype)
                when(j < me // 2, clear)
        elif mode == "a2a":
            own = (x_refs[i].at[me], y_refs[i].at[me])
        else:
            own = (x_refs[i], y_refs[i].at[me])
            if mode == "pair":
                for block in range(n):
                    def clear(block=block):
                        y_refs[i][block] = jnp.zeros(y_refs[i].shape[1:], y_refs[i].dtype)
                    when(block // 2 > me // 2, clear)
        copy = pltpu.make_async_copy(own[0], own[1], local_sem.at[i])
        copy.start()
        locals_.append(copy)

    forwards = []
    for i, (axis, mode, _) in enumerate(items):
        if mode != "pair":
            continue
        me = lax.axis_index(axis)
        sibling, others = pair_peers(axis)
        for block in others:
            arrived = remote(i, axis, y_refs[i].at[block], block, block, i * stride + block, i * stride + block)
            copy = remote(
                i, axis, y_refs[i].at[block], block, sibling, forward_base + i * stride + block,
                i * stride + block,
            )

            def relay(arrived=arrived, copy=copy):
                arrived.wait_recv()
                copy.start()

            when(block // 2 < me // 2, relay)
            forwards.append((copy, block // 2 < me // 2))

    for i, (axis, mode, _) in enumerate(items):
        for peer, slot, condition in plan(axis, mode)[1]:
            incoming = remote(i, axis, y_refs[i].at[slot], slot, peer, i * stride + slot, i * stride + slot)
            when(condition, incoming.wait_recv)
    for copy, condition in sends + forwards:
        when(condition, copy.wait_send)
    for copy in locals_:
        copy.wait()


def exchange(arrays, items, collective_id):
    count = len(arrays)
    items = tuple(items)

    def out_shape(a, axis, mode):
        n = lax.axis_size(axis)
        if mode == "a2a":
            return a.shape
        if mode in ("sib", "same"):
            return (n // 2,) + a.shape[1:]
        return (n,) + a.shape

    out_shapes = [jax.ShapeDtypeStruct(out_shape(a, axis, mode), a.dtype) for a, (axis, mode, _) in zip(arrays, items)]
    moved = sum(math.prod(o.shape) * a.dtype.itemsize for a, o in zip(arrays, out_shapes))
    slots = count * max(lax.axis_size(axis) for axis, _, _ in items)
    space = [pl.BlockSpec(memory_space=pl.ANY if hbm else pltpu.VMEM) for _, _, hbm in items]
    return pl.pallas_call(
        functools.partial(exchange_kernel, items),
        out_shape=out_shapes,
        in_specs=space,
        out_specs=[pl.BlockSpec(memory_space=pltpu.VMEM)] * count,
        scratch_shapes=[
            pltpu.SemaphoreType.DMA((2 * slots,)),
            pltpu.SemaphoreType.DMA((slots,)),
            pltpu.SemaphoreType.DMA((count,)),
        ],
        compiler_params=pltpu.CompilerParams(
            collective_id=collective_id, has_side_effects=True, vmem_limit_bytes=48 * 1024 * 1024
        ),
        cost_estimate=pl.CostEstimate(flops=0, transcendentals=0, bytes_accessed=2 * moved),
    )(*arrays)


def head_mass_kernel(query_rows, starts_ref, query_ref, latent_ref, sums_ref, out_ref):
    rows, width = out_ref.shape
    scores = lax.dot_general(
        query_ref[...], latent_ref[...], (((1,), (1,)), ((), ())), preferred_element_type=jnp.float32
    )
    mass = jnp.exp(scores * main_scale - sums_ref[...])
    mass = jnp.sum(mass.reshape(rows, mass.shape[0] // rows, width), axis=1)
    own_first = lax.axis_index("ha") * rows
    row_ids = lax.broadcasted_iota(jnp.int32, (rows, width), 0)
    starts = jnp.zeros((rows, width), jnp.int32)
    for row in range(rows):
        starts = jnp.where(row_ids == row, starts_ref[own_first + row], starts)
    positions = lax.axis_index("pb") * query_rows + own_first + row_ids
    columns = pl.program_id(0) * width + lax.broadcasted_iota(jnp.int32, (rows, width), 1)
    seen = (columns >= starts) & (columns <= positions)
    out_ref[...] = jnp.where(seen, mass, 0.0)


def head_mass(flat_query, latent_piece, flat_sums, window_start, rows):
    query_rows = window_start.shape[0]
    tokens, latent_width = latent_piece.shape
    width = math.gcd(tokens, 1024)
    flat_rows = flat_query.shape[0]
    return pl.pallas_call(
        functools.partial(head_mass_kernel, query_rows),
        out_shape=jax.ShapeDtypeStruct((rows, tokens), jnp.float32),
        grid_spec=pltpu.PrefetchScalarGridSpec(
            num_scalar_prefetch=1,
            grid=(tokens // width,),
            in_specs=[
                pl.BlockSpec((flat_rows, latent_width), lambda k, starts: (0, 0)),
                pl.BlockSpec((width, latent_width), lambda k, starts: (k, 0)),
                pl.BlockSpec((flat_rows, 1), lambda k, starts: (0, 0)),
            ],
            out_specs=pl.BlockSpec((rows, width), lambda k, starts: (0, k)),
        ),
        cost_estimate=pl.CostEstimate(
            flops=2 * flat_rows * tokens * latent_width,
            transcendentals=flat_rows * tokens,
            bytes_accessed=flat_query.size * 2 + latent_piece.size * 2 + rows * tokens * 4,
        ),
    )(window_start, flat_query, latent_piece, flat_sums)


def indexer_kernel(query_rows, starts_ref, index_ref, keys_ref, weight_ref, probs_ref, qgrad_ref, wgrad_ref,
                   kgrad_ref):
    rows, tokens = probs_ref.shape
    flat = index_ref.shape[0]
    heads = flat // rows
    index = index_ref[...]
    keys = keys_ref[...]
    weight = weight_ref[...]
    active = lax.dot_general(index, keys, (((1,), (1,)), ((), ())), preferred_element_type=jnp.float32)
    relu_act = jnp.maximum(active, 0.0)
    logits = jnp.sum((weight * relu_act).reshape(rows, heads, tokens), axis=1)

    own_first = lax.axis_index("ha") * rows
    row_ids = lax.broadcasted_iota(jnp.int32, (rows, tokens), 0)
    starts = jnp.zeros((rows, tokens), jnp.int32)
    for row in range(rows):
        starts = jnp.where(row_ids == row, starts_ref[own_first + row], starts)
    positions = lax.axis_index("pb") * query_rows + own_first + row_ids
    columns = lax.broadcasted_iota(jnp.int32, (rows, tokens), 1)
    seen = (columns >= starts) & (columns <= positions)

    probs = probs_ref[...]
    target = probs / jnp.sum(probs, axis=1, keepdims=True)
    masked = jnp.where(seen, logits, very_low)
    row_top = jnp.max(masked, axis=1, keepdims=True)
    expo = jnp.where(seen, jnp.exp(masked - row_top), 0.0)
    grad = jnp.where(seen, expo / jnp.sum(expo, axis=1, keepdims=True) - target, 0.0)
    grad = jnp.broadcast_to(grad[:, None, :], (rows, heads, tokens)).reshape(flat, tokens)

    wgrad_ref[...] = jnp.sum(grad * relu_act, axis=1, keepdims=True)
    coeffs = jnp.where(active > 0.0, grad * weight, 0.0).astype(jnp.bfloat16)
    qgrad_ref[...] = jnp.dot(coeffs, keys, preferred_element_type=jnp.float32).astype(qgrad_ref.dtype)
    kgrad_ref[...] = lax.dot_general(
        coeffs, index, (((0,), (0,)), ((), ())), preferred_element_type=jnp.float32
    )


def indexer_grads(flat_index, keys_all, flat_weight, probs_all, window_start):
    flat, width = flat_index.shape
    rows, tokens = probs_all.shape
    vmem = pltpu.MemorySpace.VMEM
    return pl.pallas_call(
        functools.partial(indexer_kernel, window_start.shape[0]),
        out_shape=(
            jax.ShapeDtypeStruct((flat, width), jnp.bfloat16),
            jax.ShapeDtypeStruct((flat, 1), jnp.float32),
            jax.ShapeDtypeStruct((tokens, width), jnp.float32),
        ),
        in_specs=[pl.BlockSpec(memory_space=pltpu.SMEM)] + [pl.BlockSpec(memory_space=vmem)] * 4,
        out_specs=[pl.BlockSpec(memory_space=vmem)] * 3,
        compiler_params=pltpu.CompilerParams(vmem_limit_bytes=56 * 1024 * 1024),
        cost_estimate=pl.CostEstimate(
            flops=6 * flat * tokens * width, transcendentals=rows * tokens,
            bytes_accessed=(flat + tokens) * width * 2 + tokens * width * 4,
        ),
    )(window_start, flat_index, keys_all, flat_weight, probs_all)


def on_device(main_query, latent, log_sums, window_start, index_query, index_key, index_weight):
    query_rows, head_count, latent_width = main_query.shape
    index_width = index_query.shape[2]
    part_heads = index_query.shape[1]
    groups = lax.axis_size("ha")
    blocks = lax.axis_size("pb")
    tokens = query_rows * blocks
    own_rows = query_rows // groups
    index_heads = part_heads * groups
    all_heads = head_count * groups
    block_first = lax.axis_index("pb") * query_rows

    latent_parts, key_parts, query_parts, sums_parts, index_parts, weight_parts = exchange(
        [
            latent,
            index_key,
            main_query.reshape(groups, own_rows * head_count, latent_width),
            log_sums.reshape(groups, 1, own_rows * head_count),
            index_query.reshape(groups, own_rows * part_heads, index_width),
            index_weight.reshape(groups, 1, own_rows * part_heads),
        ],
        [
            ("pb", "pair", False),
            ("pb", "pair", False),
            ("ha", "a2a", True),
            ("ha", "a2a", False),
            ("ha", "a2a", False),
            ("ha", "a2a", False),
        ],
        0,
    )
    latent_piece = latent_parts.reshape(tokens, latent_width)
    keys_all = key_parts.reshape(tokens, index_width)
    local_query = (
        query_parts.reshape(groups, own_rows, head_count, latent_width)
        .transpose(1, 0, 2, 3)
        .reshape(own_rows * all_heads, latent_width)
    )
    local_sums = (
        sums_parts.reshape(groups, own_rows, head_count).transpose(1, 0, 2).reshape(own_rows * all_heads, 1)
    )
    local_index = (
        index_parts.reshape(groups, own_rows, part_heads, index_width)
        .transpose(1, 0, 2, 3)
        .reshape(own_rows, index_heads, index_width)
    )
    local_weight = (
        weight_parts.reshape(groups, own_rows, part_heads).transpose(1, 0, 2).reshape(own_rows, index_heads)
    )
    row_first = block_first + lax.axis_index("ha") * own_rows
    own_positions = row_first + jnp.arange(own_rows, dtype=jnp.int32)
    own_start = lax.dynamic_slice_in_dim(window_start, lax.axis_index("ha") * own_rows, own_rows, 0)

    probs_all = head_mass(local_query, latent_piece, local_sums, window_start, own_rows)

    flat_index = local_index.reshape(own_rows * index_heads, index_width)
    query_grad, weight_grad, key_grad = indexer_grads(
        flat_index, keys_all, local_weight.reshape(own_rows * index_heads, 1), probs_all, window_start
    )
    weight_grad = weight_grad.reshape(own_rows, index_heads)

    query_grad = query_grad.astype(jnp.bfloat16).reshape(own_rows, groups, part_heads, index_width)
    key_grad = key_grad.reshape(blocks, query_rows, index_width)
    sibling_part = exchange([key_grad], [("pb", "sib", False)], 1)[0]
    parity = lax.rem(lax.axis_index("pb"), 2)
    own_part = lax.dynamic_index_in_dim(
        key_grad.reshape(blocks // 2, 2, query_rows, index_width), parity, axis=1, keepdims=False
    )
    key_parts = exchange([own_part + sibling_part], [("pb", "same", False)], 4)[0]
    key_share = jnp.sum(key_parts, axis=0).reshape(groups, own_rows, index_width)
    key_rows, query_back, weight_back = exchange(
        [
            key_share,
            query_grad.transpose(1, 0, 2, 3).reshape(groups, own_rows * part_heads, index_width),
            weight_grad.reshape(own_rows, groups, part_heads)
            .transpose(1, 0, 2)
            .reshape(groups, 1, own_rows * part_heads),
        ],
        [("ha", "a2a", False), ("ha", "a2a", False), ("ha", "a2a", False)],
        2,
    )
    query_output = query_back.reshape(query_rows, part_heads, index_width)
    weight_output = weight_back.reshape(query_rows, part_heads)
    key_rows = jnp.sum(key_rows, axis=0).astype(jnp.bfloat16)
    key_output = exchange([key_rows], [("ha", "gather", False)], 3)[0]
    key_output = key_output.reshape(query_rows, index_width)
    return (query_output, key_output, weight_output)


def solution(mesh):
    return jax.shard_map(
        on_device,
        mesh=mesh,
        in_specs=(
            P("pb", "ha", None),
            P("pb", None),
            P("pb", "ha"),
            P("pb"),
            P("pb", "ha", None),
            P("pb", None),
            P("pb", "ha"),
        ),
        out_specs=(P("pb", "ha", None), P("pb", None), P("pb", "ha")),
        check_vma=False,
    )
```

```python
import functools
import math

import jax
import jax.numpy as jnp
from jax import lax
from jax.experimental import pallas as pl
from jax.experimental.pallas import tpu as pltpu
from jax.sharding import PartitionSpec as P

main_scale = 192.0 ** (-0.5)
very_low = -1e30
MESH = pl.DeviceIdType.MESH
AXES = ("pb", "ha")


def visible(window_start, positions, first_row, width):
    columns = first_row + jnp.arange(width, dtype=jnp.int32)
    return (columns[None, :] >= window_start[:, None]) & (columns[None, :] <= positions[:, None])


def device_of(axis, peer):
    return tuple(peer if name == axis else lax.axis_index(name) for name in AXES)


def pair_peers(axis):
    n = lax.axis_size(axis)
    me = lax.axis_index(axis)
    sibling = me + 1 - 2 * lax.rem(me, 2)
    return sibling, [lax.rem(me + 2 * step, n) for step in range(1, n // 2)]


def barrier_peers(items):
    peers = []
    for axis in sorted({axis for axis, _, _ in items}):
        n = lax.axis_size(axis)
        me = lax.axis_index(axis)
        modes = {mode for item_axis, mode, _ in items if item_axis == axis}
        sibling, others = pair_peers(axis)
        if modes == {"sib"}:
            peers += [(axis, sibling)]
        elif modes == {"same"}:
            peers += [(axis, peer) for peer in others]
        elif modes == {"pair"}:
            peers += [(axis, sibling)] + [(axis, peer) for peer in others]
        else:
            peers += [(axis, lax.rem(me + step, n)) for step in range(1, n)]
    return peers


def plan(axis, mode):
    n = lax.axis_size(axis)
    me = lax.axis_index(axis)
    sibling, others = pair_peers(axis)
    always = None
    if mode == "a2a":
        return (
            [(lax.rem(me + s, n), lax.rem(me + s, n), me, always) for s in range(1, n)],
            [(lax.rem(me + n - s, n), lax.rem(me + n - s, n), always) for s in range(1, n)],
        )
    if mode == "gather":
        return (
            [(lax.rem(me + s, n), None, me, always) for s in range(1, n)],
            [(lax.rem(me + n - s, n), lax.rem(me + n - s, n), always) for s in range(1, n)],
        )
    if mode == "sib":
        parity = lax.rem(sibling, 2)
        return (
            [(sibling, 2 * j + parity, j, always) for j in range(n // 2)],
            [(sibling, j, always) for j in range(n // 2)],
        )
    if mode == "same":
        sources = [lax.rem(me + n - 2 * s, n) for s in range(1, n // 2)]
        return (
            [(peer, peer // 2, me // 2, peer // 2 < me // 2) for peer in others],
            [(peer, peer // 2, peer // 2 > me // 2) for peer in sources],
        )
    sources = [lax.rem(sibling + 2 * s, n) for s in range(1, n // 2)]
    return (
        [(sibling, None, me, always)] + [(peer, None, me, peer // 2 > me // 2) for peer in others],
        [(sibling, sibling, always)] + [(peer, peer, peer // 2 < me // 2) for peer in sources],
    )


def when(condition, body):
    if condition is None:
        body()
    else:
        pl.when(condition)(body)


def exchange_kernel(items, *refs):
    count = len(items)
    x_refs, y_refs = refs[:count], refs[count : 2 * count]
    send_sem, recv_sem, local_sem = refs[2 * count : 2 * count + 3]
    stride = max(lax.axis_size(axis) for axis, _, _ in items)
    forward_base = count * stride

    def remote(i, axis, source, slot, target, send_slot, recv_slot):
        return pltpu.make_async_remote_copy(
            src_ref=source,
            dst_ref=y_refs[i].at[slot],
            send_sem=send_sem.at[send_slot],
            recv_sem=recv_sem.at[recv_slot],
            device_id=device_of(axis, target),
            device_id_type=MESH,
        )

    barrier = pltpu.get_barrier_semaphore()
    peers = barrier_peers(items)
    for axis, peer in peers:
        pl.semaphore_signal(barrier, inc=1, device_id=device_of(axis, peer), device_id_type=MESH)
    if peers:
        pl.semaphore_wait(barrier, len(peers))

    sends = []
    order = sorted(range(count), key=lambda i: items[i][0] != "ha")
    for i in order:
        axis, mode, _ = items[i]
        for peer, chunk, slot, condition in plan(axis, mode)[0]:
            source = x_refs[i] if chunk is None else x_refs[i].at[chunk]
            send_slot = i * stride + (chunk if mode == "sib" else peer)
            copy = remote(i, axis, source, slot, peer, send_slot, i * stride + slot)
            when(condition, copy.start)
            sends.append((copy, condition))
    locals_ = []
    for i, (axis, mode, _) in enumerate(items):
        me = lax.axis_index(axis)
        n = lax.axis_size(axis)
        if mode == "sib":
            continue
        if mode == "same":
            own = (x_refs[i].at[me // 2], y_refs[i].at[me // 2])
            for j in range(n // 2):
                def clear(j=j):
                    y_refs[i][j] = jnp.zeros(y_refs[i].shape[1:], y_refs[i].dtype)
                when(j < me // 2, clear)
        elif mode == "a2a":
            own = (x_refs[i].at[me], y_refs[i].at[me])
        else:
            own = (x_refs[i], y_refs[i].at[me])
            if mode == "pair":
                for block in range(n):
                    def clear(block=block):
                        y_refs[i][block] = jnp.zeros(y_refs[i].shape[1:], y_refs[i].dtype)
                    when(block // 2 > me // 2, clear)
        copy = pltpu.make_async_copy(own[0], own[1], local_sem.at[i])
        copy.start()
        locals_.append(copy)

    forwards = []
    for i, (axis, mode, _) in enumerate(items):
        if mode != "pair":
            continue
        me = lax.axis_index(axis)
        sibling, others = pair_peers(axis)
        for block in others:
            arrived = remote(i, axis, y_refs[i].at[block], block, block, i * stride + block, i * stride + block)
            copy = remote(
                i, axis, y_refs[i].at[block], block, sibling, forward_base + i * stride + block,
                i * stride + block,
            )

            def relay(arrived=arrived, copy=copy):
                arrived.wait_recv()
                copy.start()

            when(block // 2 < me // 2, relay)
            forwards.append((copy, block // 2 < me // 2))

    for i, (axis, mode, _) in enumerate(items):
        for peer, slot, condition in plan(axis, mode)[1]:
            incoming = remote(i, axis, y_refs[i].at[slot], slot, peer, i * stride + slot, i * stride + slot)
            when(condition, incoming.wait_recv)
    for copy, condition in sends + forwards:
        when(condition, copy.wait_send)
    for copy in locals_:
        copy.wait()


def exchange(arrays, items, collective_id):
    count = len(arrays)
    items = tuple(items)

    def out_shape(a, axis, mode):
        n = lax.axis_size(axis)
        if mode == "a2a":
            return a.shape
        if mode in ("sib", "same"):
            return (n // 2,) + a.shape[1:]
        return (n,) + a.shape

    out_shapes = [jax.ShapeDtypeStruct(out_shape(a, axis, mode), a.dtype) for a, (axis, mode, _) in zip(arrays, items)]
    moved = sum(math.prod(o.shape) * a.dtype.itemsize for a, o in zip(arrays, out_shapes))
    slots = count * max(lax.axis_size(axis) for axis, _, _ in items)
    space = [pl.BlockSpec(memory_space=pl.ANY if hbm else pltpu.VMEM) for _, _, hbm in items]
    return pl.pallas_call(
        functools.partial(exchange_kernel, items),
        out_shape=out_shapes,
        in_specs=space,
        out_specs=[pl.BlockSpec(memory_space=pltpu.VMEM)] * count,
        scratch_shapes=[
            pltpu.SemaphoreType.DMA((2 * slots,)),
            pltpu.SemaphoreType.DMA((slots,)),
            pltpu.SemaphoreType.DMA((count,)),
        ],
        compiler_params=pltpu.CompilerParams(
            collective_id=collective_id, has_side_effects=True, vmem_limit_bytes=48 * 1024 * 1024
        ),
        cost_estimate=pl.CostEstimate(flops=0, transcendentals=0, bytes_accessed=2 * moved),
    )(*arrays)


def head_mass_kernel(query_rows, starts_ref, query_ref, latent_ref, sums_ref, out_ref):
    rows, width = out_ref.shape
    scores = lax.dot_general(
        query_ref[...], latent_ref[...], (((1,), (1,)), ((), ())), preferred_element_type=jnp.float32
    )
    mass = jnp.exp(scores * main_scale - sums_ref[...])
    mass = jnp.sum(mass.reshape(rows, mass.shape[0] // rows, width), axis=1)
    own_first = lax.axis_index("ha") * rows
    row_ids = lax.broadcasted_iota(jnp.int32, (rows, width), 0)
    starts = jnp.zeros((rows, width), jnp.int32)
    for row in range(rows):
        starts = jnp.where(row_ids == row, starts_ref[own_first + row], starts)
    positions = lax.axis_index("pb") * query_rows + own_first + row_ids
    columns = pl.program_id(0) * width + lax.broadcasted_iota(jnp.int32, (rows, width), 1)
    seen = (columns >= starts) & (columns <= positions)
    out_ref[...] = jnp.where(seen, mass, 0.0)


def head_mass(flat_query, latent_piece, flat_sums, window_start, rows):
    query_rows = window_start.shape[0]
    tokens, latent_width = latent_piece.shape
    width = math.gcd(tokens, 2048)
    flat_rows = flat_query.shape[0]
    return pl.pallas_call(
        functools.partial(head_mass_kernel, query_rows),
        out_shape=jax.ShapeDtypeStruct((rows, tokens), jnp.float32),
        grid_spec=pltpu.PrefetchScalarGridSpec(
            num_scalar_prefetch=1,
            grid=(tokens // width,),
            in_specs=[
                pl.BlockSpec((flat_rows, latent_width), lambda k, starts: (0, 0)),
                pl.BlockSpec((width, latent_width), lambda k, starts: (k, 0)),
                pl.BlockSpec((flat_rows, 1), lambda k, starts: (0, 0)),
            ],
            out_specs=pl.BlockSpec((rows, width), lambda k, starts: (0, k)),
        ),
        cost_estimate=pl.CostEstimate(
            flops=2 * flat_rows * tokens * latent_width,
            transcendentals=flat_rows * tokens,
            bytes_accessed=flat_query.size * 2 + latent_piece.size * 2 + rows * tokens * 4,
        ),
    )(window_start, flat_query, latent_piece, flat_sums)


def indexer_kernel(query_rows, starts_ref, index_ref, keys_ref, weight_ref, probs_ref, qgrad_ref, wgrad_ref,
                   kgrad_ref):
    rows, tokens = probs_ref.shape
    flat = index_ref.shape[0]
    heads = flat // rows
    index = index_ref[...]
    keys = keys_ref[...]
    weight = weight_ref[...]
    active = lax.dot_general(index, keys, (((1,), (1,)), ((), ())), preferred_element_type=jnp.float32)
    relu_act = jnp.maximum(active, 0.0)
    logits = jnp.sum((weight * relu_act).reshape(rows, heads, tokens), axis=1)

    own_first = lax.axis_index("ha") * rows
    row_ids = lax.broadcasted_iota(jnp.int32, (rows, tokens), 0)
    starts = jnp.zeros((rows, tokens), jnp.int32)
    for row in range(rows):
        starts = jnp.where(row_ids == row, starts_ref[own_first + row], starts)
    positions = lax.axis_index("pb") * query_rows + own_first + row_ids
    columns = lax.broadcasted_iota(jnp.int32, (rows, tokens), 1)
    seen = (columns >= starts) & (columns <= positions)

    probs = probs_ref[...]
    target = probs / jnp.sum(probs, axis=1, keepdims=True)
    masked = jnp.where(seen, logits, very_low)
    row_top = jnp.max(masked, axis=1, keepdims=True)
    expo = jnp.where(seen, jnp.exp(masked - row_top), 0.0)
    grad = jnp.where(seen, expo / jnp.sum(expo, axis=1, keepdims=True) - target, 0.0)
    grad = jnp.broadcast_to(grad[:, None, :], (rows, heads, tokens)).reshape(flat, tokens)

    wgrad_ref[...] = jnp.sum(grad * relu_act, axis=1, keepdims=True)
    coeffs = jnp.where(active > 0.0, grad * weight, 0.0).astype(jnp.bfloat16)
    qgrad_ref[...] = jnp.dot(coeffs, keys, preferred_element_type=jnp.float32).astype(qgrad_ref.dtype)
    kgrad_ref[...] = lax.dot_general(
        coeffs, index, (((0,), (0,)), ((), ())), preferred_element_type=jnp.float32
    )


def indexer_grads(flat_index, keys_all, flat_weight, probs_all, window_start):
    flat, width = flat_index.shape
    rows, tokens = probs_all.shape
    vmem = pltpu.MemorySpace.VMEM
    return pl.pallas_call(
        functools.partial(indexer_kernel, window_start.shape[0]),
        out_shape=(
            jax.ShapeDtypeStruct((flat, width), jnp.bfloat16),
            jax.ShapeDtypeStruct((flat, 1), jnp.float32),
            jax.ShapeDtypeStruct((tokens, width), jnp.float32),
        ),
        in_specs=[pl.BlockSpec(memory_space=pltpu.SMEM)] + [pl.BlockSpec(memory_space=vmem)] * 4,
        out_specs=[pl.BlockSpec(memory_space=vmem)] * 3,
        compiler_params=pltpu.CompilerParams(vmem_limit_bytes=56 * 1024 * 1024),
        cost_estimate=pl.CostEstimate(
            flops=6 * flat * tokens * width, transcendentals=rows * tokens,
            bytes_accessed=(flat + tokens) * width * 2 + tokens * width * 4,
        ),
    )(window_start, flat_index, keys_all, flat_weight, probs_all)


def on_device(main_query, latent, log_sums, window_start, index_query, index_key, index_weight):
    query_rows, head_count, latent_width = main_query.shape
    index_width = index_query.shape[2]
    part_heads = index_query.shape[1]
    groups = lax.axis_size("ha")
    blocks = lax.axis_size("pb")
    tokens = query_rows * blocks
    own_rows = query_rows // groups
    index_heads = part_heads * groups
    all_heads = head_count * groups
    block_first = lax.axis_index("pb") * query_rows

    latent_parts, key_parts, query_parts, sums_parts, index_parts, weight_parts = exchange(
        [
            latent,
            index_key,
            main_query.reshape(groups, own_rows * head_count, latent_width),
            log_sums.reshape(groups, 1, own_rows * head_count),
            index_query.reshape(groups, own_rows * part_heads, index_width),
            index_weight.reshape(groups, 1, own_rows * part_heads),
        ],
        [
            ("pb", "pair", False),
            ("pb", "pair", False),
            ("ha", "a2a", True),
            ("ha", "a2a", False),
            ("ha", "a2a", False),
            ("ha", "a2a", False),
        ],
        0,
    )
    latent_piece = latent_parts.reshape(tokens, latent_width)
    keys_all = key_parts.reshape(tokens, index_width)
    local_query = (
        query_parts.reshape(groups, own_rows, head_count, latent_width)
        .transpose(1, 0, 2, 3)
        .reshape(own_rows * all_heads, latent_width)
    )
    local_sums = (
        sums_parts.reshape(groups, own_rows, head_count).transpose(1, 0, 2).reshape(own_rows * all_heads, 1)
    )
    local_index = (
        index_parts.reshape(groups, own_rows, part_heads, index_width)
        .transpose(1, 0, 2, 3)
        .reshape(own_rows, index_heads, index_width)
    )
    local_weight = (
        weight_parts.reshape(groups, own_rows, part_heads).transpose(1, 0, 2).reshape(own_rows, index_heads)
    )
    row_first = block_first + lax.axis_index("ha") * own_rows
    own_positions = row_first + jnp.arange(own_rows, dtype=jnp.int32)
    own_start = lax.dynamic_slice_in_dim(window_start, lax.axis_index("ha") * own_rows, own_rows, 0)

    probs_all = head_mass(local_query, latent_piece, local_sums, window_start, own_rows)

    flat_index = local_index.reshape(own_rows * index_heads, index_width)
    query_grad, weight_grad, key_grad = indexer_grads(
        flat_index, keys_all, local_weight.reshape(own_rows * index_heads, 1), probs_all, window_start
    )
    weight_grad = weight_grad.reshape(own_rows, index_heads)

    query_grad = query_grad.astype(jnp.bfloat16).reshape(own_rows, groups, part_heads, index_width)
    key_grad = key_grad.reshape(blocks, query_rows, index_width)
    sibling_part = exchange([key_grad], [("pb", "sib", False)], 1)[0]
    parity = lax.rem(lax.axis_index("pb"), 2)
    own_part = lax.dynamic_index_in_dim(
        key_grad.reshape(blocks // 2, 2, query_rows, index_width), parity, axis=1, keepdims=False
    )
    key_parts = exchange([own_part + sibling_part], [("pb", "same", False)], 4)[0]
    key_share = jnp.sum(key_parts, axis=0).reshape(groups, own_rows, index_width)
    key_rows, query_back, weight_back = exchange(
        [
            key_share,
            query_grad.transpose(1, 0, 2, 3).reshape(groups, own_rows * part_heads, index_width),
            weight_grad.reshape(own_rows, groups, part_heads)
            .transpose(1, 0, 2)
            .reshape(groups, 1, own_rows * part_heads),
        ],
        [("ha", "a2a", False), ("ha", "a2a", False), ("ha", "a2a", False)],
        2,
    )
    query_output = query_back.reshape(query_rows, part_heads, index_width)
    weight_output = weight_back.reshape(query_rows, part_heads)
    key_rows = jnp.sum(key_rows, axis=0).astype(jnp.bfloat16)
    key_output = exchange([key_rows], [("ha", "gather", False)], 3)[0]
    key_output = key_output.reshape(query_rows, index_width)
    return (query_output, key_output, weight_output)


def solution(mesh):
    return jax.shard_map(
        on_device,
        mesh=mesh,
        in_specs=(
            P("pb", "ha", None),
            P("pb", None),
            P("pb", "ha"),
            P("pb"),
            P("pb", "ha", None),
            P("pb", None),
            P("pb", "ha"),
        ),
        out_specs=(P("pb", "ha", None), P("pb", None), P("pb", "ha")),
        check_vma=False,
    )
```
